32 devices in a mesh: fsdp: 4 (over y, core), ctx: 8 (over z, x).
Axes of the slice: x: 2, y: 2, z: 4, core: 2. Of those that a mesh axis runs over, the one named last changes fastest.
Arguments:
- tokens: bfloat16 [4, 2048, 768], P('fsdp', 'ctx'), may hold values from -6 to 6
- segment_ids: int32 [4, 2048], P('fsdp', 'ctx'), may hold values from 0 to 15, as said below
- positions: int32 [4, 2048], P('fsdp', 'ctx'), may hold values from 0 to 1023, as said below
- gain_attn: bfloat16 [768], P(('fsdp', 'ctx')), may hold values from 0.5 to 1.5
- w_qkv: bfloat16 [768, 2304], P(('fsdp', 'ctx')), may hold values from -0.21875 to 0.21875
- w_out: bfloat16 [768, 768], P(('fsdp', 'ctx')), may hold values from -3 to 3
- gain_mlp: bfloat16 [768], P(('fsdp', 'ctx')), may hold values from 0.5 to 1.5
- w_in: bfloat16 [768, 2304], P(('fsdp', 'ctx')), may hold values from -0.21875 to 0.21875
- w_down: bfloat16 [1152, 768], P(None, ('fsdp', 'ctx')), may hold values from -0.1875 to 0.1875
- cotangent: bfloat16 [4, 2048, 768], P('fsdp', 'ctx'), may hold values from -6 to 6
Outputs:
- output: bfloat16 [4, 2048, 768], P('fsdp', 'ctx')
- input_grad: bfloat16 [4, 2048, 768], P('fsdp', 'ctx')
- grad_gain_attn: float32 [768], P(('fsdp', 'ctx'))
- grad_w_qkv: float32 [768, 2304], P(('fsdp', 'ctx'))
- grad_w_out: float32 [768, 768], P(('fsdp', 'ctx'))
- grad_gain_mlp: float32 [768], P(('fsdp', 'ctx'))
- grad_w_in: float32 [768, 2304], P(('fsdp', 'ctx'))
- grad_w_down: float32 [1152, 768], P(None, ('fsdp', 'ctx'))
The draws below stay inside these ranges and needn't reach their ends.
Inputs may be any that keep to these rules, and one draw needn't show every extreme that they name: `segment_ids`: along each sequence the ids never fall and every id is used; one document holds exactly 1024 tokens, the others share the rest. `positions`: A token's place within its document, counting from 0.
All inputs are finite; a program needn't handle non-finite values.
Results may differ from the reference program's by a relative error of at most 0.019.
Values may be sent and summed in bfloat16 or wider, within the bound.
No kernel may reach another device: no remote copies, remote signals or barrier semaphores. Data moves between devices by JAX's collectives and lax.ppermute only.
A program may use at most 192 MiB of HBM per device.

```python
import math
import jax
import jax.numpy as jnp
from jax import lax

D = 768
FF = 1152
HD = 64
DOCS = 16
SEQ = 2048
SEQS = 4


def document_layout(key):
    base = jax.random.fold_in(key, 7)
    half = SEQ // 2

    def one_sequence(seq_key):
        cut_key, big_key = jax.random.split(seq_key)
        order = jax.random.permutation(cut_key, half - 1).astype(jnp.int32) + 1
        cuts = jnp.sort(order[:DOCS - 2])
        bounds = jnp.concatenate([jnp.zeros((1,), jnp.int32), cuts, jnp.full((1,), half, jnp.int32)])
        small = bounds[1:] - bounds[:-1]
        big_index = jax.random.randint(big_key, (), 0, DOCS).astype(jnp.int32)
        slots = jnp.arange(DOCS).astype(jnp.int32)
        before = jnp.take(small, jnp.clip(slots, 0, DOCS - 2))
        after = jnp.take(small, jnp.clip(slots - 1, 0, DOCS - 2))
        lengths = jnp.where(slots < big_index, before, jnp.where(slots == big_index, half, after)).astype(jnp.int32)
        starts = (jnp.cumsum(lengths) - lengths).astype(jnp.int32)
        places = jnp.arange(SEQ).astype(jnp.int32)
        doc_ids = (jnp.sum((places[:, None] >= starts[None, :]).astype(jnp.int32), axis=1) - 1).astype(jnp.int32)
        offsets = (places - jnp.take(starts, doc_ids)).astype(jnp.int32)
        return (doc_ids, offsets)
    seq_keys = jax.random.split(base, SEQS)
    return jax.vmap(one_sequence)(seq_keys)


def draw_segment_ids(key, part):
    return document_layout(key)[0]


def draw_positions(key, part):
    return document_layout(key)[1]


def block_levels(key, shape, pieces, least, largest):
    def one(axis_at, parts):
        draws = jax.random.uniform(jax.random.fold_in(jax.random.fold_in(key, 6), axis_at), (parts,), jnp.float32, least / len(pieces), largest / len(pieces))
        return jnp.repeat(jnp.exp(draws), shape[axis_at] // parts).reshape((-1,) + (1,) * (len(shape) - axis_at - 1))

    level = one(*pieces[0])
    for cut in pieces[1:]:
        level = level * one(*cut)
    return level


def centred(rng, extent, scale, reach, cuts=(), held_as=jnp.bfloat16):
    array = jax.random.normal(rng, extent, jnp.float32) * scale
    if len(cuts) > 0:
        array = block_levels(rng, extent, cuts, -0.22, 0.18) * array
    return jnp.clip(array, min=-reach, max=reach).astype(held_as)


def setup_inputs(seed: int = 0) -> dict:
    key_list = jax.random.split(jax.random.key(seed), 11)
    tokens = centred(key_list[0], (SEQS, SEQ, D), 1.0, 6.0, ((0, 4), (1, 8)))
    segment_ids = draw_segment_ids(jax.random.fold_in(key_list[10], 71), 0)
    positions = draw_positions(jax.random.fold_in(key_list[10], 71), 0)
    gain_attn = jnp.clip(1.0 + 0.1 * jax.random.normal(key_list[3], (D,), jnp.float32), 0.5, 1.5).astype(jnp.bfloat16)
    w_qkv = centred(key_list[4], (D, 3 * D), D ** -0.5, 0.21875, ((0, 32),))
    w_out = centred(key_list[5], (D, D), 4 ** -0.5, 3.0, ((0, 32),))
    gain_mlp = jnp.clip(1.0 + 0.1 * jax.random.normal(key_list[6], (D,), jnp.float32), 0.5, 1.5).astype(jnp.bfloat16)
    w_in = centred(key_list[7], (D, 2 * FF), D ** -0.5, 0.21875, ((0, 32),))
    w_down = centred(key_list[8], (FF, D), FF ** -0.5, 0.1875, ((1, 32),))
    cotangent = centred(key_list[9], (SEQS, SEQ, D), 1.0, 6.0, ((0, 4), (1, 8)))
    return {"tokens": tokens, "segment_ids": segment_ids, "positions": positions, "gain_attn": gain_attn, "w_qkv": w_qkv, "w_out": w_out, "gain_mlp": gain_mlp, "w_in": w_in, "w_down": w_down, "cotangent": cotangent}


EPS = 1e-05
THETA = 160000.0
NEG = -1e+30
HIGH = lax.Precision.HIGHEST
ROOT_HALF = 0.7071067811865476

@jax.custom_vjp
def low(v):
    return lax.optimization_barrier(v.astype(jnp.bfloat16)).astype(jnp.float32)

@jax.custom_vjp
def low_back(v):
    return v

def low_keep(v):
    return (low(v), None)

def low_pass(kept, grad):
    return (grad,)

def back_keep(v):
    return (v, None)

def back_low(kept, grad):
    return (low(grad),)
low.defvjp(low_keep, low_pass)
low_back.defvjp(back_keep, back_low)

def layer_norm(values):
    center = values - lax.optimization_barrier(jnp.mean(values, axis=-1, keepdims=True))
    spread = lax.optimization_barrier(jnp.mean(center * center, axis=-1, keepdims=True))
    return center * lax.rsqrt(spread + EPS)

def rotate_half(values):
    half = values.shape[-1] // 2
    return jnp.concatenate([-values[..., half:], values[..., :half]], axis=-1)

def rotary(values, cosine, sine):
    return values * cosine + rotate_half(values) * sine

def matmul(left, right):
    return jnp.dot(left, right, precision=HIGH, preferred_element_type=jnp.float32)

def attend_block(queries, query_docs, keys, values, key_docs):
    scores = low_back(jnp.einsum('thd,khd->htk', queries, keys, precision=HIGH) * HD ** (-0.5))
    mask = (query_docs[:, None] == key_docs[None, :])[None]
    masked = jnp.where(mask, scores, NEG)
    top = lax.optimization_barrier(jnp.max(masked, axis=-1, keepdims=True))
    expo = jnp.where(mask, jnp.exp(masked - top), 0.0)
    weights = low(expo / lax.optimization_barrier(jnp.sum(expo, axis=-1, keepdims=True)))
    return jnp.einsum('htk,khd->thd', weights, values, precision=HIGH)

def forward_one(inputs, doc_ids, places, gain_one, w_joined, w_proj, gain_two, w_up, w_back):
    rows = inputs.shape[0]
    heads = D // HD
    rates = THETA ** (-jnp.arange(0, HD, 2).astype(jnp.float32) / HD)
    freqs = places.astype(jnp.float32)[:, None] * rates[None, :]
    angles = jnp.concatenate([freqs, freqs], axis=-1)[:, None, :]
    cosine = jnp.cos(angles)
    sine = jnp.sin(angles)
    hidden_one = low(layer_norm(inputs) * gain_one)
    joined = low_back(matmul(hidden_one, w_joined))
    query = low(rotary(joined[:, :D].reshape(rows, heads, HD), cosine, sine))
    keys = low(rotary(joined[:, D:2 * D].reshape(rows, heads, HD), cosine, sine))
    values = low(joined[:, 2 * D:].reshape(rows, heads, HD))
    block_rows = math.gcd(rows, 512)
    blocks = rows // block_rows
    attend = jax.checkpoint(lambda packed: attend_block(packed[0], packed[1], keys, values, doc_ids))
    attended = lax.map(attend, (query.reshape(blocks, block_rows, heads, HD), doc_ids.reshape(blocks, block_rows)))
    attended = low(low_back(attended.reshape(rows, D)))
    middle = inputs + low_back(matmul(attended, w_proj))
    hidden_two = low(layer_norm(middle) * gain_two)
    upward = low_back(matmul(hidden_two, w_up))
    inner = upward[:, :FF]
    gate = upward[:, FF:]
    cdf = 0.5 * (1.0 + jax.scipy.special.erf(inner * ROOT_HALF))
    product = low(inner * cdf * gate)
    return middle + low_back(matmul(product, w_back))

def reference(tokens, segment_ids, positions, gain_attn, w_qkv, w_out, gain_mlp, w_in, w_down, cotangent):
    floats = [a.astype(jnp.float32) for a in (tokens, gain_attn, w_qkv, w_out, gain_mlp, w_in, w_down)]

    def whole(inputs, gain_one, w_joined, w_proj, gain_two, w_up, w_back):

        def one_sequence(packed):
            return forward_one(packed[0], packed[1], packed[2], gain_one, w_joined, w_proj, gain_two, w_up, w_back)
        return lax.map(one_sequence, (inputs, segment_ids, positions))
    output, pull = jax.vjp(whole, *floats)
    grads = pull(cotangent.astype(jnp.float32))
    return (output.astype(jnp.bfloat16), grads[0].astype(jnp.bfloat16), grads[1], grads[2], grads[3], grads[4], grads[5], grads[6])
```

```python
import math

import jax
import jax.numpy as jnp
from jax import lax
from jax.experimental import pallas as pl
from jax.experimental.pallas import tpu as pltpu
from jax.sharding import PartitionSpec as P

HD = 64
SLOTS = 2
LANES = SLOTS * HD
EPS = 1e-05
THETA = 160000.0
NEG = -1e30
ROOT_HALF = 0.7071067811865476
INV_ROOT_TWO_PI = 0.3989422804014327
VMEM_BYTES = 50 * 1024 * 1024
AXES = ("fsdp", "ctx")

f32 = jnp.float32
bf16 = jnp.bfloat16


def norm_rows(values):
    center = values - jnp.mean(values, axis=-1, keepdims=True)
    spread = jnp.mean(center * center, axis=-1, keepdims=True)
    inverse = lax.rsqrt(spread + EPS)
    return (center * inverse, inverse)


def norm_back(grad_normed, normed, inverse):
    return inverse * (
        grad_normed
        - jnp.mean(grad_normed, axis=-1, keepdims=True)
        - normed * jnp.mean(grad_normed * normed, axis=-1, keepdims=True)
    )


def rotate_half(values):
    lane = lax.broadcasted_iota(jnp.int32, values.shape, 1)
    ahead = pltpu.roll(values, LANES - HD // 2, 1)
    behind = pltpu.roll(values, HD // 2, 1)
    return jnp.where(lane % HD < HD // 2, -ahead, behind)


def dot_tt(left, right):
    return lax.dot_general(left, right, (((1,), (1,)), ((), ())), preferred_element_type=f32)


def dot_rows(left, right):
    return lax.dot_general(left, right, (((0,), (0,)), ((), ())), preferred_element_type=f32)


def params():
    return pltpu.CompilerParams(
        dimension_semantics=("arbitrary",), vmem_limit_bytes=VMEM_BYTES
    )


def project_kernel(order_ref, x_ref, gain_ref, w_ref, cos_ref, sin_ref, hidden_ref, qkv_ref):
    rows = hidden_ref.shape[0]
    normed, _ = norm_rows(x_ref[0, :rows, :].astype(f32))
    hidden = (normed * gain_ref[...].astype(f32)).astype(bf16)
    hidden_ref[...] = hidden
    joined = jnp.dot(hidden, w_ref[:, : 3 * LANES], preferred_element_type=f32)
    cosine = cos_ref[...]
    sine = sin_ref[...]
    query = joined[:, :LANES]
    keys = joined[:, LANES : 2 * LANES]
    query = (query * cosine + rotate_half(query) * sine).astype(bf16)
    keys = (keys * cosine + rotate_half(keys) * sine).astype(bf16)
    qkv_ref[:, :LANES] = query * bf16(HD**-0.5)
    qkv_ref[:, LANES : 2 * LANES] = keys
    qkv_ref[:, 2 * LANES :] = joined[:, 2 * LANES :].astype(bf16)


def project(order, arrived, gain, w_heads, cosine, sine, rows):
    count, held, width = arrived.shape
    total = count * rows
    sorted_block = lambda i, order: (order[i], 0)
    fixed = lambda i, order: (0, 0)
    return pl.pallas_call(
        project_kernel,
        grid_spec=pltpu.PrefetchScalarGridSpec(
            num_scalar_prefetch=1,
            grid=(count,),
            in_specs=[
                pl.BlockSpec((1, held, width), lambda i, order: (i, 0, 0)),
                pl.BlockSpec((1, width), fixed),
                pl.BlockSpec(w_heads.shape, fixed),
                pl.BlockSpec((rows, LANES), sorted_block),
                pl.BlockSpec((rows, LANES), sorted_block),
            ],
            out_specs=[
                pl.BlockSpec((rows, width), sorted_block),
                pl.BlockSpec((rows, 3 * LANES), sorted_block),
            ],
        ),
        out_shape=[
            jax.ShapeDtypeStruct((total, width), bf16),
            jax.ShapeDtypeStruct((total, 3 * LANES), bf16),
        ],
        compiler_params=params(),
        name="project",
    )(order, arrived, gain, w_heads, cosine, sine)


def attend_kernel(lo_ref, hi_ref, ok_ref, q_ref, k_ref, v_ref, doc_col_ref, doc_row_ref,
                  low_ref, att_ref, lse_ref):
    block = pl.program_id(0)
    rows = q_ref.shape[0]
    lane = lax.broadcasted_iota(jnp.int32, (rows, LANES), 1)
    docs = doc_col_ref[...]
    query = q_ref[...]
    att_ref[...] = jnp.zeros((rows, LANES), f32)
    lse_ref[...] = jnp.zeros((rows, LANES), f32)
    for slot in range(SLOTS):
        mine = lane // HD == slot

        @pl.when(ok_ref[block * SLOTS + slot] == 1)
        def _():
            q_slot = jnp.where(mine, query, bf16(0))

            def step(at, carry):
                run_max, run_sum, accum = carry
                span = pl.ds(pl.multiple_of(at * rows, rows), rows)
                scores = dot_tt(q_slot, k_ref[span, :])
                same = docs == doc_row_ref[pl.ds(at, 1), :]
                scores = jnp.where(same, scores, NEG)
                new_max = jnp.maximum(run_max, jnp.max(scores, axis=1, keepdims=True))
                expo = jnp.where(same, jnp.exp(scores - new_max), 0.0)
                factor = jnp.exp(run_max - new_max)
                run_sum = run_sum * factor + jnp.sum(expo, axis=1, keepdims=True)
                accum = accum * factor + jnp.dot(
                    expo.astype(bf16), v_ref[span, :], preferred_element_type=f32
                )
                return (new_max, run_sum, accum)

            start = (
                jnp.full((rows, 1), NEG, f32),
                jnp.zeros((rows, 1), f32),
                jnp.zeros((rows, LANES), f32),
            )
            top, total, accum = lax.fori_loop(lo_ref[block], hi_ref[block], step, start)
            att_ref[...] = jnp.where(mine, accum / total, att_ref[...])
            lse_ref[...] = jnp.where(mine, top + jnp.log(total), lse_ref[...])

    low_ref[0] = att_ref[...].astype(bf16)


def attend(lo, hi, ok, qkv, doc_col, doc_row, rows):
    total = qkv.shape[0]
    count = total // rows
    whole = lambda part: pl.BlockSpec((total, LANES), lambda i, *s: (0, part))
    mine = pl.BlockSpec((rows, LANES), lambda i, *s: (i, 0))
    return pl.pallas_call(
        attend_kernel,
        grid_spec=pltpu.PrefetchScalarGridSpec(
            num_scalar_prefetch=3,
            grid=(count,),
            in_specs=[
                mine,
                whole(1),
                whole(2),
                pl.BlockSpec((rows, 1), lambda i, *s: (i, 0)),
                pl.BlockSpec((count, rows), lambda i, *s: (0, 0)),
            ],
            out_specs=[
                pl.BlockSpec((1, rows, LANES), lambda i, *s: (i, 0, 0)),
                mine,
                mine,
            ],
        ),
        out_shape=[
            jax.ShapeDtypeStruct((count, rows, LANES), bf16),
            jax.ShapeDtypeStruct((total, LANES), f32),
            jax.ShapeDtypeStruct((total, LANES), f32),
        ],
        compiler_params=params(),
        name="attend",
    )(lo, hi, ok, qkv, qkv, qkv, doc_col, doc_row)


def attend_back_kernel(lo_ref, hi_ref, ok_ref, q_ref, k_ref, v_ref, doc_col_ref, doc_row_ref,
                       grad_ref, att_ref, lse_ref, cos_ref, sin_ref, out_ref, dk_ref, dv_ref):
    block = pl.program_id(0)
    count = pl.num_programs(0)
    rows = q_ref.shape[0]
    lane = lax.broadcasted_iota(jnp.int32, (rows, LANES), 1)

    @pl.when(block == 0)
    def _():
        dk_ref[...] = jnp.zeros(dk_ref.shape, f32)
        dv_ref[...] = jnp.zeros(dv_ref.shape, f32)

    docs = doc_col_ref[...]
    query = q_ref[...]
    grads = grad_ref[0]
    spread = grads.astype(f32) * att_ref[...]
    log_sums = lse_ref[...]
    here = pl.ds(pl.multiple_of(block * rows, rows), rows)

    def turn_back(values, span):
        return values * cos_ref[span, :] - rotate_half(values * sin_ref[span, :])

    out_ref[block, :, :LANES] = jnp.zeros((rows, LANES), bf16)
    for slot in range(SLOTS):
        mine = lane // HD == slot

        @pl.when(ok_ref[block * SLOTS + slot] == 1)
        def _():
            q_slot = jnp.where(mine, query, bf16(0))
            g_slot = jnp.where(mine, grads, bf16(0))
            delta = jnp.sum(jnp.where(mine, spread, 0.0), axis=1, keepdims=True)
            log_sum = log_sums[:, slot * HD : slot * HD + 1]

            def step(at, grad_query):
                span = pl.ds(pl.multiple_of(at * rows, rows), rows)
                keys = k_ref[span, :]
                scores = dot_tt(q_slot, keys)
                same = docs == doc_row_ref[pl.ds(at, 1), :]
                probs = jnp.exp(jnp.where(same, scores, NEG) - log_sum)
                dv_ref[span, :] += dot_rows(probs.astype(bf16), g_slot)
                grad_probs = dot_tt(g_slot, v_ref[span, :])
                grad_scores = (probs * (grad_probs - delta)).astype(bf16)
                dk_ref[span, :] += dot_rows(grad_scores, q_slot)
                return grad_query + jnp.dot(grad_scores, keys, preferred_element_type=f32)

            grad_query = lax.fori_loop(
                lo_ref[block], hi_ref[block], step, jnp.zeros((rows, LANES), f32)
            )
            turned = turn_back(grad_query * HD**-0.5, here).astype(bf16)
            out_ref[block, :, :LANES] = jnp.where(mine, turned, out_ref[block, :, :LANES])

    @pl.when(block == count - 1)
    def _():
        def finish(at, carry):
            span = pl.ds(pl.multiple_of(at * rows, rows), rows)
            out_ref[at, :, LANES : 2 * LANES] = turn_back(dk_ref[span, :], span).astype(bf16)
            out_ref[at, :, 2 * LANES :] = dv_ref[span, :].astype(bf16)
            return carry

        lax.fori_loop(0, count, finish, 0)


def attend_back(lo, hi, ok, qkv, doc_col, doc_row, grads, att, lse, cosine, sine, rows):
    total = qkv.shape[0]
    count = total // rows
    whole = lambda part: pl.BlockSpec((total, LANES), lambda i, *s: (0, part))
    mine = pl.BlockSpec((rows, LANES), lambda i, *s: (i, 0))
    return pl.pallas_call(
        attend_back_kernel,
        grid_spec=pltpu.PrefetchScalarGridSpec(
            num_scalar_prefetch=3,
            grid=(count,),
            in_specs=[
                mine,
                whole(1),
                whole(2),
                pl.BlockSpec((rows, 1), lambda i, *s: (i, 0)),
                pl.BlockSpec((count, rows), lambda i, *s: (0, 0)),
                pl.BlockSpec((1, rows, LANES), lambda i, *s: (i, 0, 0)),
                mine,
                mine,
                whole(0),
                whole(0),
            ],
            out_specs=pl.BlockSpec((count, rows, 3 * LANES), lambda i, *s: (0, 0, 0)),
            scratch_shapes=[pltpu.VMEM((total, LANES), f32), pltpu.VMEM((total, LANES), f32)],
        ),
        out_shape=jax.ShapeDtypeStruct((count, rows, 3 * LANES), bf16),
        compiler_params=params(),
        name="attend_back",
    )(lo, hi, ok, qkv, qkv, qkv, doc_col, doc_row, grads, att, lse, cosine, sine)


def program(fsdp, ctx):
    def on_device(tokens, segment_ids, positions, gain_attn, w_qkv, w_out, gain_mlp, w_in, w_down,
                  cotangent):
        rows, width = tokens.shape[1:]
        shard = w_qkv.shape[0]
        heads = width // HD
        common = math.gcd(heads, ctx)
        splits = ctx // common
        units = heads // common
        first = [min(units * c // splits, heads - SLOTS) for c in range(ctx)]
        owners = [
            [
                (c, slot)
                for c in range(ctx)
                for slot in range(SLOTS)
                if first[c] + slot == head
                and max(units * c, head * splits) < min(units * (c + 1), (head + 1) * splits)
            ]
            for head in range(heads)
        ]
        me = lax.axis_index("ctx")
        blocks = jnp.arange(ctx, dtype=jnp.int32)

        packed = jnp.concatenate([w_out, w_in, w_down.T], axis=1)
        mlp_all = lax.all_gather(packed, AXES, axis=0, tiled=True)

        gains = jnp.concatenate(
            [gain_attn[:, None], gain_mlp[:, None], jnp.zeros((shard, LANES - 2), bf16)], axis=1
        )
        head_cols = jnp.stack(
            [
                jnp.concatenate(
                    [
                        w_qkv[:, part * width + first[c] * HD : part * width + first[c] * HD + LANES]
                        for part in range(3)
                    ]
                    + [gains],
                    axis=1,
                )
                for c in range(ctx)
            ]
        )
        w_heads = lax.all_to_all(head_cols, "ctx", 0, 0, tiled=True).reshape(ctx * shard, 4 * LANES)
        w_heads = lax.all_gather(w_heads, "fsdp", axis=0, tiled=True)
        gain_one = w_heads[:, 3 * LANES].reshape(1, width)
        gain_two = w_heads[:, 3 * LANES + 1].reshape(1, width).astype(f32)

        places = jnp.concatenate(
            [segment_ids, positions // 64, positions % 64], axis=1
        ).astype(bf16)
        places = places.reshape(-1, width)
        places = jnp.concatenate([places, jnp.zeros((8 - places.shape[0], width), bf16)], axis=0)
        block = jnp.concatenate([tokens[0], places], axis=0)
        outer = ctx // 2
        ring = [(o * 2 + i, (o + 1) % outer * 2 + i) for o in range(outer) for i in range(2)]
        swap = [(c, c ^ 1) for c in range(ctx)]
        arrived = []
        order = []
        for step in range(outer):
            if step > 0:
                block = lax.ppermute(block, "ctx", ring)
            arrived += [block, lax.ppermute(block, "ctx", swap)]
            source = (me // 2 + outer - step) % outer * 2 + me % 2
            order += [source, source ^ 1]
        arrived = jnp.stack(arrived)
        order = jnp.stack(order).astype(jnp.int32)
        infos = arrived[:, rows : rows + 3 * rows // width, :].reshape(ctx, 3, rows).astype(f32)
        pick = (blocks[:, None] == order[None, :]).astype(f32)
        infos = jnp.sum(pick[:, :, None, None] * infos[None], axis=1)
        docs = infos[:, 0].astype(jnp.int32)
        spots = (infos[:, 1] * 64 + infos[:, 2]).reshape(ctx * rows, 1)
        first_doc = docs[:, 0]
        last_doc = docs[:, rows - 1]
        lo = jnp.sum((last_doc[None, :] < first_doc[:, None]).astype(jnp.int32), axis=1)
        hi = jnp.sum((first_doc[None, :] <= last_doc[:, None]).astype(jnp.int32), axis=1)
        unit = (
            (jnp.asarray(first, jnp.int32)[me] + jnp.arange(SLOTS, dtype=jnp.int32))[None, :] * splits
            + (blocks % splits)[:, None]
        )
        ok = ((unit >= units * me) & (unit < units * (me + 1))).astype(jnp.int32).reshape(-1)
        half = jnp.arange(LANES) % (HD // 2)
        rates = THETA ** (-2.0 * half.astype(f32) / HD)
        angles = spots * rates[None, :]
        cosine = jnp.cos(angles)
        sine = jnp.sin(angles)
        doc_col = docs.reshape(ctx * rows, 1)

        hidden_one, qkv = project(order, arrived, gain_one, w_heads, cosine, sine, rows)
        att_low, att, lse = attend(lo, hi, ok, qkv, doc_col, docs, rows)
        att_in = lax.all_to_all(att_low, "ctx", 0, 0, tiled=True)

        def join(parts, at):
            pieces = []
            for head in range(heads):
                terms = [
                    parts[c, :, at + slot * HD : at + (slot + 1) * HD] for c, slot in owners[head]
                ]
                total = terms[0].astype(f32)
                for term in terms[1:]:
                    total = total + term.astype(f32)
                pieces.append(total.astype(bf16))
            return jnp.concatenate(pieces, axis=1)

        attended = join(att_in, 0)

        inputs = tokens[0].astype(f32)
        w_proj = mlp_all[:, :width]
        w_up = mlp_all[:, width : width + w_in.shape[1]]
        w_back_t = mlp_all[:, width + w_in.shape[1] :]
        hidden_units = w_down.shape[0]
        middle = inputs + jnp.dot(attended, w_proj, preferred_element_type=f32)
        normed_two, inverse_two = norm_rows(middle)
        hidden_two = (normed_two * gain_two).astype(bf16)
        upward = jnp.dot(hidden_two, w_up, preferred_element_type=f32)
        inner = upward[:, :hidden_units]
        gate = upward[:, hidden_units:]
        cdf = 0.5 * (1.0 + jax.scipy.special.erf(inner * ROOT_HALF))
        gelu_value = inner * cdf
        product = (gelu_value * gate).astype(bf16)
        output = (middle + dot_tt(product, w_back_t)).astype(bf16)[None]
        grad_low = cotangent[0]
        grad_product = jnp.dot(grad_low, w_back_t, preferred_element_type=f32)
        grad_inner = (
            grad_product * gate * (cdf + inner * jnp.exp(-0.5 * inner * inner) * INV_ROOT_TWO_PI)
        )
        grad_gate = grad_product * gelu_value
        grad_up = jnp.concatenate([grad_inner, grad_gate], axis=1).astype(bf16)
        grad_hidden_two = dot_tt(grad_up, w_up)
        grad_middle = grad_low.astype(f32) + norm_back(
            grad_hidden_two * gain_two, normed_two, inverse_two
        )
        grad_branch = grad_middle.astype(bf16)
        grad_attended = dot_tt(grad_branch, w_proj).astype(bf16)
        grad_heads = jnp.stack(
            [grad_attended[:, first[c] * HD : first[c] * HD + LANES] for c in range(ctx)]
        )
        grad_heads = lax.all_to_all(grad_heads, "ctx", 0, 0, tiled=True)

        grad_packed = jnp.concatenate(
            [
                dot_rows(attended, grad_branch),
                dot_rows(hidden_two, grad_up),
                dot_rows(grad_low, product),
            ],
            axis=1,
        ).astype(bf16)
        grad_packed = lax.psum_scatter(grad_packed, "fsdp", scatter_dimension=0, tiled=True)
        grad_packed = lax.psum_scatter(grad_packed, "ctx", scatter_dimension=0, tiled=True)
        grad_packed = grad_packed.astype(f32)
        sum_w_out = grad_packed[:, :width]
        sum_w_in = grad_packed[:, width : width + w_in.shape[1]]
        sum_w_down = grad_packed[:, width + w_in.shape[1] :].T
        sum_gain_mlp = jnp.sum(w_in.astype(f32) * sum_w_in, axis=1) / gain_mlp.astype(f32)

        w_joined = lax.all_gather(w_qkv, AXES, axis=0, tiled=True)
        grad_joined = attend_back(
            lo, hi, ok, qkv, doc_col, docs, grad_heads, att, lse, cosine, sine, rows
        )
        grad_cols = dot_rows(hidden_one, grad_joined.reshape(ctx * rows, 3 * LANES)).astype(bf16)
        grad_joined = lax.all_to_all(grad_joined, "ctx", 0, 0, tiled=True)
        grad_joined = jnp.concatenate([join(grad_joined, part * LANES) for part in range(3)], axis=1)
        grad_hidden_one = dot_tt(grad_joined, w_joined)
        normed_one, inverse_one = norm_rows(inputs)
        input_grad = grad_middle + norm_back(
            grad_hidden_one * gain_one.astype(f32), normed_one, inverse_one
        )

        grad_cols = grad_cols.reshape(fsdp, ctx * shard, 3 * LANES)
        grad_cols = lax.all_to_all(grad_cols, "fsdp", 0, 0, tiled=True)
        grad_cols = jnp.sum(grad_cols.astype(f32), axis=0).astype(bf16)
        grad_cols = lax.all_to_all(grad_cols.reshape(ctx, shard, 3 * LANES), "ctx", 0, 0, tiled=True)
        grad_cols = grad_cols.astype(f32)
        pieces = []
        for part in range(3):
            for head in range(heads):
                total = 0.0
                for c, slot in owners[head]:
                    at = part * LANES + slot * HD
                    total = total + grad_cols[c, :, at : at + HD]
                pieces.append(total)
        sum_w_qkv = jnp.concatenate(pieces, axis=1)
        sum_gain_attn = jnp.sum(w_qkv.astype(f32) * sum_w_qkv, axis=1) / gain_attn.astype(f32)
        return (
            output,
            input_grad.astype(bf16)[None],
            sum_gain_attn,
            sum_w_qkv,
            sum_w_out,
            sum_gain_mlp,
            sum_w_in,
            sum_w_down,
        )

    return on_device


def solution(mesh):
    rows = P(AXES, None)
    tokens = P("fsdp", "ctx", None)
    return jax.shard_map(
        program(mesh.shape["fsdp"], mesh.shape["ctx"]),
        mesh=mesh,
        in_specs=(
            tokens,
            P("fsdp", "ctx"),
            P("fsdp", "ctx"),
            P(AXES),
            rows,
            rows,
            P(AXES),
            rows,
            P(None, AXES),
            tokens,
        ),
        out_specs=(tokens, tokens, P(AXES), rows, rows, P(AXES), rows, P(None, AXES)),
        check_vma=False,
    )
```

```python
import functools
import math

import jax
import jax.numpy as jnp
from jax import lax
from jax.experimental import pallas as pl
from jax.experimental.pallas import tpu as pltpu
from jax.sharding import PartitionSpec as P

HD = 64
SLOTS = 2
LANES = SLOTS * HD
GRAIN = 128
KEY_TILE = 512
CHUNK = 384
EPS = 1e-05
THETA = 160000.0
NEG = -1e30
ROOT_HALF = 0.7071067811865476
INV_ROOT_TWO_PI = 0.3989422804014327
VMEM_BYTES = 50 * 1024 * 1024
AXES = ("fsdp", "ctx")

f32 = jnp.float32
bf16 = jnp.bfloat16


def norm_rows(values):
    center = values - jnp.mean(values, axis=-1, keepdims=True)
    spread = jnp.mean(center * center, axis=-1, keepdims=True)
    inverse = lax.rsqrt(spread + EPS)
    return (center * inverse, inverse)


def norm_back(grad_normed, normed, inverse):
    return inverse * (
        grad_normed
        - jnp.mean(grad_normed, axis=-1, keepdims=True)
        - normed * jnp.mean(grad_normed * normed, axis=-1, keepdims=True)
    )


def rotate_half(values):
    lane = lax.broadcasted_iota(jnp.int32, values.shape, 1)
    ahead = pltpu.roll(values, LANES - HD // 2, 1)
    behind = pltpu.roll(values, HD // 2, 1)
    return jnp.where(lane % HD < HD // 2, -ahead, behind)


def dot_tt(left, right):
    return lax.dot_general(left, right, (((1,), (1,)), ((), ())), preferred_element_type=f32)


def dot_rows(left, right):
    return lax.dot_general(left, right, (((0,), (0,)), ((), ())), preferred_element_type=f32)


def params():
    return pltpu.CompilerParams(
        dimension_semantics=("arbitrary",), vmem_limit_bytes=VMEM_BYTES
    )


def spread_kernel(first, w_ref, gain_one_ref, gain_two_ref, doc_ref, place_ref, out_ref):
    shard, columns = w_ref.shape
    width = columns // 3
    rows = doc_ref.shape[1]
    square = (shard, shard)
    eye = lax.broadcasted_iota(jnp.int32, square, 0) == lax.broadcasted_iota(jnp.int32, square, 1)

    def upright(ref):
        spread = jnp.where(eye, ref[...].astype(f32), 0.0)
        return jnp.sum(spread, axis=1, keepdims=True).astype(bf16)

    lane = lax.broadcasted_iota(jnp.int32, (shard, LANES), 1)
    gains = jnp.where(
        lane == 0, upright(gain_one_ref), jnp.where(lane == 1, upright(gain_two_ref), bf16(0))
    )
    place = place_ref[...]
    top = jnp.concatenate([doc_ref[...], place >> 6], axis=1).astype(f32)
    low = jnp.concatenate([place & 63, jnp.zeros_like(place)], axis=1).astype(f32)
    row = lax.broadcasted_iota(jnp.int32, (8, 2 * rows), 0)
    places = jnp.where(row == 0, top, jnp.where(row == 1, low, 0.0)).astype(bf16)
    for c, head in enumerate(first):
        for part in range(3):
            at = part * width + head * HD
            out_ref[c, :shard, part * LANES : (part + 1) * LANES] = w_ref[:, at : at + LANES]
        out_ref[c, :shard, 3 * LANES :] = gains
        out_ref[c, shard:, :] = places


def spread(first, w_qkv, gain_one, gain_two, docs, places):
    shard = w_qkv.shape[0]
    return pl.pallas_call(
        functools.partial(spread_kernel, first),
        out_shape=jax.ShapeDtypeStruct((len(first), shard + 8, 4 * LANES), bf16),
        compiler_params=pltpu.CompilerParams(vmem_limit_bytes=VMEM_BYTES),
        name="spread",
    )(w_qkv, gain_one[None], gain_two[None], docs, places)


def project_kernel(masks, at_ref, own_ref, other_ref, w_ref, cos_ref, sin_ref, *refs):
    hidden_ref, qkv_ref, turned_ref, gains_ref, w_all = refs[-5:]
    rows = own_ref.shape[0]
    share = w_ref.shape[1]
    for i, mask in enumerate(masks):
        start = pl.multiple_of((at_ref[2] ^ mask) * share, share)
        w_all[pl.ds(start, share), :] = w_ref[i]
    gains = jnp.transpose(w_all[:, 3 * LANES :].astype(f32))
    gains_ref[...] = gains[:8]
    gain = gains[:1]
    for flip, x_ref in enumerate((own_ref, other_ref)):
        span = pl.ds(pl.multiple_of((at_ref[1] ^ flip) * rows, rows), rows)
        normed, _ = norm_rows(x_ref[...].astype(f32))
        hidden = (normed * gain).astype(bf16)
        hidden_ref[span, :] = hidden
        joined = jnp.dot(hidden, w_all[:, : 3 * LANES], preferred_element_type=f32)
        cosine = cos_ref[span, :]
        sine = sin_ref[span, :]
        query = joined[:, :LANES]
        keys = joined[:, LANES : 2 * LANES]
        values = joined[:, 2 * LANES :]
        query = (query * cosine + rotate_half(query) * sine).astype(bf16)
        keys = keys * cosine + rotate_half(keys) * sine
        qkv_ref[span, :LANES] = query * bf16(HD**-0.5)
        qkv_ref[span, LANES : 2 * LANES] = keys.astype(bf16)
        qkv_ref[span, 2 * LANES :] = values.astype(bf16)
        turned_ref[:LANES, span] = jnp.transpose(keys).astype(bf16)
        turned_ref[LANES:, span] = jnp.transpose(values).astype(bf16)


def project(masks, at, own, other, w_parts, cosine, sine, total, held):
    rows, width = own.shape
    fixed = lambda shape: pl.BlockSpec(shape, lambda i, at: (0,) * len(shape))
    pair = lambda width: pl.BlockSpec((2 * rows, width), lambda i, at: (at[0], 0))
    shapes = [
        jax.ShapeDtypeStruct((total, width), bf16),
        jax.ShapeDtypeStruct((total, 3 * LANES), bf16),
        jax.ShapeDtypeStruct((2 * LANES, total), bf16),
    ]
    return pl.pallas_call(
        functools.partial(project_kernel, masks),
        grid_spec=pltpu.PrefetchScalarGridSpec(
            num_scalar_prefetch=1,
            grid=(1,),
            in_specs=[
                fixed((rows, width)),
                fixed((rows, width)),
                fixed(w_parts.shape),
                pair(LANES),
                pair(LANES),
            ]
            + [pl.BlockSpec(memory_space=pl.ANY) for _ in held],
            out_specs=[
                pair(width),
                pair(3 * LANES),
                pl.BlockSpec((2 * LANES, 2 * rows), lambda i, at: (0, at[0])),
                fixed((8, width)),
            ],
            scratch_shapes=[pltpu.VMEM((width, 4 * LANES), bf16)],
        ),
        out_shape=shapes + [jax.ShapeDtypeStruct((8, width), f32)],
        input_output_aliases={6 + i: i for i in range(len(held))},
        compiler_params=params(),
        cost_estimate=pl.CostEstimate(
            flops=2 * 2 * rows * width * 3 * LANES, bytes_accessed=6 << 20, transcendentals=0
        ),
        name="project",
    )(at, own, other, w_parts, cosine, sine, *held)


def gather_rows(units_ref, ref, units, part):
    lane = lax.broadcasted_iota(jnp.int32, (part, LANES), 1)
    chunks = []
    for i in range(units):
        start = pl.multiple_of(units_ref[units + i] * part, part)
        chunk = ref[pl.ds(start, part), :]
        chunks.append(jnp.where(lane // HD == units_ref[i], chunk, jnp.zeros_like(chunk)))
    return jnp.concatenate(chunks, axis=0)


def scatter_rows(units_ref, acc_ref, values, units, part):
    lane = lax.broadcasted_iota(jnp.int32, (part, LANES), 1)
    acc_ref[...] = jnp.zeros(acc_ref.shape, f32)
    for i in range(units):
        start = pl.multiple_of(units_ref[units + i] * part, part)
        chunk = values[i * part : (i + 1) * part]
        acc_ref[pl.ds(start, part), :] += jnp.where(lane // HD == units_ref[i], chunk, 0.0)


def across(slab, wide):
    if wide <= LANES:
        return slab[:, :wide]
    return jnp.concatenate([slab] * (wide // LANES), axis=1)


def fold(values, reduce):
    rows, wide = values.shape
    return reduce(values.reshape(rows // 8, 8, wide), axis=0)


def tile_span(base_ref, block, at, tile):
    return pl.ds(pl.multiple_of(base_ref[block] * GRAIN + at * tile, GRAIN), tile)


def attend_kernel(units, tile, base_ref, count_ref, units_ref, q_ref, k_ref, vt_ref, doc_ref, doc_q_ref,
                  low_ref, att_ref, lse_ref, s_ref, acc_ref):
    block = pl.program_id(0)
    wide = s_ref.shape[1]
    part = wide // units
    queries = gather_rows(units_ref, q_ref, units, part)
    doc_q = doc_q_ref[0]

    def score(at, top):
        span = tile_span(base_ref, block, at, tile)
        scores = dot_tt(k_ref[span, :], queries)
        scores = jnp.where(across(doc_ref[span, :], wide) == doc_q, scores, NEG)
        s_ref[span, :] = scores
        return jnp.maximum(top, fold(scores, jnp.max))

    count = count_ref[block]
    top = lax.fori_loop(0, count, score, jnp.full((8, wide), NEG, f32))
    top = jnp.max(top, axis=0, keepdims=True)

    def weigh(at, carry):
        total, accum = carry
        span = tile_span(base_ref, block, at, tile)
        expo = jnp.exp(s_ref[span, :] - top)
        total = total + fold(expo, jnp.sum)
        accum = accum + jnp.dot(vt_ref[:, span], expo.astype(bf16), preferred_element_type=f32)
        return (total, accum)

    total, accum = lax.fori_loop(
        0, count, weigh, (jnp.zeros((8, wide), f32), jnp.zeros((LANES, wide), f32))
    )
    total = jnp.sum(total, axis=0, keepdims=True)
    att = accum / total
    att_ref[0] = att
    lse_ref[0] = top + jnp.log(total)
    scatter_rows(units_ref, acc_ref, jnp.transpose(att), units, part)
    low_ref[0] = acc_ref[...].astype(bf16)


def attend(base, tiles, unit_places, qkv, turned, doc_slab, doc_q, rows, tile):
    total = qkv.shape[0]
    count = total // rows
    units = unit_places.shape[0] // 2
    wide = doc_q.shape[2]
    return pl.pallas_call(
        functools.partial(attend_kernel, units, tile),
        grid_spec=pltpu.PrefetchScalarGridSpec(
            num_scalar_prefetch=3,
            grid=(count,),
            in_specs=[
                pl.BlockSpec((rows, LANES), lambda i, *s: (i, 0)),
                pl.BlockSpec((total, LANES), lambda i, *s: (0, 1)),
                pl.BlockSpec((LANES, total), lambda i, *s: (1, 0)),
                pl.BlockSpec((total, LANES), lambda i, *s: (0, 0)),
                pl.BlockSpec((1, 1, wide), lambda i, *s: (i, 0, 0)),
            ],
            out_specs=[
                pl.BlockSpec((1, rows, LANES), lambda i, *s: (i, 0, 0)),
                pl.BlockSpec((1, LANES, wide), lambda i, *s: (i, 0, 0)),
                pl.BlockSpec((1, 1, wide), lambda i, *s: (i, 0, 0)),
            ],
            scratch_shapes=[pltpu.VMEM((total, wide), f32), pltpu.VMEM((rows, LANES), f32)],
        ),
        out_shape=[
            jax.ShapeDtypeStruct((count, rows, LANES), bf16),
            jax.ShapeDtypeStruct((count, LANES, wide), f32),
            jax.ShapeDtypeStruct((count, 1, wide), f32),
        ],
        compiler_params=params(),
        cost_estimate=pl.CostEstimate(
            flops=4 * count * wide * total * LANES,
            bytes_accessed=8 << 20,
            transcendentals=count * wide * total,
        ),
        name="attend",
    )(base, tiles, unit_places, qkv, qkv, turned, doc_slab, doc_q)


def attend_back_kernel(units, tile, base_ref, count_ref, units_ref, q_ref, k_ref, v_ref, kt_ref, doc_ref,
                       doc_q_ref, grad_ref, att_ref, lse_ref, cos_ref, sin_ref,
                       out_ref, dk_ref, dv_ref, acc_ref):
    block = pl.program_id(0)
    count = pl.num_programs(0)
    rows = acc_ref.shape[0]
    wide = att_ref.shape[2]
    part = wide // units

    @pl.when(block == 0)
    def _():
        dk_ref[...] = jnp.zeros(dk_ref.shape, f32)
        dv_ref[...] = jnp.zeros(dv_ref.shape, f32)

    def turn_back(values, span):
        return values * cos_ref[span, :] - rotate_half(values * sin_ref[span, :])

    queries = gather_rows(units_ref, q_ref, units, part)
    grads = gather_rows(units_ref, grad_ref.at[0], units, part)
    delta = jnp.sum(jnp.transpose(grads.astype(f32)) * att_ref[0], axis=0, keepdims=True)
    log_sum = lse_ref[0]
    doc_q = doc_q_ref[0]

    def step(at, grad_query):
        span = tile_span(base_ref, block, at, tile)
        scores = dot_tt(k_ref[span, :], queries)
        grad_probs = dot_tt(v_ref[span, :], grads)
        scores = jnp.where(across(doc_ref[span, :], wide) == doc_q, scores, NEG)
        probs = jnp.exp(scores - log_sum)
        dv_ref[span, :] += jnp.dot(probs.astype(bf16), grads, preferred_element_type=f32)
        grad_scores = (probs * (grad_probs - delta)).astype(bf16)
        dk_ref[span, :] += jnp.dot(grad_scores, queries, preferred_element_type=f32)
        return grad_query + jnp.dot(kt_ref[:, span], grad_scores, preferred_element_type=f32)

    grad_query = lax.fori_loop(
        0, count_ref[block], step, jnp.zeros((LANES, wide), f32)
    )
    scatter_rows(units_ref, acc_ref, jnp.transpose(grad_query) * HD**-0.5, units, part)
    here = pl.ds(pl.multiple_of(block * rows, rows), rows)
    out_ref[block, :, :LANES] = turn_back(acc_ref[...], here).astype(bf16)

    @pl.when(block == count - 1)
    def _():
        def finish(at, carry):
            span = pl.ds(pl.multiple_of(at * rows, rows), rows)
            out_ref[at, :, LANES : 2 * LANES] = turn_back(dk_ref[span, :], span).astype(bf16)
            out_ref[at, :, 2 * LANES :] = dv_ref[span, :].astype(bf16)
            return carry

        lax.fori_loop(0, count, finish, 0)


def attend_back(base, tiles, unit_places, qkv, turned, doc_slab, doc_q, grads, att, lse, cosine, sine,
                rows, tile):
    total = qkv.shape[0]
    count = total // rows
    units = unit_places.shape[0] // 2
    wide = doc_q.shape[2]
    whole = lambda part: pl.BlockSpec((total, LANES), lambda i, *s: (0, part))
    each = lambda *shape: pl.BlockSpec((1,) + shape, lambda i, *s: (i, 0, 0))
    return pl.pallas_call(
        functools.partial(attend_back_kernel, units, tile),
        grid_spec=pltpu.PrefetchScalarGridSpec(
            num_scalar_prefetch=3,
            grid=(count,),
            in_specs=[
                pl.BlockSpec((rows, LANES), lambda i, *s: (i, 0)),
                whole(1),
                whole(2),
                pl.BlockSpec((LANES, total), lambda i, *s: (0, 0)),
                whole(0),
                each(1, wide),
                each(rows, LANES),
                each(LANES, wide),
                each(1, wide),
                whole(0),
                whole(0),
            ],
            out_specs=pl.BlockSpec((count, rows, 3 * LANES), lambda i, *s: (0, 0, 0)),
            scratch_shapes=[
                pltpu.VMEM((total, LANES), f32),
                pltpu.VMEM((total, LANES), f32),
                pltpu.VMEM((rows, LANES), f32),
            ],
        ),
        out_shape=jax.ShapeDtypeStruct((count, rows, 3 * LANES), bf16),
        compiler_params=params(),
        cost_estimate=pl.CostEstimate(
            flops=10 * count * wide * total * LANES,
            bytes_accessed=12 << 20,
            transcendentals=count * wide * total,
        ),
        name="attend_back",
    )(base, tiles, unit_places, qkv, qkv, qkv, turned, doc_slab, doc_q, grads, att, lse, cosine, sine)


def join_heads(parts_ref, at, owners):
    rows = parts_ref.shape[1]
    side = lax.broadcasted_iota(jnp.int32, (rows, LANES), 1) // HD
    tiles = []
    for tile in range(len(owners) // SLOTS):
        column = jnp.zeros((rows, LANES), f32)
        for half in range(SLOTS):
            for c, slot in owners[tile * SLOTS + half]:
                slab = parts_ref[c, :, at : at + LANES].astype(f32)
                if slot != half:
                    slab = pltpu.roll(slab, HD, 1)
                column = column + jnp.where(side == half, slab, 0.0)
        tiles.append(column.astype(bf16))
    return jnp.concatenate(tiles, axis=1)


def middle_kernel(owners, first, att_ref, tokens_ref, gain_ref, cot_ref, weights_ref,
                  output_ref, grad_heads_ref, grad_middle_ref, attended_ref, branch_ref,
                  hidden_ref, grad_up_ref, product_ref,
                  proj_ref, up_ref, down_ref, sems):
    width = tokens_ref.shape[1]
    units = product_ref.shape[1]
    copies = []
    at = 0
    for i, ref in enumerate((proj_ref, up_ref, down_ref)):
        span = weights_ref.at[:, at : at + ref.shape[1]]
        copies.append(pltpu.make_async_copy(span, ref, sems.at[i]))
        copies[-1].start()
        at += ref.shape[1]
    gain = gain_ref[1:2, :]
    cot = cot_ref[...]
    attended = join_heads(att_ref, 0, owners)
    attended_ref[...] = attended
    copies[0].wait()
    middle = tokens_ref[...].astype(f32) + jnp.dot(
        attended, proj_ref[...], preferred_element_type=f32
    )
    normed, inverse = norm_rows(middle)
    hidden = (normed * gain).astype(bf16)
    hidden_ref[...] = hidden
    copies[1].wait()
    copies[2].wait()
    result = middle
    grad_hidden = jnp.zeros(middle.shape, f32)
    for at in range(0, units, CHUNK):
        one = slice(at, at + CHUNK)
        two = slice(units + at, units + at + CHUNK)
        inner = jnp.dot(hidden, up_ref[:, one], preferred_element_type=f32)
        gate = jnp.dot(hidden, up_ref[:, two], preferred_element_type=f32)
        grad_product = jnp.dot(cot, down_ref[:, one], preferred_element_type=f32)
        cdf = 0.5 * (1.0 + lax.erf(inner * ROOT_HALF))
        gelu_value = inner * cdf
        product = (gelu_value * gate).astype(bf16)
        product_ref[:, one] = product
        slope = cdf + inner * jnp.exp(-0.5 * inner * inner) * INV_ROOT_TWO_PI
        grad_inner = (grad_product * gate * slope).astype(bf16)
        grad_gate = (grad_product * gelu_value).astype(bf16)
        grad_up_ref[:, one] = grad_inner
        grad_up_ref[:, two] = grad_gate
        result = result + dot_tt(product, down_ref[:, one])
        grad_hidden = grad_hidden + dot_tt(grad_inner, up_ref[:, one])
        grad_hidden = grad_hidden + dot_tt(grad_gate, up_ref[:, two])
    output_ref[...] = result.astype(bf16)
    grad_middle = cot.astype(f32) + norm_back(grad_hidden * gain, normed, inverse)
    grad_middle_ref[...] = grad_middle
    grad_branch = grad_middle.astype(bf16)
    branch_ref[...] = grad_branch
    grad_attended = dot_tt(grad_branch, proj_ref[...])
    for c, head in enumerate(first):
        grad_heads_ref[c] = grad_attended[:, head * HD : head * HD + LANES].astype(bf16)


def middle_stage(owners, first, att_in, tokens, gains, cot, weights, units):
    rows, width = tokens.shape
    vmem = pl.BlockSpec(memory_space=pltpu.VMEM)
    shape = jax.ShapeDtypeStruct
    return pl.pallas_call(
        functools.partial(middle_kernel, owners, first),
        in_specs=[vmem] * 4 + [pl.BlockSpec(memory_space=pl.ANY)],
        out_specs=[vmem] * 8,
        out_shape=[
            shape((rows, width), bf16),
            shape((len(first), rows, LANES), bf16),
            shape((rows, width), f32),
            shape((rows, width), bf16),
            shape((rows, width), bf16),
            shape((rows, width), bf16),
            shape((rows, 2 * units), bf16),
            shape((rows, units), bf16),
        ],
        scratch_shapes=[
            pltpu.VMEM((width, width), bf16),
            pltpu.VMEM((width, 2 * units), bf16),
            pltpu.VMEM((width, units), bf16),
            pltpu.SemaphoreType.DMA((3,)),
        ],
        compiler_params=pltpu.CompilerParams(vmem_limit_bytes=VMEM_BYTES),
        cost_estimate=pl.CostEstimate(
            flops=4 * rows * width * (width + 3 * units),
            bytes_accessed=10 << 20,
            transcendentals=2 * rows * units,
        ),
        name="middle_stage",
    )(att_in, tokens, gains, cot, weights)


def finish_kernel(owners, at, parts_ref, tokens_ref, gain_ref, grad_ref, weights_ref, out_ref,
                  w_ref, sem):
    copy = pltpu.make_async_copy(weights_ref.at[:, at : at + w_ref.shape[1]], w_ref, sem)
    copy.start()
    joined = jnp.concatenate(
        [join_heads(parts_ref, part * LANES, owners) for part in range(3)], axis=1
    )
    normed, inverse = norm_rows(tokens_ref[...].astype(f32))
    copy.wait()
    grad_hidden = dot_tt(joined, w_ref[...])
    back = norm_back(grad_hidden * gain_ref[:1, :], normed, inverse)
    out_ref[...] = (grad_ref[...] + back).astype(bf16)


def finish(owners, at, parts, tokens, gains, grad_middle, weights):
    rows, width = tokens.shape
    vmem = pl.BlockSpec(memory_space=pltpu.VMEM)
    return pl.pallas_call(
        functools.partial(finish_kernel, owners, at),
        in_specs=[vmem] * 4 + [pl.BlockSpec(memory_space=pl.ANY)],
        out_specs=vmem,
        out_shape=jax.ShapeDtypeStruct((rows, width), bf16),
        scratch_shapes=[pltpu.VMEM((width, 3 * width), bf16), pltpu.SemaphoreType.DMA],
        compiler_params=pltpu.CompilerParams(vmem_limit_bytes=VMEM_BYTES),
        cost_estimate=pl.CostEstimate(
            flops=6 * rows * width * width, bytes_accessed=6 << 20, transcendentals=0
        ),
        name="finish",
    )(parts, tokens, gains, grad_middle, weights)


def split_rows(side, value, at, kept_ref, gone_ref):
    halves, share = kept_ref.shape[:2]
    span = slice(at, at + value.shape[1])
    for f in range(2 * halves):
        block = value[f * share : (f + 1) * share].astype(bf16)

        @pl.when(side == f % 2)
        def _():
            kept_ref[f // 2, :, span] = block

        @pl.when(side != f % 2)
        def _():
            gone_ref[f // 2, :, span] = block


def weight_grads_kernel(side_ref, *refs):
    kept_ref, gone_ref = refs[-2:]
    at = 0
    for left_ref, right_ref in zip(refs[0:-2:2], refs[1:-2:2]):
        left = jnp.transpose(left_ref[...])
        columns = right_ref.shape[1]
        for start in range(0, columns, CHUNK):
            value = jnp.dot(
                left, right_ref[:, start : start + CHUNK], preferred_element_type=f32
            )
            split_rows(side_ref[0], value, at + start, kept_ref, gone_ref)
        at += columns


def head_grads_kernel(side_ref, left_ref, right_ref, kept_ref, gone_ref, acc_ref):
    acc_ref[...] = jnp.zeros(acc_ref.shape, f32)
    count, rows, _ = right_ref.shape

    def step(at, carry):
        span = pl.ds(pl.multiple_of(at * rows, rows), rows)
        left = jnp.transpose(left_ref[span, :])
        acc_ref[...] += jnp.dot(left, right_ref[at], preferred_element_type=f32)
        return carry

    lax.fori_loop(0, count, step, 0)
    split_rows(side_ref[0], acc_ref[...], 0, kept_ref, gone_ref)


def split_grads(kernel, fsdp, side, operands, width, columns, scratch, name):
    vmem = pl.BlockSpec(memory_space=pltpu.VMEM)
    half = jax.ShapeDtypeStruct((fsdp // 2, width // fsdp, columns), bf16)
    rows = operands[0].shape[0]
    return pl.pallas_call(
        kernel,
        in_specs=[pl.BlockSpec(memory_space=pltpu.SMEM)] + [vmem] * len(operands),
        out_specs=[vmem, vmem],
        out_shape=[half, half],
        scratch_shapes=scratch,
        compiler_params=pltpu.CompilerParams(vmem_limit_bytes=VMEM_BYTES),
        cost_estimate=pl.CostEstimate(
            flops=2 * rows * width * columns, bytes_accessed=4 * width * columns, transcendentals=0
        ),
        name=name,
    )(side, *operands)


def halvings(count):
    return [1 << i for i in range(count.bit_length() - 1)]


def flips(count, bit):
    return [(i, i ^ bit) for i in range(count)]


def halve(blocks, index, bit):
    pairs = blocks.reshape((-1, 2) + blocks.shape[1:])
    side = index // bit % 2
    kept = lax.dynamic_index_in_dim(pairs, side, 1, keepdims=False)
    gone = lax.dynamic_index_in_dim(pairs, 1 - side, 1, keepdims=False)
    return kept, gone.astype(bf16)


def sum_rest(blocks, axis, count, index):
    while blocks.shape[0] > 1:
        bit = count // blocks.shape[0]
        kept, gone = halve(blocks, index // bit, 1)
        got = lax.ppermute(gone, axis, flips(count, bit))
        blocks = kept.astype(f32) + got.astype(f32)
    return blocks[0]


def exchange(blocks, axis, index):
    count = blocks.shape[0]
    held = blocks[:, None]
    masks = [0]
    for bit in halvings(count):
        pairs = held.reshape((-1, 2) + held.shape[1:])
        side = index // bit % 2
        kept = lax.dynamic_index_in_dim(pairs, side, 1, keepdims=False)
        gone = lax.dynamic_index_in_dim(pairs, 1 - side, 1, keepdims=False)
        got = lax.ppermute(gone, axis, flips(count, bit))
        held = jnp.concatenate([kept, got], axis=1)
        masks += [mask ^ bit for mask in masks]
    source = index ^ jnp.asarray(masks, jnp.int32)
    pick = jnp.arange(count, dtype=jnp.int32)[:, None] == source[None, :]
    return jnp.sum(jnp.where(pick[:, :, None, None], held.astype(f32), 0.0), axis=1)


def program(fsdp, ctx):
    def on_device(tokens, segment_ids, positions, gain_attn, w_qkv, w_out, gain_mlp, w_in, w_down,
                  cotangent):
        rows, width = tokens.shape[1:]
        shard = w_qkv.shape[0]
        heads = width // HD
        common = math.gcd(heads, ctx)
        splits = ctx // common
        units = heads // common
        part = rows // splits
        tile = KEY_TILE
        first = [min(units * c // splits, heads - SLOTS) for c in range(ctx)]
        owners = [
            [
                (c, slot)
                for c in range(ctx)
                for slot in range(SLOTS)
                if first[c] + slot == head
                and max(units * c, head * splits) < min(units * (c + 1), (head + 1) * splits)
            ]
            for head in range(heads)
        ]
        me = lax.axis_index("ctx")
        mine = lax.axis_index("fsdp")
        total = ctx * rows

        outer = ctx // 2
        ring = [(o * 2 + i, (o + 1) % outer * 2 + i) for o in range(outer) for i in range(2)]
        swap = [(c, c ^ 1) for c in range(ctx)]
        bits = halvings(fsdp)[::-1]
        masks = [0]
        own = [tokens[0]]
        other = []
        step = 0
        while step < outer or bits:
            if step > 0 and bits:
                bit = bits.pop(0)
                got = lax.ppermute(w_parts, "fsdp", flips(fsdp, bit))
                w_parts = jnp.concatenate([w_parts, got], axis=0)
                masks += [mask ^ bit for mask in masks]
            if step < outer:
                other.append(lax.ppermute(own[step], "ctx", swap))
            if step < outer - 1:
                own.append(lax.ppermute(own[step], "ctx", ring))
            if step == 0:
                sent = spread(first, w_qkv, gain_attn, gain_mlp, segment_ids, positions)
                sent = lax.all_to_all(sent, "ctx", 0, 0, tiled=True)
                w_parts = sent[:, :shard, :].reshape(1, ctx * shard, 4 * LANES)
            if step < outer - 1:
                own[-1], other[-1], w_parts = lax.optimization_barrier(
                    (own[-1], other[-1], w_parts)
                )
            step += 1
        infos = sent[:, shard : shard + 2, :].astype(f32)
        docs = infos[:, 0, :rows].astype(jnp.int32)
        spots = (infos[:, 0, rows:] * 64 + infos[:, 1, :rows]).reshape(total, 1)
        half = jnp.arange(LANES) % (HD // 2)
        rates = THETA ** (-2.0 * half.astype(f32) / HD)
        angles = spots * rates[None, :]
        cosine = jnp.cos(angles)
        sine = jnp.sin(angles)
        doc_slab = jnp.broadcast_to(docs.reshape(total, 1), (total, LANES))
        edges = docs.reshape(total // GRAIN, GRAIN)
        lo = jnp.sum((edges[None, :, -1] < docs[:, :1]).astype(jnp.int32), axis=1)
        hi = jnp.sum((edges[None, :, 0] <= docs[:, rows - 1 :]).astype(jnp.int32), axis=1)
        count = (hi - lo + tile // GRAIN - 1) // (tile // GRAIN)
        base = jnp.minimum(lo, total // GRAIN - count * (tile // GRAIN))
        unit = units * me + jnp.arange(units, dtype=jnp.int32)
        first_head = jnp.minimum(units * me // splits, heads - SLOTS)
        unit_slot = unit // splits - first_head
        unit_part = unit % splits
        unit_places = jnp.concatenate([unit_slot, unit_part]).astype(jnp.int32)
        pick = unit_part[:, None] == jnp.arange(splits, dtype=jnp.int32)[None, :]
        doc_q = jnp.sum(
            jnp.where(pick[None, :, :, None], docs.reshape(ctx, 1, splits, part), 0), axis=2
        ).reshape(ctx, 1, units * part)

        held = []
        for step in range(outer):
            at = jnp.stack([(me // 2 + outer - step) % outer, me % 2, mine]).astype(jnp.int32)
            *held, gains = project(
                masks, at, own[step], other[step], w_parts, cosine, sine, total, held
            )
        hidden_one, qkv, turned = held
        att_low, att, lse = attend(base, count, unit_places, qkv, turned, doc_slab, doc_q, rows, tile)
        att_in = lax.all_to_all(att_low, "ctx", 0, 0, tiled=True)

        packed = jnp.concatenate([w_out, w_in, w_down.T, w_qkv], axis=1)
        weights = lax.all_gather(packed, AXES, axis=0, tiled=True)

        cot = cotangent[0]
        output, grad_heads, grad_middle, attended, grad_branch, hidden_two, grad_up, product = (
            middle_stage(
                owners, first, att_in, tokens[0], gains, cot, weights, w_down.shape[0]
            )
        )
        grad_heads = lax.all_to_all(grad_heads, "ctx", 0, 0, tiled=True)

        side = (mine % 2).astype(jnp.int32).reshape(1)
        columns = packed.shape[1] - w_qkv.shape[1]
        kept, gone = split_grads(
            weight_grads_kernel, fsdp, side,
            [attended, grad_branch, hidden_two, grad_up, cot, product],
            width, columns, [], "weight_grads",
        )
        got = lax.ppermute(gone, "fsdp", flips(fsdp, 1))
        grad_heads, kept, got = lax.optimization_barrier((grad_heads, kept, got))
        grad_packed = kept.astype(f32) + got.astype(f32)
        grad_packed = sum_rest(grad_packed, "fsdp", fsdp, mine).reshape(ctx, shard, columns)
        kept, gone = halve(grad_packed, me, 1)
        got = lax.ppermute(gone, "ctx", flips(ctx, 1))

        grad_joined = attend_back(
            base, count, unit_places, qkv, turned, doc_slab, doc_q, grad_heads, att, lse, cosine,
            sine, rows, tile,
        )
        kept_cols, gone_cols = split_grads(
            head_grads_kernel, fsdp, side, [hidden_one, grad_joined], width, 3 * LANES,
            [pltpu.VMEM((width, 3 * LANES), f32)], "head_grads",
        )
        got_cols = lax.ppermute(gone_cols, "fsdp", flips(fsdp, 1))
        grad_cols = kept_cols.astype(f32) + got_cols.astype(f32)
        grad_cols = sum_rest(grad_cols, "fsdp", fsdp, mine)
        grad_joined = lax.all_to_all(grad_joined, "ctx", 0, 0, tiled=True)
        grad_joined, grad_cols, kept, got = lax.optimization_barrier(
            (grad_joined, grad_cols, kept, got)
        )
        input_grad = finish(
            owners, columns, grad_joined, tokens[0], gains, grad_middle, weights
        )
        grad_packed = sum_rest(kept.astype(f32) + got.astype(f32), "ctx", ctx, me)
        sum_w_out = grad_packed[:, :width]
        sum_w_in = grad_packed[:, width : width + w_in.shape[1]]
        sum_w_down = grad_packed[:, width + w_in.shape[1] :].T
        sum_gain_mlp = jnp.sum(w_in.astype(f32) * sum_w_in, axis=1) / gain_mlp.astype(f32)

        grad_cols = exchange(grad_cols.astype(bf16).reshape(ctx, shard, 3 * LANES), "ctx", me)
        pieces = []
        for part in range(3):
            for head in range(heads):
                column = 0.0
                for c, slot in owners[head]:
                    at = part * LANES + slot * HD
                    column = column + grad_cols[c, :, at : at + HD]
                pieces.append(column)
        sum_w_qkv = jnp.concatenate(pieces, axis=1)
        sum_gain_attn = jnp.sum(w_qkv.astype(f32) * sum_w_qkv, axis=1) / gain_attn.astype(f32)
        return (
            output[None],
            input_grad[None],
            sum_gain_attn,
            sum_w_qkv,
            sum_w_out,
            sum_gain_mlp,
            sum_w_in,
            sum_w_down,
        )

    return on_device


def solution(mesh):
    rows = P(AXES, None)
    tokens = P("fsdp", "ctx", None)
    return jax.shard_map(
        program(mesh.shape["fsdp"], mesh.shape["ctx"]),
        mesh=mesh,
        in_specs=(
            tokens,
            P("fsdp", "ctx"),
            P("fsdp", "ctx"),
            P(AXES),
            rows,
            rows,
            P(AXES),
            rows,
            P(None, AXES),
            tokens,
        ),
        out_specs=(tokens, tokens, P(AXES), rows, rows, P(AXES), rows, P(None, AXES)),
        check_vma=False,
    )
```

```python
import functools
import math

import jax
import jax.numpy as jnp
from jax import lax
from jax.experimental import pallas as pl
from jax.experimental.pallas import tpu as pltpu
from jax.sharding import PartitionSpec as P

HD = 64
SLOTS = 2
LANES = SLOTS * HD
GRAIN = 128
KEY_TILE = 512
CHUNK = 384
EPS = 1e-05
THETA = 160000.0
NEG = -1e30
ROOT_HALF = 0.7071067811865476
INV_ROOT_TWO_PI = 0.3989422804014327
VMEM_BYTES = 58 * 1024 * 1024
AXES = ("fsdp", "ctx")

f32 = jnp.float32
bf16 = jnp.bfloat16


def norm_rows(values):
    center = values - jnp.mean(values, axis=-1, keepdims=True)
    spread = jnp.mean(center * center, axis=-1, keepdims=True)
    inverse = lax.rsqrt(spread + EPS)
    return (center * inverse, inverse)


def norm_back(grad_normed, normed, inverse):
    return inverse * (
        grad_normed
        - jnp.mean(grad_normed, axis=-1, keepdims=True)
        - normed * jnp.mean(grad_normed * normed, axis=-1, keepdims=True)
    )


def rotate_half(values):
    lane = lax.broadcasted_iota(jnp.int32, values.shape, 1)
    ahead = pltpu.roll(values, LANES - HD // 2, 1)
    behind = pltpu.roll(values, HD // 2, 1)
    return jnp.where(lane % HD < HD // 2, -ahead, behind)


def dot_tt(left, right):
    return lax.dot_general(left, right, (((1,), (1,)), ((), ())), preferred_element_type=f32)


def dot_rows(left, right):
    return lax.dot_general(left, right, (((0,), (0,)), ((), ())), preferred_element_type=f32)


def params():
    return pltpu.CompilerParams(
        dimension_semantics=("arbitrary",), vmem_limit_bytes=VMEM_BYTES
    )


def spread_kernel(first, *refs):
    sems, out_ref = refs[-1], refs[5]
    copies = [
        pltpu.make_async_copy(refs[i], refs[6 + i], sems.at[i]) for i in range(5)
    ]
    for copy in copies:
        copy.start()
    for copy in copies:
        copy.wait()
    w_ref, gain_one_ref, gain_two_ref, doc_ref, place_ref = refs[6:11]
    shard, columns = w_ref.shape
    width = columns // 3
    rows = doc_ref.shape[1]
    square = (shard, shard)
    eye = lax.broadcasted_iota(jnp.int32, square, 0) == lax.broadcasted_iota(jnp.int32, square, 1)

    def upright(ref):
        spread = jnp.where(eye, ref[...].astype(f32), 0.0)
        return jnp.sum(spread, axis=1, keepdims=True).astype(bf16)

    lane = lax.broadcasted_iota(jnp.int32, (shard, LANES), 1)
    gains = jnp.where(
        lane == 0, upright(gain_one_ref), jnp.where(lane == 1, upright(gain_two_ref), bf16(0))
    )
    place = place_ref[...]
    top = jnp.concatenate([doc_ref[...], place >> 6], axis=1).astype(f32)
    low = jnp.concatenate([place & 63, jnp.zeros_like(place)], axis=1).astype(f32)
    row = lax.broadcasted_iota(jnp.int32, (8, 2 * rows), 0)
    places = jnp.where(row == 0, top, jnp.where(row == 1, low, 0.0)).astype(bf16)
    for c, head in enumerate(first):
        for part in range(3):
            at = part * width + head * HD
            out_ref[c, :shard, part * LANES : (part + 1) * LANES] = w_ref[:, at : at + LANES]
        out_ref[c, :shard, 3 * LANES :] = gains
        out_ref[c, shard:, :] = places


def spread(first, w_qkv, gain_one, gain_two, docs, places):
    shard = w_qkv.shape[0]
    operands = (w_qkv, gain_one[None], gain_two[None], docs, places)
    return pl.pallas_call(
        functools.partial(spread_kernel, first),
        in_specs=[pl.BlockSpec(memory_space=pl.ANY)] * 5,
        out_specs=pl.BlockSpec(memory_space=pltpu.VMEM),
        out_shape=jax.ShapeDtypeStruct((len(first), shard + 8, 4 * LANES), bf16),
        scratch_shapes=[pltpu.VMEM(array.shape, array.dtype) for array in operands]
        + [pltpu.SemaphoreType.DMA((5,))],
        compiler_params=pltpu.CompilerParams(vmem_limit_bytes=VMEM_BYTES),
        name="spread",
    )(*operands)


def ready_kernel(masks, at_ref, w_ref, w_out_ref, gains_ref):
    share = w_ref.shape[1]
    for i, mask in enumerate(masks):
        start = pl.multiple_of((at_ref[0] ^ mask) * share, share)
        w_out_ref[pl.ds(start, share), :] = w_ref[i]
    gains_ref[...] = jnp.transpose(w_out_ref[:, 3 * LANES :].astype(f32))[:8]


def ready(masks, at, w_parts):
    count, share, columns = w_parts.shape
    vmem = pl.BlockSpec(memory_space=pltpu.VMEM)
    return pl.pallas_call(
        functools.partial(ready_kernel, masks),
        in_specs=[pl.BlockSpec(memory_space=pltpu.SMEM), vmem],
        out_specs=[vmem, vmem],
        out_shape=[
            jax.ShapeDtypeStruct((count * share, columns), bf16),
            jax.ShapeDtypeStruct((8, count * share), f32),
        ],
        compiler_params=pltpu.CompilerParams(vmem_limit_bytes=VMEM_BYTES),
        name="ready",
    )(at, w_parts)


def project_kernel(at_ref, own_ref, other_ref, w_ref, gains_ref, cos_ref, sin_ref, *refs):
    hidden_ref, qkv_ref, turned_ref = refs[-3:]
    own = pl.program_id(0) == 0
    x = jnp.where(own, own_ref[...], other_ref[...]).astype(f32)
    normed, _ = norm_rows(x)
    hidden = (normed * gains_ref[:1, :]).astype(bf16)
    hidden_ref[...] = hidden
    joined = jnp.dot(hidden, w_ref[...], preferred_element_type=f32)
    cosine = cos_ref[...]
    sine = sin_ref[...]
    query = joined[:, :LANES]
    keys = joined[:, LANES : 2 * LANES]
    values = joined[:, 2 * LANES :]
    query = (query * cosine + rotate_half(query) * sine).astype(bf16)
    keys = keys * cosine + rotate_half(keys) * sine
    qkv_ref[:, :LANES] = query * bf16(HD**-0.5)
    qkv_ref[:, LANES : 2 * LANES] = keys.astype(bf16)
    qkv_ref[:, 2 * LANES :] = values.astype(bf16)
    turned_ref[:LANES, :] = jnp.transpose(keys).astype(bf16)
    turned_ref[LANES:, :] = jnp.transpose(values).astype(bf16)


def project(at, own, other, w_heads, gains, cosine, sine, total, held):
    rows, width = own.shape
    fixed = lambda *shape: pl.BlockSpec(shape, lambda i, at: (0,) * len(shape))
    block = lambda i, at: at[0] * 2 + (at[1] ^ i)
    tall = lambda width: pl.BlockSpec((rows, width), lambda i, at: (block(i, at), 0))
    shapes = [
        jax.ShapeDtypeStruct((total, width), bf16),
        jax.ShapeDtypeStruct((total, 3 * LANES), bf16),
        jax.ShapeDtypeStruct((2 * LANES, total), bf16),
    ]
    return pl.pallas_call(
        project_kernel,
        grid_spec=pltpu.PrefetchScalarGridSpec(
            num_scalar_prefetch=1,
            grid=(2,),
            in_specs=[
                fixed(rows, width),
                fixed(rows, width),
                fixed(width, 3 * LANES),
                fixed(8, width),
                tall(LANES),
                tall(LANES),
            ]
            + [pl.BlockSpec(memory_space=pl.ANY) for _ in held],
            out_specs=[
                tall(width),
                tall(3 * LANES),
                pl.BlockSpec((2 * LANES, rows), lambda i, at: (0, block(i, at))),
            ],
        ),
        out_shape=shapes,
        input_output_aliases={7 + i: i for i in range(len(held))},
        compiler_params=params(),
        cost_estimate=pl.CostEstimate(
            flops=2 * 2 * rows * width * 3 * LANES, bytes_accessed=6 << 20, transcendentals=0
        ),
        name="project",
    )(at, own, other, w_heads, gains, cosine, sine, *held)


def gather_rows(units_ref, ref, units, part):
    lane = lax.broadcasted_iota(jnp.int32, (part, LANES), 1)
    chunks = []
    for i in range(units):
        start = pl.multiple_of(units_ref[units + i] * part, part)
        chunk = ref[pl.ds(start, part), :]
        chunks.append(jnp.where(lane // HD == units_ref[i], chunk, jnp.zeros_like(chunk)))
    return jnp.concatenate(chunks, axis=0)


def scatter_rows(units_ref, acc_ref, values, units, part):
    lane = lax.broadcasted_iota(jnp.int32, (part, LANES), 1)
    acc_ref[...] = jnp.zeros(acc_ref.shape, f32)
    for i in range(units):
        start = pl.multiple_of(units_ref[units + i] * part, part)
        chunk = values[i * part : (i + 1) * part]
        acc_ref[pl.ds(start, part), :] += jnp.where(lane // HD == units_ref[i], chunk, 0.0)


def across(slab, wide):
    if wide <= LANES:
        return slab[:, :wide]
    return jnp.concatenate([slab] * (wide // LANES), axis=1)


def fold(values, reduce):
    rows, wide = values.shape
    return reduce(values.reshape(rows // 8, 8, wide), axis=0)


def tile_span(base_ref, block, at, tile):
    return pl.ds(pl.multiple_of(base_ref[block] * GRAIN + at * tile, GRAIN), tile)


def attend_kernel(units, tile, base_ref, count_ref, units_ref, q_ref, k_ref, vt_ref, doc_ref, doc_q_ref,
                  low_ref, att_ref, lse_ref, s_ref, acc_ref):
    block = pl.program_id(0)
    wide = s_ref.shape[1]
    part = wide // units
    queries = gather_rows(units_ref, q_ref, units, part)
    doc_q = doc_q_ref[0]

    def score(at, top):
        span = tile_span(base_ref, block, at, tile)
        scores = dot_tt(k_ref[span, :], queries)
        scores = jnp.where(across(doc_ref[span, :], wide) == doc_q, scores, NEG)
        s_ref[span, :] = scores
        return jnp.maximum(top, fold(scores, jnp.max))

    count = count_ref[block]
    top = lax.fori_loop(0, count, score, jnp.full((8, wide), NEG, f32))
    top = jnp.max(top, axis=0, keepdims=True)

    def weigh(at, carry):
        total, accum = carry
        span = tile_span(base_ref, block, at, tile)
        expo = jnp.exp(s_ref[span, :] - top)
        total = total + fold(expo, jnp.sum)
        accum = accum + jnp.dot(vt_ref[:, span], expo.astype(bf16), preferred_element_type=f32)
        return (total, accum)

    total, accum = lax.fori_loop(
        0, count, weigh, (jnp.zeros((8, wide), f32), jnp.zeros((LANES, wide), f32))
    )
    total = jnp.sum(total, axis=0, keepdims=True)
    att = accum / total
    att_ref[0] = att
    lse_ref[0] = top + jnp.log(total)
    scatter_rows(units_ref, acc_ref, jnp.transpose(att), units, part)
    low_ref[0] = acc_ref[...].astype(bf16)


def attend(base, tiles, unit_places, qkv, turned, doc_slab, doc_q, rows, tile):
    total = qkv.shape[0]
    count = total // rows
    units = unit_places.shape[0] // 2
    wide = doc_q.shape[2]
    return pl.pallas_call(
        functools.partial(attend_kernel, units, tile),
        grid_spec=pltpu.PrefetchScalarGridSpec(
            num_scalar_prefetch=3,
            grid=(count,),
            in_specs=[
                pl.BlockSpec((rows, LANES), lambda i, *s: (i, 0)),
                pl.BlockSpec((total, LANES), lambda i, *s: (0, 1)),
                pl.BlockSpec((LANES, total), lambda i, *s: (1, 0)),
                pl.BlockSpec((total, LANES), lambda i, *s: (0, 0)),
                pl.BlockSpec((1, 1, wide), lambda i, *s: (i, 0, 0)),
            ],
            out_specs=[
                pl.BlockSpec((1, rows, LANES), lambda i, *s: (i, 0, 0)),
                pl.BlockSpec((1, LANES, wide), lambda i, *s: (i, 0, 0)),
                pl.BlockSpec((1, 1, wide), lambda i, *s: (i, 0, 0)),
            ],
            scratch_shapes=[pltpu.VMEM((total, wide), f32), pltpu.VMEM((rows, LANES), f32)],
        ),
        out_shape=[
            jax.ShapeDtypeStruct((count, rows, LANES), bf16),
            jax.ShapeDtypeStruct((count, LANES, wide), f32),
            jax.ShapeDtypeStruct((count, 1, wide), f32),
        ],
        compiler_params=params(),
        cost_estimate=pl.CostEstimate(
            flops=4 * count * wide * total * LANES,
            bytes_accessed=8 << 20,
            transcendentals=count * wide * total,
        ),
        name="attend",
    )(base, tiles, unit_places, qkv, qkv, turned, doc_slab, doc_q)


def attend_back_kernel(units, tile, base_ref, count_ref, units_ref, q_ref, k_ref, v_ref, kt_ref, doc_ref,
                       doc_q_ref, grad_ref, att_ref, lse_ref, cos_ref, sin_ref,
                       out_ref, dk_ref, dv_ref, acc_ref):
    block = pl.program_id(0)
    count = pl.num_programs(0)
    rows = acc_ref.shape[0]
    wide = att_ref.shape[2]
    part = wide // units

    @pl.when(block == 0)
    def _():
        dk_ref[...] = jnp.zeros(dk_ref.shape, f32)
        dv_ref[...] = jnp.zeros(dv_ref.shape, f32)

    def turn_back(values, span):
        return values * cos_ref[span, :] - rotate_half(values * sin_ref[span, :])

    queries = gather_rows(units_ref, q_ref, units, part)
    grads = gather_rows(units_ref, grad_ref.at[0], units, part)
    delta = jnp.sum(jnp.transpose(grads.astype(f32)) * att_ref[0], axis=0, keepdims=True)
    log_sum = lse_ref[0]
    doc_q = doc_q_ref[0]

    def step(at, grad_query):
        span = tile_span(base_ref, block, at, tile)
        scores = dot_tt(k_ref[span, :], queries)
        grad_probs = dot_tt(v_ref[span, :], grads)
        scores = jnp.where(across(doc_ref[span, :], wide) == doc_q, scores, NEG)
        probs = jnp.exp(scores - log_sum)
        dv_ref[span, :] += jnp.dot(probs.astype(bf16), grads, preferred_element_type=f32)
        grad_scores = (probs * (grad_probs - delta)).astype(bf16)
        dk_ref[span, :] += jnp.dot(grad_scores, queries, preferred_element_type=f32)
        return grad_query + jnp.dot(kt_ref[:, span], grad_scores, preferred_element_type=f32)

    grad_query = lax.fori_loop(
        0, count_ref[block], step, jnp.zeros((LANES, wide), f32)
    )
    scatter_rows(units_ref, acc_ref, jnp.transpose(grad_query) * HD**-0.5, units, part)
    here = pl.ds(pl.multiple_of(block * rows, rows), rows)
    out_ref[block, :, :LANES] = turn_back(acc_ref[...], here).astype(bf16)

    @pl.when(block == count - 1)
    def _():
        def finish(at, carry):
            span = pl.ds(pl.multiple_of(at * rows, rows), rows)
            out_ref[at, :, LANES : 2 * LANES] = turn_back(dk_ref[span, :], span).astype(bf16)
            out_ref[at, :, 2 * LANES :] = dv_ref[span, :].astype(bf16)
            return carry

        lax.fori_loop(0, count, finish, 0)


def attend_back(base, tiles, unit_places, qkv, turned, doc_slab, doc_q, grads, att, lse, cosine, sine,
                rows, tile):
    total = qkv.shape[0]
    count = total // rows
    units = unit_places.shape[0] // 2
    wide = doc_q.shape[2]
    whole = lambda part: pl.BlockSpec((total, LANES), lambda i, *s: (0, part))
    each = lambda *shape: pl.BlockSpec((1,) + shape, lambda i, *s: (i, 0, 0))
    return pl.pallas_call(
        functools.partial(attend_back_kernel, units, tile),
        grid_spec=pltpu.PrefetchScalarGridSpec(
            num_scalar_prefetch=3,
            grid=(count,),
            in_specs=[
                pl.BlockSpec((rows, LANES), lambda i, *s: (i, 0)),
                whole(1),
                whole(2),
                pl.BlockSpec((LANES, total), lambda i, *s: (0, 0)),
                whole(0),
                each(1, wide),
                each(rows, LANES),
                each(LANES, wide),
                each(1, wide),
                whole(0),
                whole(0),
            ],
            out_specs=pl.BlockSpec((count, rows, 3 * LANES), lambda i, *s: (0, 0, 0)),
            scratch_shapes=[
                pltpu.VMEM((total, LANES), f32),
                pltpu.VMEM((total, LANES), f32),
                pltpu.VMEM((rows, LANES), f32),
            ],
        ),
        out_shape=jax.ShapeDtypeStruct((count, rows, 3 * LANES), bf16),
        compiler_params=params(),
        cost_estimate=pl.CostEstimate(
            flops=10 * count * wide * total * LANES,
            bytes_accessed=12 << 20,
            transcendentals=count * wide * total,
        ),
        name="attend_back",
    )(base, tiles, unit_places, qkv, qkv, qkv, turned, doc_slab, doc_q, grads, att, lse, cosine, sine)


def join_heads(parts_ref, at, owners):
    rows = parts_ref.shape[1]
    side = lax.broadcasted_iota(jnp.int32, (rows, LANES), 1) // HD
    tiles = []
    for tile in range(len(owners) // SLOTS):
        column = jnp.zeros((rows, LANES), f32)
        for half in range(SLOTS):
            for c, slot in owners[tile * SLOTS + half]:
                slab = parts_ref[c, :, at : at + LANES].astype(f32)
                if slot != half:
                    slab = pltpu.roll(slab, HD, 1)
                column = column + jnp.where(side == half, slab, 0.0)
        tiles.append(column.astype(bf16))
    return jnp.concatenate(tiles, axis=1)


def fetch_rows(place_ref, metas, refs, target_ref, at, sems):
    copies = []
    for ref, blocks in zip(refs, metas):
        for index, (flip, back) in enumerate(blocks):
            count = ref.shape[1]
            turn = lax.rem(place_ref[1] + place_ref[2] - back, place_ref[2])
            row = (place_ref[0] ^ flip) * place_ref[3] + turn * count
            row = pl.multiple_of(row, count) if count < target_ref.shape[0] else 0
            target = target_ref.at[pl.ds(row, count), pl.ds(at, ref.shape[2])]
            copies.append(pltpu.make_async_copy(ref.at[index], target, sems.at[len(copies)]))
            copies[-1].start()
    return copies


def middle_kernel(owners, first, metas, cut, place_ref, att_ref, tokens_ref, gain_ref, cot_ref,
                  *refs):
    count = len(metas[0]) + len(metas[1])
    sources = refs[:count]
    (output_ref, grad_heads_ref, grad_middle_ref, attended_ref, branch_ref, hidden_ref,
     grad_up_ref, product_ref, w_ref, sems_a, sems_b) = refs[count:]
    width = tokens_ref.shape[1]
    units = product_ref.shape[1]
    copies_a = fetch_rows(place_ref, metas[0], sources[: len(metas[0])], w_ref, 0, sems_a)
    copies_b = fetch_rows(place_ref, metas[1], sources[len(metas[0]) :], w_ref, cut, sems_b)
    up = width
    down = width + 2 * units
    gain = gain_ref[1:2, :]
    cot = cot_ref[...]
    attended = join_heads(att_ref, 0, owners)
    attended_ref[...] = attended
    for copy in copies_a:
        copy.wait()
    middle = tokens_ref[...].astype(f32) + jnp.dot(
        attended, w_ref[:, :width], preferred_element_type=f32
    )
    normed, inverse = norm_rows(middle)
    hidden = (normed * gain).astype(bf16)
    hidden_ref[...] = hidden
    for copy in copies_b:
        copy.wait()
    result = middle
    grad_hidden = jnp.zeros(middle.shape, f32)
    for at in range(0, units, CHUNK):
        one = slice(at, at + CHUNK)
        two = slice(units + at, units + at + CHUNK)
        w_one = w_ref[:, up + at : up + at + CHUNK]
        w_two = w_ref[:, up + units + at : up + units + at + CHUNK]
        w_down = w_ref[:, down + at : down + at + CHUNK]
        inner = jnp.dot(hidden, w_one, preferred_element_type=f32)
        gate = jnp.dot(hidden, w_two, preferred_element_type=f32)
        grad_product = jnp.dot(cot, w_down, preferred_element_type=f32)
        cdf = 0.5 * (1.0 + lax.erf(inner * ROOT_HALF))
        gelu_value = inner * cdf
        product = (gelu_value * gate).astype(bf16)
        product_ref[:, one] = product
        slope = cdf + inner * jnp.exp(-0.5 * inner * inner) * INV_ROOT_TWO_PI
        grad_inner = (grad_product * gate * slope).astype(bf16)
        grad_gate = (grad_product * gelu_value).astype(bf16)
        grad_up_ref[:, one] = grad_inner
        grad_up_ref[:, two] = grad_gate
        result = result + dot_tt(product, w_down)
        grad_hidden = grad_hidden + dot_tt(grad_inner, w_one)
        grad_hidden = grad_hidden + dot_tt(grad_gate, w_two)
    output_ref[...] = result.astype(bf16)
    grad_middle = cot.astype(f32) + norm_back(grad_hidden * gain, normed, inverse)
    grad_middle_ref[...] = grad_middle
    grad_branch = grad_middle.astype(bf16)
    branch_ref[...] = grad_branch
    grad_attended = dot_tt(grad_branch, w_ref[:, :width])
    for c, head in enumerate(first):
        grad_heads_ref[c] = grad_attended[:, head * HD : head * HD + LANES].astype(bf16)


def middle_stage(owners, first, place, att_in, tokens, gains, cot, parts_a, parts_b, units):
    rows, width = tokens.shape
    arrays = [[array for array, _ in parts] for parts in (parts_a, parts_b)]
    metas = [[blocks for _, blocks in parts] for parts in (parts_a, parts_b)]
    vmem = pl.BlockSpec(memory_space=pltpu.VMEM)
    shape = jax.ShapeDtypeStruct
    return pl.pallas_call(
        functools.partial(middle_kernel, owners, first, metas, arrays[0][0].shape[-1]),
        in_specs=[pl.BlockSpec(memory_space=pltpu.SMEM)]
        + [vmem] * 4
        + [pl.BlockSpec(memory_space=pl.ANY)] * (len(arrays[0]) + len(arrays[1])),
        out_specs=[vmem] * 8,
        out_shape=[
            shape((rows, width), bf16),
            shape((len(first), rows, LANES), bf16),
            shape((rows, width), f32),
            shape((rows, width), bf16),
            shape((rows, width), bf16),
            shape((rows, width), bf16),
            shape((rows, 2 * units), bf16),
            shape((rows, units), bf16),
        ],
        scratch_shapes=[pltpu.VMEM((width, 2 * arrays[0][0].shape[-1]), bf16)]
        + [pltpu.SemaphoreType.DMA((sum(len(b) for b in blocks),)) for blocks in metas],
        compiler_params=pltpu.CompilerParams(vmem_limit_bytes=VMEM_BYTES),
        cost_estimate=pl.CostEstimate(
            flops=6 * rows * width * (width + 3 * units),
            bytes_accessed=10 << 20,
            transcendentals=2 * rows * units,
        ),
        name="middle_stage",
    )(place, att_in, tokens, gains, cot, *arrays[0], *arrays[1])


def settle_kernel(metas, place_ref, *refs):
    out_ref, sems = refs[-2:]
    for copy in fetch_rows(place_ref, metas, refs[:-2], out_ref, 0, sems):
        copy.wait()


def settle(place, parts, width):
    arrays = [array for array, _ in parts]
    metas = [blocks for _, blocks in parts]
    anywhere = pl.BlockSpec(memory_space=pl.ANY)
    return pl.pallas_call(
        functools.partial(settle_kernel, metas),
        in_specs=[pl.BlockSpec(memory_space=pltpu.SMEM)] + [anywhere] * len(arrays),
        out_specs=pl.BlockSpec(memory_space=pltpu.VMEM),
        out_shape=jax.ShapeDtypeStruct((width, arrays[0].shape[-1]), bf16),
        scratch_shapes=[pltpu.SemaphoreType.DMA((sum(len(b) for b in metas),))],
        compiler_params=pltpu.CompilerParams(vmem_limit_bytes=VMEM_BYTES),
        cost_estimate=pl.CostEstimate(flops=0, bytes_accessed=8 << 20, transcendentals=0),
        name="settle",
    )(place, *arrays)


def finish_kernel(owners, parts_ref, tokens_ref, gain_ref, grad_ref, w_ref, out_ref):
    joined = jnp.concatenate(
        [join_heads(parts_ref, part * LANES, owners) for part in range(3)], axis=1
    )
    normed, inverse = norm_rows(tokens_ref[...].astype(f32))
    grad_hidden = dot_tt(joined, w_ref[...])
    back = norm_back(grad_hidden * gain_ref[:1, :], normed, inverse)
    out_ref[...] = (grad_ref[...] + back).astype(bf16)


def finish(owners, joined, tokens, gains, grad_middle, w_joined):
    rows, width = tokens.shape
    vmem = pl.BlockSpec(memory_space=pltpu.VMEM)
    return pl.pallas_call(
        functools.partial(finish_kernel, owners),
        in_specs=[vmem] * 5,
        out_specs=vmem,
        out_shape=jax.ShapeDtypeStruct((rows, width), bf16),
        compiler_params=pltpu.CompilerParams(vmem_limit_bytes=VMEM_BYTES),
        cost_estimate=pl.CostEstimate(
            flops=6 * rows * width * width, bytes_accessed=6 << 20, transcendentals=0
        ),
        name="finish",
    )(joined, tokens, gains, grad_middle, w_joined)


def half_rows(pairs, side, share, refs, lt_ref, emit):
    at = 0
    for pair in range(pairs):
        lt_ref[pair] = jnp.transpose(refs[2 * pair][...])
    for pair in range(pairs):
        right_ref = refs[2 * pair + 1]
        columns = right_ref.shape[1]
        for start in range(0, columns, CHUNK):
            right = right_ref[:, start : start + CHUNK]
            for half in range(lt_ref.shape[1] // share // 2):
                row = pl.multiple_of((2 * half + side) * share, share)
                emit(
                    half,
                    at + start,
                    jnp.dot(lt_ref[pair, pl.ds(row, share), :], right, preferred_element_type=f32),
                )
        at += columns


def pieces_of(cut, at, value):
    end = at + value.shape[1]
    found = []
    if at < cut:
        found.append((0, at, value[:, : min(end, cut) - at]))
    if end > cut:
        found.append((1, max(at, cut) - cut, value[:, max(at, cut) - at :]))
    return found


def gone_grads_kernel(pairs, cut, sides_ref, *refs):
    outs = refs[2 * pairs : 2 * pairs + 2]
    share = outs[0].shape[1]

    def emit(half, at, value):
        for which, start, piece in pieces_of(cut, at, value):
            span = slice(start, start + piece.shape[1])
            outs[which][half, :, span] = piece.astype(bf16)

    half_rows(pairs, 1 - sides_ref[0], share, refs, refs[-1], emit)


def kept_grads_kernel(pairs, cut, sides_ref, *refs):
    gots = refs[2 * pairs : 2 * pairs + 2]
    mine_a, other_a, mine_b, other_b = refs[2 * pairs + 2 : 2 * pairs + 6]
    share = gots[0].shape[1]
    shard = mine_b.shape[1]
    outer = share // shard // 2

    def emit(half, at, value):
        for which, start, piece in pieces_of(cut, at, value):
            span = slice(start, start + piece.shape[1])
            total = (piece + gots[which][half, :, span].astype(f32)).astype(bf16)
            if which == 0:

                @pl.when(sides_ref[1] == half)
                def _():
                    mine_a[0, :, span] = total

                @pl.when(sides_ref[1] != half)
                def _():
                    other_a[0, :, span] = total

            else:
                for x in range(2):
                    to = (mine_b, other_b)

                    @pl.when(sides_ref[2] == x)
                    def _():
                        for z in range(outer):
                            for flip in range(2):
                                row = (z * 2 + (x ^ flip)) * shard
                                to[flip][half * outer + z, :, span] = total[row : row + shard]

    half_rows(pairs, sides_ref[0], share, refs, refs[-1], emit)


def weight_grads(kernel, sides, operands, gots, outs, cut, name):
    vmem = pl.BlockSpec(memory_space=pltpu.VMEM)
    rows, width = operands[0].shape
    columns = sum(array.shape[1] for array in operands[1::2])
    return pl.pallas_call(
        functools.partial(kernel, len(operands) // 2, cut),
        in_specs=[pl.BlockSpec(memory_space=pltpu.SMEM)] + [vmem] * (len(operands) + len(gots)),
        out_specs=[vmem] * len(outs),
        out_shape=[jax.ShapeDtypeStruct(shape, bf16) for shape in outs],
        scratch_shapes=[pltpu.VMEM((len(operands) // 2, width, rows), bf16)],
        compiler_params=pltpu.CompilerParams(vmem_limit_bytes=VMEM_BYTES),
        cost_estimate=pl.CostEstimate(
            flops=rows * width * columns, bytes_accessed=3 * width * columns, transcendentals=0
        ),
        name=name,
    )(sides, *operands, *gots)


def head_grads_kernel(sides_ref, left_ref, right_ref, kept_ref, gone_ref, acc_ref):
    acc_ref[...] = jnp.zeros(acc_ref.shape, f32)
    count, rows, _ = right_ref.shape
    halves, share = kept_ref.shape[:2]

    def step(at, carry):
        span = pl.ds(pl.multiple_of(at * rows, rows), rows)
        left = jnp.transpose(left_ref[span, :])
        acc_ref[...] += jnp.dot(left, right_ref[at], preferred_element_type=f32)
        return carry

    lax.fori_loop(0, count, step, 0)
    for half in range(halves):
        for flip, ref in enumerate((kept_ref, gone_ref)):
            row = pl.multiple_of((2 * half + (sides_ref[0] ^ flip)) * share, share)
            ref[half] = acc_ref[pl.ds(row, share), :].astype(bf16)


def head_grads(fsdp, sides, hidden, grad_joined):
    total, width = hidden.shape
    columns = grad_joined.shape[2]
    vmem = pl.BlockSpec(memory_space=pltpu.VMEM)
    half = jax.ShapeDtypeStruct((fsdp // 2, width // fsdp, columns), bf16)
    return pl.pallas_call(
        head_grads_kernel,
        in_specs=[pl.BlockSpec(memory_space=pltpu.SMEM), vmem, vmem],
        out_specs=[vmem, vmem],
        out_shape=[half, half],
        scratch_shapes=[pltpu.VMEM((width, columns), f32)],
        compiler_params=pltpu.CompilerParams(vmem_limit_bytes=VMEM_BYTES),
        cost_estimate=pl.CostEstimate(
            flops=2 * total * width * columns,
            bytes_accessed=2 * total * (width + columns),
            transcendentals=0,
        ),
        name="head_grads",
    )(sides, hidden, grad_joined)


def add_halves_kernel(picks, joined, sides_ref, *refs):
    pairs = len(picks)
    outs = refs[2 * pairs :]
    begin = 0
    for i, pick in enumerate(picks):
        kept_ref, got_ref = refs[2 * i], refs[2 * i + 1]
        columns = kept_ref.shape[-1]
        for at in range(kept_ref.shape[0]):
            for flip in range(2):
                side = sides_ref[pick] ^ flip
                total = kept_ref[at, side].astype(f32) + got_ref[at, side].astype(f32)
                if joined:
                    outs[flip][at, :, begin : begin + columns] = total.astype(bf16)
                else:
                    outs[2 * i + flip][at] = total.astype(bf16)
        begin += columns


def add_halves(sides, pairs, joined=False):
    flat = []
    shapes = []
    for kept, got, axis, _ in pairs:
        shape = kept.shape
        shape = (
            math.prod(shape[:axis]), 2, math.prod(shape[axis + 1 : -1]), shape[-1]
        )
        flat += [kept.reshape(shape), got.reshape(shape)]
        shapes += [(shape[0], shape[2], shape[3])] * 2
    if joined:
        columns = sum(shape[2] for shape in shapes) // 2
        shapes = [shapes[0][:2] + (columns,)] * 2
    vmem = pl.BlockSpec(memory_space=pltpu.VMEM)
    size = sum(array.size for array in flat)
    return pl.pallas_call(
        functools.partial(add_halves_kernel, [pair[3] for pair in pairs], joined),
        in_specs=[pl.BlockSpec(memory_space=pltpu.SMEM)] + [vmem] * len(flat),
        out_specs=[vmem] * len(shapes),
        out_shape=[jax.ShapeDtypeStruct(shape, bf16) for shape in shapes],
        compiler_params=pltpu.CompilerParams(vmem_limit_bytes=VMEM_BYTES),
        cost_estimate=pl.CostEstimate(flops=size, bytes_accessed=3 * size, transcendentals=0),
        name="add_halves",
    )(sides, *flat)


def flips(count, bit):
    return [(i, i ^ bit) for i in range(count)]


def gate(*values):
    return lax.optimization_barrier(values)


def program(fsdp, ctx):
    def on_device(tokens, segment_ids, positions, gain_attn, w_qkv, w_out, gain_mlp, w_in, w_down,
                  cotangent):
        rows, width = tokens.shape[1:]
        shard = w_qkv.shape[0]
        share = ctx * shard
        heads = width // HD
        common = math.gcd(heads, ctx)
        splits = ctx // common
        units = heads // common
        part = rows // splits
        total = ctx * rows
        outer = ctx // 2
        first = [min(units * c // splits, heads - SLOTS) for c in range(ctx)]
        owners = [
            [
                (c, slot)
                for c in range(ctx)
                for slot in range(SLOTS)
                if first[c] + slot == head
                and max(units * c, head * splits) < min(units * (c + 1), (head + 1) * splits)
            ]
            for head in range(heads)
        ]
        me = lax.axis_index("ctx")
        mine = lax.axis_index("fsdp")
        sides = jnp.stack([mine % 2, mine // 2 % 2, me % 2, me // 2 % 2, me // 4 % 2])
        sides = sides.astype(jnp.int32)
        place = jnp.stack([mine, me // 2, 0 * me + outer, 0 * me + share]).astype(jnp.int32)
        swap = flips(ctx, 1)
        turn = lambda back: [
            (o * 2 + i, (o + back) % outer * 2 + i) for o in range(outer) for i in range(2)
        ]
        by_y = flips(fsdp, 2)
        by_core = flips(fsdp, 1)
        by_hand = (fsdp, ctx) == (4, 8) and shard % 8 == 0
        tile = KEY_TILE
        cot = cotangent[0]
        packed = jnp.concatenate([w_out, w_in, w_down.T], axis=1)
        columns = packed.shape[1]
        cut = (columns // LANES + 1) // 2 * LANES

        def weave(own, got):
            low = jnp.where(me % 2 == 0, own, got)
            high = jnp.where(me % 2 == 0, got, own)
            return jnp.concatenate([low, high], axis=1)

        def tables(sent):
            infos = sent[:, shard : shard + 2, :].astype(f32)
            docs = infos[:, 0, :rows].astype(jnp.int32)
            spots = (infos[:, 0, rows:] * 64 + infos[:, 1, :rows]).reshape(total, 1)
            half = jnp.arange(LANES) % (HD // 2)
            rates = THETA ** (-2.0 * half.astype(f32) / HD)
            angles = spots * rates[None, :]
            doc_slab = jnp.broadcast_to(docs.reshape(total, 1), (total, LANES))
            edges = docs.reshape(total // GRAIN, GRAIN)
            lo = jnp.sum((edges[None, :, -1] < docs[:, :1]).astype(jnp.int32), axis=1)
            hi = jnp.sum((edges[None, :, 0] <= docs[:, rows - 1 :]).astype(jnp.int32), axis=1)
            count = (hi - lo + tile // GRAIN - 1) // (tile // GRAIN)
            base = jnp.minimum(lo, total // GRAIN - count * (tile // GRAIN))
            unit = units * me + jnp.arange(units, dtype=jnp.int32)
            first_head = jnp.minimum(units * me // splits, heads - SLOTS)
            unit_places = jnp.concatenate([unit // splits - first_head, unit % splits])
            pick = (unit % splits)[:, None] == jnp.arange(splits, dtype=jnp.int32)[None, :]
            doc_q = jnp.sum(
                jnp.where(pick[None, :, :, None], docs.reshape(ctx, 1, splits, part), 0), axis=2
            ).reshape(ctx, 1, units * part)
            return (
                jnp.cos(angles), jnp.sin(angles), doc_slab, base, count,
                unit_places.astype(jnp.int32), doc_q,
            )

        sent = spread(first, w_qkv, gain_attn, gain_mlp, segment_ids, positions)
        sent = lax.all_to_all(sent, "ctx", 0, 0, tiled=True)
        masks = [0]
        if by_hand:
            own = [tokens[0]]
            near = [jnp.stack(
                [packed[:, :cut], jnp.pad(packed[:, cut:], ((0, 0), (0, 2 * cut - columns)))]
            )]
            own.append(lax.ppermute(own[0], "ctx", turn(1)))
            other = [lax.ppermute(own[0], "ctx", swap)]
            near.append(lax.ppermute(near[0], "ctx", turn(1)))
            own[1], other[0], near[1], sent = gate(own[1], other[0], near[1], sent)

        w_parts = sent[:, :shard, :].reshape(1, share, 4 * LANES)
        bit = fsdp // 2
        while bit:
            got = lax.ppermute(w_parts, "fsdp", flips(fsdp, bit))
            w_parts = jnp.concatenate([w_parts, got], axis=0)
            masks += [mask ^ bit for mask in masks]
            bit //= 2
        known = tables(sent)
        if by_hand:
            own.append(lax.ppermute(own[1], "ctx", turn(1)))
            other.append(lax.ppermute(own[1], "ctx", swap))
            near.append(lax.ppermute(near[1], "ctx", turn(1)))
            low_a = jnp.stack([near[0][0], near[1][0]])
            low_b = jnp.stack([near[0][1], near[1][1]])
            own[2], other[1], near[2], low_a, low_b, w_parts, known = gate(
                own[2], other[1], near[2], low_a, low_b, w_parts, known
            )
        cosine, sine, doc_slab, base, count, unit_places, doc_q = known

        w_heads, gains = ready(masks, mine.astype(jnp.int32).reshape(1), w_parts)

        def project_pair(step, held):
            at = jnp.stack([(me // 2 + outer - step) % outer, me % 2]).astype(jnp.int32)
            return project(
                at, own[step], other[step], w_heads, gains, cosine, sine, total, held
            )

        if by_hand:
            own.append(lax.ppermute(own[2], "ctx", turn(1)))
            other.append(lax.ppermute(own[2], "ctx", swap))
            near.append(lax.ppermute(near[2], "ctx", turn(1)))
            next_a = lax.ppermute(low_a, "ctx", swap)
            next_b = lax.ppermute(low_b, "fsdp", by_y)
            held = project_pair(1, project_pair(0, []))
            own[3], other[2], near[3], next_a, next_b, held = gate(
                own[3], other[2], near[3], next_a, next_b, held
            )

            other.append(lax.ppermute(own[3], "ctx", swap))
            high_a = jnp.stack([near[2][0], near[3][0]])
            high_b = jnp.stack([near[2][1], near[3][1]])
            past_a = lax.ppermute(high_a, "ctx", swap)
            past_b = lax.ppermute(high_b, "fsdp", by_y)
            ring_c = [w_qkv] + [lax.ppermute(w_qkv, "ctx", turn(back)) for back in range(1, outer)]
            held = project_pair(2, held)
            other[3], past_a, past_b, ring_c, held = gate(other[3], past_a, past_b, ring_c, held)

            pair_a = jnp.concatenate([weave(low_a, next_a), weave(high_a, past_a)])
            pair_b = jnp.concatenate([low_b, next_b, high_b, past_b])
            far_a = lax.ppermute(pair_a, "fsdp", by_y)
            far_b = lax.ppermute(pair_b, "ctx", swap)
            held = project_pair(3, held)
        else:
            blocks = lax.all_gather(tokens[0], "ctx", axis=0, tiled=True)
            blocks = blocks.reshape(outer, 2, rows, width)
            held = []
            for step in range(outer):
                at = jnp.asarray([step, 0], jnp.int32)
                held = project(
                    at, blocks[step, 0], blocks[step, 1], w_heads, gains, cosine, sine, total, held
                )
        hidden_one, qkv, turned = held
        att_low, att, lse = attend(
            base, count, unit_places, qkv, turned, doc_slab, doc_q, rows, tile
        )
        if by_hand:
            att_low, far_a, far_b = gate(att_low, far_a, far_b)
            pair_b = weave(pair_b, far_b)
            arrays = [pair_a, far_a, lax.ppermute(pair_a, "fsdp", by_core),
                      lax.ppermute(far_a, "fsdp", by_core),
                      pair_b, lax.ppermute(pair_b, "fsdp", by_core)]
            metas_a = [[(flip + 2 * far, back) for back in range(outer)]
                       for flip in range(2) for far in range(2)]
            metas_b = [[(flip + 2 * near, back) for near in (0, 1) for back in (0, 1)]
                       + [(flip + 2 * near, back) for near in (0, 1) for back in (2, 3)]
                       for flip in range(2)]
            att_in = lax.all_to_all(att_low, "ctx", 0, 0, tiled=True)
            pair_c = jnp.stack(ring_c)
            att_in, arrays, pair_c = gate(att_in, arrays, pair_c)
            near_c = lax.ppermute(pair_c, "ctx", swap)
        else:
            att_in = lax.all_to_all(att_low, "ctx", 0, 0, tiled=True)
            every = lax.all_gather(packed, AXES, axis=0, tiled=True)
            arrays = [every[None, :, :cut], every[None, :, cut:]]
            metas_a = metas_b = [[(0, 0)]]
            place = jnp.stack([0 * me, 0 * me, 0 * me + 1, 0 * me]).astype(jnp.int32)
            w_joined = lax.all_gather(w_qkv, AXES, axis=0, tiled=True)
        parts_a = list(zip(arrays, metas_a))
        parts_b = list(zip(arrays[len(metas_a) :], metas_b))

        output, grad_heads, grad_middle, attended, grad_branch, hidden_two, grad_up, product = (
            middle_stage(
                owners, first, place, att_in, tokens[0], gains, cot, parts_a, parts_b,
                w_down.shape[0],
            )
        )
        operands = [attended, grad_branch, hidden_two, grad_up, cot, product]
        grad_heads = lax.all_to_all(grad_heads, "ctx", 0, 0, tiled=True)
        if by_hand:
            rest = columns - cut
            gone_a, gone_b = weight_grads(
                gone_grads_kernel, sides, operands, [], [(2, share, cut), (2, share, rest)], cut,
                "gone_grads",
            )
            got_a = lax.ppermute(gone_a, "fsdp", by_core)
            got_b = lax.ppermute(gone_b, "fsdp", by_core)
            mine_a, other_a, mine_b, other_b = weight_grads(
                kept_grads_kernel, sides, operands, [got_a, got_b],
                [(1, share, cut)] * 2 + [(2 * outer, shard, rest)] * 2, cut, "kept_grads",
            )
            grad_heads, mine_a, other_a, mine_b, other_b, near_c = gate(
                grad_heads, mine_a, other_a, mine_b, other_b, near_c
            )
            got_a = lax.ppermute(other_a, "fsdp", by_y)
            got_b = lax.ppermute(other_b, "ctx", swap)
        else:
            grad_packed = jnp.concatenate(
                [dot_rows(left, right) for left, right in zip(operands[::2], operands[1::2])],
                axis=1,
            ).astype(bf16)
            grad_packed = lax.psum_scatter(grad_packed, "fsdp", scatter_dimension=0, tiled=True)
            grad_packed = lax.psum_scatter(grad_packed, "ctx", scatter_dimension=0, tiled=True)
            grad_packed = grad_packed.astype(f32)

        grad_joined = attend_back(
            base, count, unit_places, qkv, turned, doc_slab, doc_q, grad_heads, att, lse, cosine,
            sine, rows, tile,
        )
        if by_hand:
            grad_joined, mine_a, got_a, mine_b, got_b = gate(
                grad_joined, mine_a, got_a, mine_b, got_b
            )
            pair_c = weave(pair_c, near_c)
            far_c = lax.ppermute(pair_c, "fsdp", by_y)
            joined_in = lax.all_to_all(grad_joined, "ctx", 0, 0, tiled=True)
            by_x = lambda array: array.reshape(outer, 2, shard, array.shape[-1])
            mine_a, other_a, mine_b, other_b = add_halves(
                sides,
                [(by_x(mine_a), by_x(got_a), 1, 2),
                 (mine_b.reshape(2, share // 2, rest), got_b.reshape(2, share // 2, rest), 0, 1)],
            )
            sides_late, other_a, other_b = gate(sides, other_a, other_b)
            got_a = lax.ppermute(other_a, "ctx", swap)
            got_b = lax.ppermute(other_b, "fsdp", by_y)
            kept_cols, gone_cols = head_grads(fsdp, sides_late, hidden_one, grad_joined)
            mine_a, got_a, mine_b, got_b, kept_cols, gone_cols = gate(
                mine_a, got_a, mine_b, got_b, kept_cols, gone_cols
            )
            pairs = lambda array: array.reshape(outer // 2, 2, shard, array.shape[-1])
            kept, gone = add_halves(
                sides,
                [(pairs(mine_a), pairs(got_a), 1, 3), (pairs(mine_b), pairs(got_b), 1, 3)],
                joined=True,
            )
            got = lax.ppermute(gone, "ctx", flips(ctx, 2))
            got_cols = lax.ppermute(gone_cols, "fsdp", by_core)
            kept, got, kept_cols, got_cols, far_c = gate(kept, got, kept_cols, got_cols, far_c)
            kept, gone = add_halves(sides, [(kept, got, 0, 4)])
            got = lax.ppermute(gone, "ctx", flips(ctx, 4))
            kept_cols, gone_cols = add_halves(sides, [(kept_cols, got_cols, 0, 1)])
            got_cols = lax.ppermute(gone_cols, "fsdp", by_y)
            arrays = [pair_c, far_c, lax.ppermute(pair_c, "fsdp", by_core),
                      lax.ppermute(far_c, "fsdp", by_core)]
            w_joined = settle(place, list(zip(arrays, metas_a)), width)
            joined_in, kept, got, kept_cols, got_cols, w_joined = gate(
                joined_in, kept, got, kept_cols, got_cols, w_joined
            )
            grad_packed = kept[0].astype(f32) + got[0].astype(f32)
            grad_cols = (kept_cols[0].astype(f32) + got_cols[0].astype(f32)).astype(bf16)
        else:
            joined_in = lax.all_to_all(grad_joined, "ctx", 0, 0, tiled=True)
            grad_cols = dot_rows(hidden_one, grad_joined.reshape(total, 3 * LANES)).astype(bf16)
            grad_cols = lax.psum_scatter(grad_cols, "fsdp", scatter_dimension=0, tiled=True)
        input_grad = finish(owners, joined_in, tokens[0], gains, grad_middle, w_joined)
        grad_cols = grad_cols.reshape(ctx, shard, 3 * LANES)
        grad_cols = lax.all_to_all(grad_cols, "ctx", 0, 0, tiled=True).astype(f32)

        sum_w_out = grad_packed[:, :width]
        sum_w_in = grad_packed[:, width : width + w_in.shape[1]]
        sum_w_down = grad_packed[:, width + w_in.shape[1] :].T
        sum_gain_mlp = jnp.sum(w_in.astype(f32) * sum_w_in, axis=1) / gain_mlp.astype(f32)
        pieces = []
        for third in range(3):
            for head in range(heads):
                column = 0.0
                for c, slot in owners[head]:
                    at = third * LANES + slot * HD
                    column = column + grad_cols[c, :, at : at + HD]
                pieces.append(column)
        sum_w_qkv = jnp.concatenate(pieces, axis=1)
        sum_gain_attn = jnp.sum(w_qkv.astype(f32) * sum_w_qkv, axis=1) / gain_attn.astype(f32)
        return (
            output[None],
            input_grad[None],
            sum_gain_attn,
            sum_w_qkv,
            sum_w_out,
            sum_gain_mlp,
            sum_w_in,
            sum_w_down,
        )

    return on_device


def solution(mesh):
    rows = P(AXES, None)
    tokens = P("fsdp", "ctx", None)
    return jax.shard_map(
        program(mesh.shape["fsdp"], mesh.shape["ctx"]),
        mesh=mesh,
        in_specs=(
            tokens,
            P("fsdp", "ctx"),
            P("fsdp", "ctx"),
            P(AXES),
            rows,
            rows,
            P(AXES),
            rows,
            P(None, AXES),
            tokens,
        ),
        out_specs=(tokens, tokens, P(AXES), rows, rows, P(AXES), rows, P(None, AXES)),
        check_vma=False,
    )
```

```python
import functools
import math

import jax
import jax.numpy as jnp
from jax import lax
from jax.experimental import pallas as pl
from jax.experimental.pallas import tpu as pltpu
from jax.sharding import PartitionSpec as P

HD = 64
SLOTS = 2
LANES = SLOTS * HD
UNITS = 3
GRAIN = 128
KEY_TILE = 512
CHUNK = 384
EPS = 1e-05
THETA = 160000.0
NEG = -1e30
ROOT_HALF = 0.7071067811865476
INV_ROOT_TWO_PI = 0.3989422804014327
VMEM_BYTES = 58 * 1024 * 1024
AXES = ("fsdp", "ctx")

f32 = jnp.float32
bf16 = jnp.bfloat16


def norm_rows(values):
    center = values - jnp.mean(values, axis=-1, keepdims=True)
    spread = jnp.mean(center * center, axis=-1, keepdims=True)
    inverse = lax.rsqrt(spread + EPS)
    return (center * inverse, inverse)


def norm_back(grad_normed, normed, inverse):
    return inverse * (
        grad_normed
        - jnp.mean(grad_normed, axis=-1, keepdims=True)
        - normed * jnp.mean(grad_normed * normed, axis=-1, keepdims=True)
    )


def rotate_half(values):
    lane = lax.broadcasted_iota(jnp.int32, values.shape, 1)
    ahead = pltpu.roll(values, LANES - HD // 2, 1)
    behind = pltpu.roll(values, HD // 2, 1)
    return jnp.where(lane % HD < HD // 2, -ahead, behind)


def dot_tt(left, right):
    return lax.dot_general(left, right, (((1,), (1,)), ((), ())), preferred_element_type=f32)


def dot_rows(left, right):
    return lax.dot_general(left, right, (((0,), (0,)), ((), ())), preferred_element_type=f32)


def params():
    return pltpu.CompilerParams(
        dimension_semantics=("arbitrary",), vmem_limit_bytes=VMEM_BYTES
    )


def spread_kernel(first, *refs):
    sems, out_ref = refs[-1], refs[5]
    copies = [
        pltpu.make_async_copy(refs[i], refs[6 + i], sems.at[i]) for i in range(5)
    ]
    for copy in copies:
        copy.start()
    for copy in copies:
        copy.wait()
    w_ref, gain_one_ref, gain_two_ref, doc_ref, place_ref = refs[6:11]
    shard, columns = w_ref.shape
    width = columns // 3
    rows = doc_ref.shape[1]
    square = (shard, shard)
    eye = lax.broadcasted_iota(jnp.int32, square, 0) == lax.broadcasted_iota(jnp.int32, square, 1)

    def upright(ref):
        spread = jnp.where(eye, ref[...].astype(f32), 0.0)
        return jnp.sum(spread, axis=1, keepdims=True).astype(bf16)

    lane = lax.broadcasted_iota(jnp.int32, (shard, LANES), 1)
    gains = jnp.where(
        lane == 0, upright(gain_one_ref), jnp.where(lane == 1, upright(gain_two_ref), bf16(0))
    )
    place = place_ref[...]
    top = jnp.concatenate([doc_ref[...], place >> 6], axis=1).astype(f32)
    low = jnp.concatenate([place & 63, jnp.zeros_like(place)], axis=1).astype(f32)
    row = lax.broadcasted_iota(jnp.int32, (8, 2 * rows), 0)
    places = jnp.where(row == 0, top, jnp.where(row == 1, low, 0.0)).astype(bf16)
    for c, head in enumerate(first):
        for part in range(3):
            at = part * width + head * HD
            out_ref[c, :shard, part * LANES : (part + 1) * LANES] = w_ref[:, at : at + LANES]
        out_ref[c, :shard, 3 * LANES :] = gains
        out_ref[c, shard:, :] = places


def spread(first, w_qkv, gain_one, gain_two, docs, places):
    shard = w_qkv.shape[0]
    operands = (w_qkv, gain_one[None], gain_two[None], docs, places)
    return pl.pallas_call(
        functools.partial(spread_kernel, first),
        in_specs=[pl.BlockSpec(memory_space=pl.ANY)] * 5,
        out_specs=pl.BlockSpec(memory_space=pltpu.VMEM),
        out_shape=jax.ShapeDtypeStruct((len(first), shard + 8, 4 * LANES), bf16),
        scratch_shapes=[pltpu.VMEM(array.shape, array.dtype) for array in operands]
        + [pltpu.SemaphoreType.DMA((5,))],
        compiler_params=pltpu.CompilerParams(vmem_limit_bytes=VMEM_BYTES),
        name="spread",
    )(*operands)


def ready_kernel(masks, at_ref, w_ref, w_out_ref, gains_ref):
    share = w_ref.shape[1]
    for i, mask in enumerate(masks):
        start = pl.multiple_of((at_ref[0] ^ mask) * share, share)
        w_out_ref[pl.ds(start, share), :] = w_ref[i]
    gains_ref[...] = jnp.transpose(w_out_ref[:, 3 * LANES :].astype(f32))[:8]


def ready(masks, at, w_parts):
    count, share, columns = w_parts.shape
    vmem = pl.BlockSpec(memory_space=pltpu.VMEM)
    return pl.pallas_call(
        functools.partial(ready_kernel, masks),
        in_specs=[pl.BlockSpec(memory_space=pltpu.SMEM), vmem],
        out_specs=[vmem, vmem],
        out_shape=[
            jax.ShapeDtypeStruct((count * share, columns), bf16),
            jax.ShapeDtypeStruct((8, count * share), f32),
        ],
        compiler_params=pltpu.CompilerParams(vmem_limit_bytes=VMEM_BYTES),
        name="ready",
    )(at, w_parts)


def project_kernel(at_ref, own_ref, other_ref, w_ref, gains_ref, cos_ref, sin_ref, *refs):
    hidden_ref, qkv_ref, turned_ref = refs[-3:]
    own = pl.program_id(0) == 0
    x = jnp.where(own, own_ref[...], other_ref[...]).astype(f32)
    normed, _ = norm_rows(x)
    hidden = (normed * gains_ref[:1, :]).astype(bf16)
    hidden_ref[...] = hidden
    joined = jnp.dot(hidden, w_ref[...], preferred_element_type=f32)
    cosine = cos_ref[...]
    sine = sin_ref[...]
    query = joined[:, :LANES]
    keys = joined[:, LANES : 2 * LANES]
    values = joined[:, 2 * LANES :]
    query = (query * cosine + rotate_half(query) * sine).astype(bf16)
    keys = keys * cosine + rotate_half(keys) * sine
    qkv_ref[:, :LANES] = query * bf16(HD**-0.5)
    qkv_ref[:, LANES : 2 * LANES] = keys.astype(bf16)
    qkv_ref[:, 2 * LANES :] = values.astype(bf16)
    turned_ref[:LANES, :] = jnp.transpose(keys).astype(bf16)
    turned_ref[LANES:, :] = jnp.transpose(values).astype(bf16)


def project(at, own, other, w_heads, gains, cosine, sine, total, held):
    rows, width = own.shape
    fixed = lambda *shape: pl.BlockSpec(shape, lambda i, at: (0,) * len(shape))
    block = lambda i, at: at[0] * 2 + (at[1] ^ i)
    tall = lambda width: pl.BlockSpec((rows, width), lambda i, at: (block(i, at), 0))
    shapes = [
        jax.ShapeDtypeStruct((total, width), bf16),
        jax.ShapeDtypeStruct((total, 3 * LANES), bf16),
        jax.ShapeDtypeStruct((2 * LANES, total), bf16),
    ]
    return pl.pallas_call(
        project_kernel,
        grid_spec=pltpu.PrefetchScalarGridSpec(
            num_scalar_prefetch=1,
            grid=(2,),
            in_specs=[
                fixed(rows, width),
                fixed(rows, width),
                fixed(width, 3 * LANES),
                fixed(8, width),
                tall(LANES),
                tall(LANES),
            ]
            + [pl.BlockSpec(memory_space=pl.ANY) for _ in held],
            out_specs=[
                tall(width),
                tall(3 * LANES),
                pl.BlockSpec((2 * LANES, rows), lambda i, at: (0, block(i, at))),
            ],
        ),
        out_shape=shapes,
        input_output_aliases={7 + i: i for i in range(len(held))},
        compiler_params=params(),
        cost_estimate=pl.CostEstimate(
            flops=2 * 2 * rows * width * 3 * LANES, bytes_accessed=6 << 20, transcendentals=0
        ),
        name="project",
    )(at, own, other, w_heads, gains, cosine, sine, *held)


def gather_rows(units_ref, ref, units, part):
    lane = lax.broadcasted_iota(jnp.int32, (part, LANES), 1)
    chunks = []
    for i in range(units):
        start = pl.multiple_of(units_ref[units + i] * part, part)
        chunk = ref[pl.ds(start, part), :]
        chunks.append(jnp.where(lane // HD == units_ref[i], chunk, jnp.zeros_like(chunk)))
    return jnp.concatenate(chunks, axis=0)


def scatter_rows(units_ref, acc_ref, values, units, part):
    lane = lax.broadcasted_iota(jnp.int32, (part, LANES), 1)
    acc_ref[...] = jnp.zeros(acc_ref.shape, f32)
    for i in range(units):
        start = pl.multiple_of(units_ref[units + i] * part, part)
        chunk = values[i * part : (i + 1) * part]
        acc_ref[pl.ds(start, part), :] += jnp.where(lane // HD == units_ref[i], chunk, 0.0)


def pack_units(units_ref, acc_ref, part):
    half = part // 2

    def slab(unit, start, size, want):
        values = acc_ref[pl.ds(start, size), :]
        here = jnp.full(values.shape, units_ref[unit], jnp.int32) == want
        return jnp.where(here, values, pltpu.roll(values, HD, 1))

    def beside(left, right):
        left_side = lax.broadcasted_iota(jnp.int32, left.shape, 1) < HD
        return jnp.where(left_side, left, right)

    starts = [pl.multiple_of(units_ref[UNITS + unit] * part, part) for unit in range(UNITS)]
    top = beside(slab(0, starts[0], part, 0), slab(1, starts[1], part, 1))
    low = beside(slab(2, starts[2], half, 0), slab(2, starts[2] + half, half, 1))
    return jnp.concatenate([top, low], axis=0)


def unpack_units(units_ref, packed, part):
    half = part // 2
    values = packed.astype(f32)
    turned = pltpu.roll(values, HD, 1)
    side = lax.broadcasted_iota(jnp.int32, values.shape, 1) // HD

    def piece(unit, home, start, size):
        slot = jnp.full(values.shape, units_ref[unit], jnp.int32)
        chosen = jnp.where(slot == home, values, turned)
        return jnp.where(side == slot, chosen, 0.0)[start : start + size]

    return jnp.concatenate(
        [
            piece(0, 0, 0, part),
            piece(1, 1, 0, part),
            piece(2, 0, part, half),
            piece(2, 1, part, half),
        ],
        axis=0,
    ).astype(bf16)


def across(slab, wide):
    if wide <= LANES:
        return slab[:, :wide]
    return jnp.concatenate([slab] * (wide // LANES), axis=1)


def fold(values, reduce):
    rows, wide = values.shape
    return reduce(values.reshape(rows // 8, 8, wide), axis=0)


def tile_span(base_ref, block, at, tile):
    return pl.ds(pl.multiple_of(base_ref[block] * GRAIN + at * tile, GRAIN), tile)


def attend_kernel(units, tile, base_ref, count_ref, units_ref, q_ref, k_ref, vt_ref, doc_ref, doc_q_ref,
                  low_ref, att_ref, lse_ref, s_ref, acc_ref):
    block = pl.program_id(0)
    wide = s_ref.shape[1]
    part = wide // units
    queries = gather_rows(units_ref, q_ref, units, part)
    doc_q = doc_q_ref[0]

    def score(at, top):
        span = tile_span(base_ref, block, at, tile)
        scores = dot_tt(k_ref[span, :], queries)
        scores = jnp.where(across(doc_ref[span, :], wide) == doc_q, scores, NEG)
        s_ref[span, :] = scores
        return jnp.maximum(top, fold(scores, jnp.max))

    count = count_ref[block]
    top = lax.fori_loop(0, count, score, jnp.full((8, wide), NEG, f32))
    top = jnp.max(top, axis=0, keepdims=True)

    def weigh(at, carry):
        total, accum = carry
        span = tile_span(base_ref, block, at, tile)
        expo = jnp.exp(s_ref[span, :] - top)
        total = total + fold(expo, jnp.sum)
        accum = accum + jnp.dot(vt_ref[:, span], expo.astype(bf16), preferred_element_type=f32)
        return (total, accum)

    total, accum = lax.fori_loop(
        0, count, weigh, (jnp.zeros((8, wide), f32), jnp.zeros((LANES, wide), f32))
    )
    total = jnp.sum(total, axis=0, keepdims=True)
    att = accum / total
    att_ref[0] = att
    lse_ref[0] = top + jnp.log(total)
    scatter_rows(units_ref, acc_ref, jnp.transpose(att), units, part)
    low_ref[0] = pack_units(units_ref, acc_ref, part).astype(bf16)


def attend(base, tiles, unit_places, qkv, turned, doc_slab, doc_q, rows, tile):
    total = qkv.shape[0]
    count = total // rows
    units = unit_places.shape[0] // 2
    wide = doc_q.shape[2]
    return pl.pallas_call(
        functools.partial(attend_kernel, units, tile),
        grid_spec=pltpu.PrefetchScalarGridSpec(
            num_scalar_prefetch=3,
            grid=(count,),
            in_specs=[
                pl.BlockSpec((rows, LANES), lambda i, *s: (i, 0)),
                pl.BlockSpec((total, LANES), lambda i, *s: (0, 1)),
                pl.BlockSpec((LANES, total), lambda i, *s: (1, 0)),
                pl.BlockSpec((total, LANES), lambda i, *s: (0, 0)),
                pl.BlockSpec((1, 1, wide), lambda i, *s: (i, 0, 0)),
            ],
            out_specs=[
                pl.BlockSpec((1, wide // 2, LANES), lambda i, *s: (i, 0, 0)),
                pl.BlockSpec((1, LANES, wide), lambda i, *s: (i, 0, 0)),
                pl.BlockSpec((1, 1, wide), lambda i, *s: (i, 0, 0)),
            ],
            scratch_shapes=[pltpu.VMEM((total, wide), f32), pltpu.VMEM((rows, LANES), f32)],
        ),
        out_shape=[
            jax.ShapeDtypeStruct((count, wide // 2, LANES), bf16),
            jax.ShapeDtypeStruct((count, LANES, wide), f32),
            jax.ShapeDtypeStruct((count, 1, wide), f32),
        ],
        compiler_params=params(),
        cost_estimate=pl.CostEstimate(
            flops=4 * count * wide * total * LANES,
            bytes_accessed=8 << 20,
            transcendentals=count * wide * total,
        ),
        name="attend",
    )(base, tiles, unit_places, qkv, qkv, turned, doc_slab, doc_q)


def attend_back_kernel(units, tile, base_ref, count_ref, units_ref, q_ref, k_ref, v_ref, kt_ref, doc_ref,
                       doc_q_ref, grad_ref, att_ref, lse_ref, cos_ref, sin_ref,
                       out_ref, send_ref, dk_ref, dv_ref, acc_ref):
    block = pl.program_id(0)
    count = pl.num_programs(0)
    rows = acc_ref.shape[0]
    wide = att_ref.shape[2]
    part = wide // units

    @pl.when(block == 0)
    def _():
        dk_ref[...] = jnp.zeros(dk_ref.shape, f32)
        dv_ref[...] = jnp.zeros(dv_ref.shape, f32)

    def turn_back(values, span):
        return values * cos_ref[span, :] - rotate_half(values * sin_ref[span, :])

    queries = gather_rows(units_ref, q_ref, units, part)
    grads = unpack_units(units_ref, grad_ref[0], part)
    delta = jnp.sum(jnp.transpose(grads.astype(f32)) * att_ref[0], axis=0, keepdims=True)
    log_sum = lse_ref[0]
    doc_q = doc_q_ref[0]

    def step(at, grad_query):
        span = tile_span(base_ref, block, at, tile)
        scores = dot_tt(k_ref[span, :], queries)
        grad_probs = dot_tt(v_ref[span, :], grads)
        scores = jnp.where(across(doc_ref[span, :], wide) == doc_q, scores, NEG)
        probs = jnp.exp(scores - log_sum)
        dv_ref[span, :] += jnp.dot(probs.astype(bf16), grads, preferred_element_type=f32)
        grad_scores = (probs * (grad_probs - delta)).astype(bf16)
        dk_ref[span, :] += jnp.dot(grad_scores, queries, preferred_element_type=f32)
        return grad_query + jnp.dot(kt_ref[:, span], grad_scores, preferred_element_type=f32)

    grad_query = lax.fori_loop(
        0, count_ref[block], step, jnp.zeros((LANES, wide), f32)
    )
    scatter_rows(units_ref, acc_ref, jnp.transpose(grad_query) * HD**-0.5, units, part)
    here = pl.ds(pl.multiple_of(block * rows, rows), rows)
    turned = turn_back(acc_ref[...], here)
    out_ref[block, :, :LANES] = turned.astype(bf16)
    acc_ref[...] = turned
    send_ref[block, : wide // 2, :] = pack_units(units_ref, acc_ref, part).astype(bf16)

    @pl.when(block == count - 1)
    def _():
        def finish(at, carry):
            span = pl.ds(pl.multiple_of(at * rows, rows), rows)
            keys = turn_back(dk_ref[span, :], span).astype(bf16)
            values = dv_ref[span, :].astype(bf16)
            out_ref[at, :, LANES : 2 * LANES] = keys
            out_ref[at, :, 2 * LANES :] = values
            send_ref[at, wide // 2 : wide // 2 + rows, :] = keys
            send_ref[at, wide // 2 + rows :, :] = values
            return carry

        lax.fori_loop(0, count, finish, 0)


def attend_back(base, tiles, unit_places, qkv, turned, doc_slab, doc_q, grads, att, lse, cosine, sine,
                rows, tile):
    total = qkv.shape[0]
    count = total // rows
    units = unit_places.shape[0] // 2
    wide = doc_q.shape[2]
    whole = lambda part: pl.BlockSpec((total, LANES), lambda i, *s: (0, part))
    each = lambda *shape: pl.BlockSpec((1,) + shape, lambda i, *s: (i, 0, 0))
    return pl.pallas_call(
        functools.partial(attend_back_kernel, units, tile),
        grid_spec=pltpu.PrefetchScalarGridSpec(
            num_scalar_prefetch=3,
            grid=(count,),
            in_specs=[
                pl.BlockSpec((rows, LANES), lambda i, *s: (i, 0)),
                whole(1),
                whole(2),
                pl.BlockSpec((LANES, total), lambda i, *s: (0, 0)),
                whole(0),
                each(1, wide),
                each(wide // 2, LANES),
                each(LANES, wide),
                each(1, wide),
                whole(0),
                whole(0),
            ],
            out_specs=[
                pl.BlockSpec((count, rows, 3 * LANES), lambda i, *s: (0, 0, 0)),
                pl.BlockSpec((count, wide // 2 + 2 * rows, LANES), lambda i, *s: (0, 0, 0)),
            ],
            scratch_shapes=[
                pltpu.VMEM((total, LANES), f32),
                pltpu.VMEM((total, LANES), f32),
                pltpu.VMEM((rows, LANES), f32),
            ],
        ),
        out_shape=[
            jax.ShapeDtypeStruct((count, rows, 3 * LANES), bf16),
            jax.ShapeDtypeStruct((count, wide // 2 + 2 * rows, LANES), bf16),
        ],
        compiler_params=params(),
        cost_estimate=pl.CostEstimate(
            flops=10 * count * wide * total * LANES,
            bytes_accessed=12 << 20,
            transcendentals=count * wide * total,
        ),
        name="attend_back",
    )(base, tiles, unit_places, qkv, qkv, qkv, turned, doc_slab, doc_q, grads, att, lse, cosine, sine)


def lanes_of(slab, at, want):
    slab = slab.astype(f32)
    return slab if at == want else pltpu.roll(slab, HD, 1)


def beside(left, right):
    side = lax.broadcasted_iota(jnp.int32, left.shape, 1) // HD
    return jnp.where(side == 0, left, right).astype(bf16)


def join_packed(parts_ref, heads, splits, part):
    half = part // 2
    tiles = []
    for tile in range(heads // SLOTS):
        blocks = []
        for piece in range(splits):
            for low in range(2):
                sides = []
                for want in range(SLOTS):
                    c, unit = divmod((tile * SLOTS + want) * splits + piece, UNITS)
                    row, at = (low * half, unit) if unit < 2 else (part, low)
                    sides.append(lanes_of(parts_ref[c, row : row + half, :], at, want))
                blocks.append(beside(*sides))
        tiles.append(jnp.concatenate(blocks, axis=0))
    return jnp.concatenate(tiles, axis=1)


def split_packed(values, out_ref, splits, part):
    half = part // 2

    def slab(unit, low, want):
        head, piece = divmod(unit, splits)
        row = piece * part + low * half
        at = head // SLOTS * LANES
        return lanes_of(values[row : row + half, at : at + LANES], head % SLOTS, want)

    for c in range(out_ref.shape[0]):
        unit = UNITS * c
        for low in range(2):
            out_ref[c, low * half : (low + 1) * half, :] = beside(
                slab(unit, low, 0), slab(unit + 1, low, 1)
            )
        out_ref[c, part:, :] = beside(slab(unit + 2, 0, 0), slab(unit + 2, 1, 1))


def join_heads(parts_ref, at, rows, owners):
    side = lax.broadcasted_iota(jnp.int32, (rows, LANES), 1) // HD
    tiles = []
    for tile in range(len(owners) // SLOTS):
        column = jnp.zeros((rows, LANES), f32)
        for half in range(SLOTS):
            for c, slot in owners[tile * SLOTS + half]:
                slab = lanes_of(parts_ref[c, at : at + rows, :], slot, half)
                column = column + jnp.where(side == half, slab, 0.0)
        tiles.append(column.astype(bf16))
    return jnp.concatenate(tiles, axis=1)


def fetch_rows(place_ref, metas, refs, target_ref, at, sems, span=None):
    copies = []
    begin, end = span or (0, refs[0].shape[2])
    for ref, blocks in zip(refs, metas):
        for index, (flip, back) in enumerate(blocks):
            count = ref.shape[1]
            turn = lax.rem(place_ref[1] + place_ref[2] - back, place_ref[2])
            row = (place_ref[0] ^ flip) * place_ref[3] + turn * count
            row = pl.multiple_of(row, count) if count < target_ref.shape[0] else 0
            target = target_ref.at[pl.ds(row, count), pl.ds(at + begin, end - begin)]
            source = ref.at[index, :, pl.ds(begin, end - begin)]
            copies.append(pltpu.make_async_copy(source, target, sems.at[len(copies)]))
            copies[-1].start()
    return copies


def middle_kernel(heads, splits, metas, cut, place_ref, att_ref, tokens_ref, gain_ref, cot_ref,
                  *refs):
    count = len(metas[0]) + len(metas[1])
    sources = refs[:count]
    (output_ref, grad_heads_ref, grad_middle_ref, attended_ref, branch_ref, hidden_ref,
     grad_up_ref, product_ref, w_ref, sems_a, sems_b, sems_c) = refs[count:]
    width = tokens_ref.shape[1]
    units = product_ref.shape[1]
    fetch = functools.partial(fetch_rows, place_ref)
    copies_a = fetch(metas[0], sources[: len(metas[0])], w_ref, 0, sems_a, (0, width))
    copies_b = fetch(metas[0], sources[: len(metas[0])], w_ref, 0, sems_c, (width, cut))
    copies_b += fetch(metas[1], sources[len(metas[0]) :], w_ref, cut, sems_b)
    up = width
    down = width + 2 * units
    gain = gain_ref[1:2, :]
    cot = cot_ref[...]
    part = tokens_ref.shape[0] // splits
    attended = join_packed(att_ref, heads, splits, part)
    attended_ref[...] = attended
    for copy in copies_a:
        copy.wait()
    middle = tokens_ref[...].astype(f32) + jnp.dot(
        attended, w_ref[:, :width], preferred_element_type=f32
    )
    normed, inverse = norm_rows(middle)
    hidden = (normed * gain).astype(bf16)
    hidden_ref[...] = hidden
    for copy in copies_b:
        copy.wait()
    result = middle
    grad_hidden = jnp.zeros(middle.shape, f32)
    for at in range(0, units, CHUNK):
        one = slice(at, at + CHUNK)
        two = slice(units + at, units + at + CHUNK)
        w_one = w_ref[:, up + at : up + at + CHUNK]
        w_two = w_ref[:, up + units + at : up + units + at + CHUNK]
        w_down = w_ref[:, down + at : down + at + CHUNK]
        inner = jnp.dot(hidden, w_one, preferred_element_type=f32)
        gate = jnp.dot(hidden, w_two, preferred_element_type=f32)
        grad_product = jnp.dot(cot, w_down, preferred_element_type=f32)
        cdf = 0.5 * (1.0 + lax.erf(inner * ROOT_HALF))
        gelu_value = inner * cdf
        product = (gelu_value * gate).astype(bf16)
        product_ref[:, one] = product
        slope = cdf + inner * jnp.exp(-0.5 * inner * inner) * INV_ROOT_TWO_PI
        grad_inner = (grad_product * gate * slope).astype(bf16)
        grad_gate = (grad_product * gelu_value).astype(bf16)
        grad_up_ref[:, one] = grad_inner
        grad_up_ref[:, two] = grad_gate
        result = result + dot_tt(product, w_down)
        grad_hidden = grad_hidden + dot_tt(grad_inner, w_one)
        grad_hidden = grad_hidden + dot_tt(grad_gate, w_two)
    output_ref[...] = result.astype(bf16)
    grad_middle = cot.astype(f32) + norm_back(grad_hidden * gain, normed, inverse)
    grad_middle_ref[...] = grad_middle
    grad_branch = grad_middle.astype(bf16)
    branch_ref[...] = grad_branch
    grad_attended = dot_tt(grad_branch, w_ref[:, :width])
    split_packed(grad_attended, grad_heads_ref, splits, part)


def middle_stage(heads, splits, place, att_in, tokens, gains, cot, parts_a, parts_b, units):
    rows, width = tokens.shape
    arrays = [[array for array, _ in parts] for parts in (parts_a, parts_b)]
    metas = [[blocks for _, blocks in parts] for parts in (parts_a, parts_b)]
    vmem = pl.BlockSpec(memory_space=pltpu.VMEM)
    shape = jax.ShapeDtypeStruct
    return pl.pallas_call(
        functools.partial(middle_kernel, heads, splits, metas, arrays[0][0].shape[-1]),
        in_specs=[pl.BlockSpec(memory_space=pltpu.SMEM)]
        + [vmem] * 4
        + [pl.BlockSpec(memory_space=pl.ANY)] * (len(arrays[0]) + len(arrays[1])),
        out_specs=[vmem] * 8,
        out_shape=[
            shape((rows, width), bf16),
            shape(att_in.shape, bf16),
            shape((rows, width), f32),
            shape((rows, width), bf16),
            shape((rows, width), bf16),
            shape((rows, width), bf16),
            shape((rows, 2 * units), bf16),
            shape((rows, units), bf16),
        ],
        scratch_shapes=[pltpu.VMEM((width, 2 * arrays[0][0].shape[-1]), bf16)]
        + [
            pltpu.SemaphoreType.DMA((sum(len(b) for b in blocks),))
            for blocks in (metas[0], metas[1], metas[0])
        ],
        compiler_params=pltpu.CompilerParams(vmem_limit_bytes=VMEM_BYTES),
        cost_estimate=pl.CostEstimate(
            flops=6 * rows * width * (width + 3 * units),
            bytes_accessed=10 << 20,
            transcendentals=2 * rows * units,
        ),
        name="middle_stage",
    )(place, att_in, tokens, gains, cot, *arrays[0], *arrays[1])


def settle_kernel(metas, place_ref, *refs):
    out_ref, sems = refs[-2:]
    for copy in fetch_rows(place_ref, metas, refs[:-2], out_ref, 0, sems):
        copy.wait()


def settle(place, parts, width):
    arrays = [array for array, _ in parts]
    metas = [blocks for _, blocks in parts]
    anywhere = pl.BlockSpec(memory_space=pl.ANY)
    return pl.pallas_call(
        functools.partial(settle_kernel, metas),
        in_specs=[pl.BlockSpec(memory_space=pltpu.SMEM)] + [anywhere] * len(arrays),
        out_specs=pl.BlockSpec(memory_space=pltpu.VMEM),
        out_shape=jax.ShapeDtypeStruct((width, arrays[0].shape[-1]), bf16),
        scratch_shapes=[pltpu.SemaphoreType.DMA((sum(len(b) for b in metas),))],
        compiler_params=pltpu.CompilerParams(vmem_limit_bytes=VMEM_BYTES),
        cost_estimate=pl.CostEstimate(flops=0, bytes_accessed=8 << 20, transcendentals=0),
        name="settle",
    )(place, *arrays)


def finish_kernel(owners, splits, parts_ref, tokens_ref, gain_ref, grad_ref, w_ref, out_ref):
    rows = tokens_ref.shape[0]
    part = rows // splits
    packed = UNITS * part // 2
    joined = jnp.concatenate(
        [
            join_packed(parts_ref, len(owners), splits, part),
            join_heads(parts_ref, packed, rows, owners),
            join_heads(parts_ref, packed + rows, rows, owners),
        ],
        axis=1,
    )
    normed, inverse = norm_rows(tokens_ref[...].astype(f32))
    grad_hidden = dot_tt(joined, w_ref[...])
    back = norm_back(grad_hidden * gain_ref[:1, :], normed, inverse)
    out_ref[...] = (grad_ref[...] + back).astype(bf16)


def finish(owners, splits, joined, tokens, gains, grad_middle, w_joined):
    rows, width = tokens.shape
    vmem = pl.BlockSpec(memory_space=pltpu.VMEM)
    return pl.pallas_call(
        functools.partial(finish_kernel, owners, splits),
        in_specs=[vmem] * 5,
        out_specs=vmem,
        out_shape=jax.ShapeDtypeStruct((rows, width), bf16),
        compiler_params=pltpu.CompilerParams(vmem_limit_bytes=VMEM_BYTES),
        cost_estimate=pl.CostEstimate(
            flops=6 * rows * width * width, bytes_accessed=6 << 20, transcendentals=0
        ),
        name="finish",
    )(joined, tokens, gains, grad_middle, w_joined)


def half_rows(pairs, side, share, refs, lt_ref, emit):
    at = 0
    for pair in range(pairs):
        lt_ref[pair] = jnp.transpose(refs[2 * pair][...])
    for pair in range(pairs):
        right_ref = refs[2 * pair + 1]
        columns = right_ref.shape[1]
        for start in range(0, columns, CHUNK):
            right = right_ref[:, start : start + CHUNK]
            for half in range(lt_ref.shape[1] // share // 2):
                row = pl.multiple_of((2 * half + side) * share, share)
                emit(
                    half,
                    at + start,
                    jnp.dot(lt_ref[pair, pl.ds(row, share), :], right, preferred_element_type=f32),
                )
        at += columns


def pieces_of(cut, at, value):
    end = at + value.shape[1]
    found = []
    if at < cut:
        found.append((0, at, value[:, : min(end, cut) - at]))
    if end > cut:
        found.append((1, max(at, cut) - cut, value[:, max(at, cut) - at :]))
    return found


def gone_grads_kernel(pairs, cut, sides_ref, *refs):
    outs = refs[2 * pairs : 2 * pairs + 2]
    share = outs[0].shape[1]

    def emit(half, at, value):
        for which, start, piece in pieces_of(cut, at, value):
            span = slice(start, start + piece.shape[1])
            outs[which][half, :, span] = piece.astype(bf16)

    half_rows(pairs, 1 - sides_ref[0], share, refs, refs[-1], emit)


def kept_grads_kernel(pairs, cut, sides_ref, *refs):
    sources = refs[2 * pairs : 2 * pairs + 2]
    targets = refs[2 * pairs + 2 : 2 * pairs + 6]
    lt_ref, got_a, got_b, sum_a, sum_b, sems = refs[2 * pairs + 6 :]
    gots = (got_a, got_b)
    copies = [
        pltpu.make_async_copy(source, got, sems.at[i])
        for i, (source, got) in enumerate(zip(sources, gots))
    ]
    for copy in copies:
        copy.start()
    share = got_a.shape[1]
    shard = sum_b.shape[2]
    outer = share // shard // 2
    waits = list(copies)

    def emit(half, at, value):
        while waits:
            waits.pop().wait()
        for which, start, piece in pieces_of(cut, at, value):
            span = slice(start, start + piece.shape[1])
            total = piece + gots[which][half, :, span].astype(f32)
            if which == 0:
                sum_a[sides_ref[1] ^ half, :, span] = total.astype(bf16)
            else:
                for z in range(outer):
                    for x in range(2):
                        row = (z * 2 + x) * shard
                        block = total[row : row + shard].astype(bf16)
                        sum_b[sides_ref[2] ^ x, half * outer + z, :, span] = block

    half_rows(pairs, sides_ref[0], share, refs, lt_ref, emit)
    copies = []
    for i, total in enumerate((sum_a, sum_b)):
        for flip in range(2):
            copies.append(
                pltpu.make_async_copy(total.at[flip], targets[2 * i + flip], sems.at[2 * i + flip])
            )
            copies[-1].start()
    for copy in copies:
        copy.wait()


def weight_grads(kernel, sides, operands, gots, outs, cut, scratch, name):
    vmem = pl.BlockSpec(memory_space=pltpu.VMEM)
    outside = pl.BlockSpec(memory_space=pl.ANY)
    rows, width = operands[0].shape
    columns = sum(array.shape[1] for array in operands[1::2])
    return pl.pallas_call(
        functools.partial(kernel, len(operands) // 2, cut),
        in_specs=[pl.BlockSpec(memory_space=pltpu.SMEM)]
        + [vmem] * len(operands)
        + [outside] * len(gots),
        out_specs=[outside if gots else vmem] * len(outs),
        out_shape=[jax.ShapeDtypeStruct(shape, bf16) for shape in outs],
        scratch_shapes=[pltpu.VMEM((len(operands) // 2, width, rows), bf16)] + scratch,
        compiler_params=pltpu.CompilerParams(vmem_limit_bytes=VMEM_BYTES),
        cost_estimate=pl.CostEstimate(
            flops=rows * width * columns, bytes_accessed=3 * width * columns, transcendentals=0
        ),
        name=name,
    )(sides, *operands, *gots)


def head_grads_kernel(sides_ref, left_ref, right_ref, kept_ref, gone_ref, acc_ref):
    acc_ref[...] = jnp.zeros(acc_ref.shape, f32)
    count, rows, _ = right_ref.shape
    halves, share = kept_ref.shape[:2]

    def step(at, carry):
        span = pl.ds(pl.multiple_of(at * rows, rows), rows)
        left = jnp.transpose(left_ref[span, :])
        acc_ref[...] += jnp.dot(left, right_ref[at], preferred_element_type=f32)
        return carry

    lax.fori_loop(0, count, step, 0)
    for half in range(halves):
        for flip, ref in enumerate((kept_ref, gone_ref)):
            row = pl.multiple_of((2 * half + (sides_ref[0] ^ flip)) * share, share)
            ref[half] = acc_ref[pl.ds(row, share), :].astype(bf16)


def head_grads(fsdp, sides, hidden, grad_joined):
    total, width = hidden.shape
    columns = grad_joined.shape[2]
    vmem = pl.BlockSpec(memory_space=pltpu.VMEM)
    half = jax.ShapeDtypeStruct((fsdp // 2, width // fsdp, columns), bf16)
    return pl.pallas_call(
        head_grads_kernel,
        in_specs=[pl.BlockSpec(memory_space=pltpu.SMEM), vmem, vmem],
        out_specs=[vmem, vmem],
        out_shape=[half, half],
        scratch_shapes=[pltpu.VMEM((width, columns), f32)],
        compiler_params=pltpu.CompilerParams(vmem_limit_bytes=VMEM_BYTES),
        cost_estimate=pl.CostEstimate(
            flops=2 * total * width * columns,
            bytes_accessed=2 * total * (width + columns),
            transcendentals=0,
        ),
        name="head_grads",
    )(sides, hidden, grad_joined)


def add_halves_kernel(picks, joined, sides_ref, *refs):
    pairs = len(picks)
    outs = refs[2 * pairs :]
    begin = 0
    for i, pick in enumerate(picks):
        kept_ref, got_ref = refs[2 * i], refs[2 * i + 1]
        columns = kept_ref.shape[-1]
        for at in range(kept_ref.shape[0]):
            for flip in range(2):
                side = sides_ref[pick] ^ flip
                total = kept_ref[at, side].astype(f32) + got_ref[at, side].astype(f32)
                if joined:
                    outs[flip][at, :, begin : begin + columns] = total.astype(bf16)
                else:
                    outs[2 * i + flip][at] = total.astype(bf16)
        begin += columns


def add_halves(sides, pairs, joined=False):
    flat = []
    shapes = []
    for kept, got, axis, _ in pairs:
        shape = kept.shape
        shape = (
            math.prod(shape[:axis]), 2, math.prod(shape[axis + 1 : -1]), shape[-1]
        )
        flat += [kept.reshape(shape), got.reshape(shape)]
        shapes += [(shape[0], shape[2], shape[3])] * 2
    if joined:
        columns = sum(shape[2] for shape in shapes) // 2
        shapes = [shapes[0][:2] + (columns,)] * 2
    vmem = pl.BlockSpec(memory_space=pltpu.VMEM)
    size = sum(array.size for array in flat)
    return pl.pallas_call(
        functools.partial(add_halves_kernel, [pair[3] for pair in pairs], joined),
        in_specs=[pl.BlockSpec(memory_space=pltpu.SMEM)] + [vmem] * len(flat),
        out_specs=[vmem] * len(shapes),
        out_shape=[jax.ShapeDtypeStruct(shape, bf16) for shape in shapes],
        compiler_params=pltpu.CompilerParams(vmem_limit_bytes=VMEM_BYTES),
        cost_estimate=pl.CostEstimate(flops=size, bytes_accessed=3 * size, transcendentals=0),
        name="add_halves",
    )(sides, *flat)


def flips(count, bit):
    return [(i, i ^ bit) for i in range(count)]


def gate(*values):
    return lax.optimization_barrier(values)


def program(fsdp, ctx):
    def on_device(tokens, segment_ids, positions, gain_attn, w_qkv, w_out, gain_mlp, w_in, w_down,
                  cotangent):
        rows, width = tokens.shape[1:]
        shard = w_qkv.shape[0]
        share = ctx * shard
        heads = width // HD
        common = math.gcd(heads, ctx)
        splits = ctx // common
        units = heads // common
        part = rows // splits
        total = ctx * rows
        outer = ctx // 2
        first = [min(units * c // splits, heads - SLOTS) for c in range(ctx)]
        owners = [
            [
                (c, slot)
                for c in range(ctx)
                for slot in range(SLOTS)
                if first[c] + slot == head
                and max(units * c, head * splits) < min(units * (c + 1), (head + 1) * splits)
            ]
            for head in range(heads)
        ]
        me = lax.axis_index("ctx")
        mine = lax.axis_index("fsdp")
        sides = jnp.stack([mine % 2, mine // 2 % 2, me % 2, me // 2 % 2, me // 4 % 2])
        sides = sides.astype(jnp.int32)
        place = jnp.stack([mine, me // 2, 0 * me + outer, 0 * me + share]).astype(jnp.int32)
        swap = flips(ctx, 1)
        turn = lambda back: [
            (o * 2 + i, (o + back) % outer * 2 + i) for o in range(outer) for i in range(2)
        ]
        by_y = flips(fsdp, 2)
        by_core = flips(fsdp, 1)
        by_hand = (fsdp, ctx) == (4, 8) and shard % 8 == 0
        tile = KEY_TILE
        cot = cotangent[0]
        packed = jnp.concatenate([w_out, w_in, w_down.T], axis=1)
        columns = packed.shape[1]
        cut = (columns // LANES + 1) // 2 * LANES

        def weave(own, got):
            low = jnp.where(me % 2 == 0, own, got)
            high = jnp.where(me % 2 == 0, got, own)
            return jnp.concatenate([low, high], axis=1)

        def tables(sent):
            infos = sent[:, shard : shard + 2, :].astype(f32)
            docs = infos[:, 0, :rows].astype(jnp.int32)
            spots = (infos[:, 0, rows:] * 64 + infos[:, 1, :rows]).reshape(total, 1)
            half = jnp.arange(LANES) % (HD // 2)
            rates = THETA ** (-2.0 * half.astype(f32) / HD)
            angles = spots * rates[None, :]
            doc_slab = jnp.broadcast_to(docs.reshape(total, 1), (total, LANES))
            edges = docs.reshape(total // GRAIN, GRAIN)
            lo = jnp.sum((edges[None, :, -1] < docs[:, :1]).astype(jnp.int32), axis=1)
            hi = jnp.sum((edges[None, :, 0] <= docs[:, rows - 1 :]).astype(jnp.int32), axis=1)
            count = (hi - lo + tile // GRAIN - 1) // (tile // GRAIN)
            base = jnp.minimum(lo, total // GRAIN - count * (tile // GRAIN))
            unit = units * me + jnp.arange(units, dtype=jnp.int32)
            first_head = jnp.minimum(units * me // splits, heads - SLOTS)
            unit_places = jnp.concatenate([unit // splits - first_head, unit % splits])
            pick = (unit % splits)[:, None] == jnp.arange(splits, dtype=jnp.int32)[None, :]
            doc_q = jnp.sum(
                jnp.where(pick[None, :, :, None], docs.reshape(ctx, 1, splits, part), 0), axis=2
            ).reshape(ctx, 1, units * part)
            return (
                jnp.cos(angles), jnp.sin(angles), doc_slab, base, count,
                unit_places.astype(jnp.int32), doc_q,
            )

        sent = spread(first, w_qkv, gain_attn, gain_mlp, segment_ids, positions)
        sent = lax.all_to_all(sent, "ctx", 0, 0, tiled=True)
        masks = [0]
        if by_hand:
            own = [tokens[0]]
            near = [jnp.stack(
                [packed[:, :cut], jnp.pad(packed[:, cut:], ((0, 0), (0, 2 * cut - columns)))]
            )]
            own.append(lax.ppermute(own[0], "ctx", turn(1)))
            other = [lax.ppermute(own[0], "ctx", swap)]
            near.append(lax.ppermute(near[0], "ctx", turn(1)))
            own[1], other[0], near[1], sent = gate(own[1], other[0], near[1], sent)

        w_parts = sent[:, :shard, :].reshape(1, share, 4 * LANES)
        bit = fsdp // 2
        while bit:
            got = lax.ppermute(w_parts, "fsdp", flips(fsdp, bit))
            w_parts = jnp.concatenate([w_parts, got], axis=0)
            masks += [mask ^ bit for mask in masks]
            bit //= 2
        known = tables(sent)
        if by_hand:
            own.append(lax.ppermute(own[1], "ctx", turn(1)))
            other.append(lax.ppermute(own[1], "ctx", swap))
            near.append(lax.ppermute(near[1], "ctx", turn(1)))
            low_a = jnp.stack([near[0][0], near[1][0]])
            low_b = jnp.stack([near[0][1], near[1][1]])
            own[2], other[1], near[2], low_a, low_b, w_parts, known = gate(
                own[2], other[1], near[2], low_a, low_b, w_parts, known
            )
        cosine, sine, doc_slab, base, count, unit_places, doc_q = known

        w_heads, gains = ready(masks, mine.astype(jnp.int32).reshape(1), w_parts)

        def project_pair(step, held):
            at = jnp.stack([(me // 2 + outer - step) % outer, me % 2]).astype(jnp.int32)
            return project(
                at, own[step], other[step], w_heads, gains, cosine, sine, total, held
            )

        if by_hand:
            own.append(lax.ppermute(own[2], "ctx", turn(1)))
            other.append(lax.ppermute(own[2], "ctx", swap))
            near.append(lax.ppermute(near[2], "ctx", turn(1)))
            next_a = lax.ppermute(low_a, "ctx", swap)
            next_b = lax.ppermute(low_b, "fsdp", by_y)
            held = project_pair(1, project_pair(0, []))
            own[3], other[2], near[3], next_a, next_b, held, late = gate(
                own[3], other[2], near[3], next_a, next_b, held, w_qkv
            )

            other.append(lax.ppermute(own[3], "ctx", swap))
            high_a = jnp.stack([near[2][0], near[3][0]])
            high_b = jnp.stack([near[2][1], near[3][1]])
            past_a = lax.ppermute(high_a, "ctx", swap)
            past_b = lax.ppermute(high_b, "fsdp", by_y)
            held = project_pair(2, held)
            ring_c = [late, lax.ppermute(late, "ctx", turn(1))]
            other[3], past_a, past_b, held, ring_c = gate(other[3], past_a, past_b, held, ring_c)
            ring_c.append(lax.ppermute(ring_c[1], "ctx", turn(1)))

            pair_a = jnp.concatenate([weave(low_a, next_a), weave(high_a, past_a)])
            pair_b = jnp.concatenate([low_b, next_b, high_b, past_b])
            far_a = lax.ppermute(pair_a, "fsdp", by_y)
            far_b = lax.ppermute(pair_b, "ctx", swap)
            held = project_pair(3, held)
        else:
            blocks = lax.all_gather(tokens[0], "ctx", axis=0, tiled=True)
            blocks = blocks.reshape(outer, 2, rows, width)
            held = []
            for step in range(outer):
                at = jnp.asarray([step, 0], jnp.int32)
                held = project(
                    at, blocks[step, 0], blocks[step, 1], w_heads, gains, cosine, sine, total, held
                )
        hidden_one, qkv, turned = held
        att_low, att, lse = attend(
            base, count, unit_places, qkv, turned, doc_slab, doc_q, rows, tile
        )
        if by_hand:
            att_low, far_a, far_b, ring_c = gate(att_low, far_a, far_b, ring_c)
            pair_b = weave(pair_b, far_b)
            arrays = [pair_a, far_a, lax.ppermute(pair_a, "fsdp", by_core),
                      lax.ppermute(far_a, "fsdp", by_core),
                      pair_b, lax.ppermute(pair_b, "fsdp", by_core)]
            metas_a = [[(flip + 2 * far, back) for back in range(outer)]
                       for flip in range(2) for far in range(2)]
            metas_b = [[(flip + 2 * near, back) for near in (0, 1) for back in (0, 1)]
                       + [(flip + 2 * near, back) for near in (0, 1) for back in (2, 3)]
                       for flip in range(2)]
            att_in = lax.all_to_all(att_low, "ctx", 0, 0, tiled=True)
            ring_c.append(lax.ppermute(ring_c[2], "ctx", turn(1)))
            pair_c = jnp.stack(ring_c)
            att_in, arrays, pair_c = gate(att_in, arrays, pair_c)
            near_c = lax.ppermute(pair_c, "ctx", swap)
        else:
            att_in = lax.all_to_all(att_low, "ctx", 0, 0, tiled=True)
            every = lax.all_gather(packed, AXES, axis=0, tiled=True)
            arrays = [every[None, :, :cut], every[None, :, cut:]]
            metas_a = metas_b = [[(0, 0)]]
            place = jnp.stack([0 * me, 0 * me, 0 * me + 1, 0 * me]).astype(jnp.int32)
            w_joined = lax.all_gather(w_qkv, AXES, axis=0, tiled=True)
        parts_a = list(zip(arrays, metas_a))
        parts_b = list(zip(arrays[len(metas_a) :], metas_b))

        output, grad_heads, grad_middle, attended, grad_branch, hidden_two, grad_up, product = (
            middle_stage(
                heads, splits, place, att_in, tokens[0], gains, cot, parts_a, parts_b,
                w_down.shape[0],
            )
        )
        operands = [attended, grad_branch, hidden_two, grad_up, cot, product]
        if by_hand:
            grad_heads, operands, near_c = gate(grad_heads, operands, near_c)
            pair_c = weave(pair_c, near_c)
            far_c = lax.ppermute(pair_c, "fsdp", by_y)
        grad_heads = lax.all_to_all(grad_heads, "ctx", 0, 0, tiled=True)
        if by_hand:
            rest = columns - cut
            gone_a, gone_b = weight_grads(
                gone_grads_kernel, sides, operands, [], [(2, share, cut), (2, share, rest)], cut,
                [], "gone_grads",
            )
            got_a = lax.ppermute(gone_a, "fsdp", by_core)
            got_b = lax.ppermute(gone_b, "fsdp", by_core)
            mine_a, other_a, mine_b, other_b = weight_grads(
                kept_grads_kernel, sides, operands, [got_a, got_b],
                [(share, cut)] * 2 + [(2 * outer, shard, rest)] * 2, cut,
                [
                    pltpu.VMEM((2, share, cut), bf16),
                    pltpu.VMEM((2, share, rest), bf16),
                    pltpu.VMEM((2, share, cut), bf16),
                    pltpu.VMEM((2, 2 * outer, shard, rest), bf16),
                    pltpu.SemaphoreType.DMA((4,)),
                ],
                "kept_grads",
            )
            grad_heads, mine_a, other_a, mine_b, other_b = gate(
                grad_heads, mine_a, other_a, mine_b, other_b
            )
            got_a = lax.ppermute(other_a, "fsdp", by_y)
            got_b = lax.ppermute(other_b, "ctx", swap)
        else:
            grad_packed = jnp.concatenate(
                [dot_rows(left, right) for left, right in zip(operands[::2], operands[1::2])],
                axis=1,
            ).astype(bf16)
            grad_packed = lax.psum_scatter(grad_packed, "fsdp", scatter_dimension=0, tiled=True)
            grad_packed = lax.psum_scatter(grad_packed, "ctx", scatter_dimension=0, tiled=True)
            grad_packed = grad_packed.astype(f32)

        grad_joined, grad_sent = attend_back(
            base, count, unit_places, qkv, turned, doc_slab, doc_q, grad_heads, att, lse, cosine,
            sine, rows, tile,
        )
        if by_hand:
            grad_joined, grad_sent, mine_a, got_a, mine_b, got_b, pair_c, far_c = gate(
                grad_joined, grad_sent, mine_a, got_a, mine_b, got_b, pair_c, far_c
            )
            joined_in = lax.all_to_all(grad_sent, "ctx", 0, 0, tiled=True)
            arrays = [pair_c, far_c, lax.ppermute(pair_c, "fsdp", by_core),
                      lax.ppermute(far_c, "fsdp", by_core)]
            by_x = lambda array: array.reshape(outer, 2, shard, array.shape[-1])
            mine_a, other_a, mine_b, other_b = add_halves(
                sides,
                [(by_x(mine_a), by_x(got_a), 1, 2),
                 (mine_b.reshape(2, share // 2, rest), got_b.reshape(2, share // 2, rest), 0, 1)],
            )
            sides_late, other_a, other_b = gate(sides, other_a, other_b)
            got_a = lax.ppermute(other_a, "ctx", swap)
            got_b = lax.ppermute(other_b, "fsdp", by_y)
            kept_cols, gone_cols = head_grads(fsdp, sides_late, hidden_one, grad_joined)
            got_cols = lax.ppermute(gone_cols, "fsdp", by_core)
            mine_a, got_a, mine_b, got_b, kept_cols, got_cols, arrays = gate(
                mine_a, got_a, mine_b, got_b, kept_cols, got_cols, arrays
            )
            w_joined = settle(place, list(zip(arrays, metas_a)), width)
            pairs = lambda array: array.reshape(outer // 2, 2, shard, array.shape[-1])
            kept, gone = add_halves(
                sides,
                [(pairs(mine_a), pairs(got_a), 1, 3), (pairs(mine_b), pairs(got_b), 1, 3)],
                joined=True,
            )
            got = lax.ppermute(gone, "ctx", flips(ctx, 2))
            kept_cols, gone_cols = add_halves(sides, [(kept_cols, got_cols, 0, 1)])
            got_cols = lax.ppermute(gone_cols, "fsdp", by_y)
            joined_in, kept, got, kept_cols, got_cols, w_joined = gate(
                joined_in, kept, got, kept_cols, got_cols, w_joined
            )
            kept, gone = add_halves(sides, [(kept, got, 0, 4)])
            got = lax.ppermute(gone, "ctx", flips(ctx, 4))
            grad_packed = kept[0].astype(f32) + got[0].astype(f32)
            grad_cols = (kept_cols[0].astype(f32) + got_cols[0].astype(f32)).astype(bf16)
            grad_cols, _ = gate(grad_cols, gone)
        else:
            joined_in = lax.all_to_all(grad_sent, "ctx", 0, 0, tiled=True)
            grad_cols = dot_rows(hidden_one, grad_joined.reshape(total, 3 * LANES)).astype(bf16)
            grad_cols = lax.psum_scatter(grad_cols, "fsdp", scatter_dimension=0, tiled=True)
        input_grad = finish(owners, splits, joined_in, tokens[0], gains, grad_middle, w_joined)
        grad_cols = grad_cols.reshape(ctx, shard, 3 * LANES)
        grad_cols = lax.all_to_all(grad_cols, "ctx", 0, 0, tiled=True).astype(f32)

        sum_w_out = grad_packed[:, :width]
        sum_w_in = grad_packed[:, width : width + w_in.shape[1]]
        sum_w_down = grad_packed[:, width + w_in.shape[1] :].T
        sum_gain_mlp = jnp.sum(w_in.astype(f32) * sum_w_in, axis=1) / gain_mlp.astype(f32)
        pieces = []
        for third in range(3):
            for head in range(heads):
                column = 0.0
                for c, slot in owners[head]:
                    at = third * LANES + slot * HD
                    column = column + grad_cols[c, :, at : at + HD]
                pieces.append(column)
        sum_w_qkv = jnp.concatenate(pieces, axis=1)
        sum_gain_attn = jnp.sum(w_qkv.astype(f32) * sum_w_qkv, axis=1) / gain_attn.astype(f32)
        return (
            output[None],
            input_grad[None],
            sum_gain_attn,
            sum_w_qkv,
            sum_w_out,
            sum_gain_mlp,
            sum_w_in,
            sum_w_down,
        )

    return on_device


def solution(mesh):
    rows = P(AXES, None)
    tokens = P("fsdp", "ctx", None)
    return jax.shard_map(
        program(mesh.shape["fsdp"], mesh.shape["ctx"]),
        mesh=mesh,
        in_specs=(
            tokens,
            P("fsdp", "ctx"),
            P("fsdp", "ctx"),
            P(AXES),
            rows,
            rows,
            P(AXES),
            rows,
            P(None, AXES),
            tokens,
        ),
        out_specs=(tokens, tokens, P(AXES), rows, rows, P(AXES), rows, P(None, AXES)),
        check_vma=False,
    )
```

```python
import functools
import math

import jax
import jax.numpy as jnp
from jax import lax
from jax.experimental import pallas as pl
from jax.experimental.pallas import tpu as pltpu
from jax.sharding import PartitionSpec as P

HD = 64
SLOTS = 2
LANES = SLOTS * HD
UNITS = 3
IDS = 16
GRAIN = 128
KEY_TILE = 512
CHUNK = 384
EPS = 1e-05
THETA = 160000.0
NEG = -1e30
ROOT_HALF = 0.7071067811865476
INV_ROOT_TWO_PI = 0.3989422804014327
VMEM_BYTES = 58 * 1024 * 1024
AXES = ("fsdp", "ctx")

f32 = jnp.float32
bf16 = jnp.bfloat16


def norm_rows(values):
    center = values - jnp.mean(values, axis=-1, keepdims=True)
    spread = jnp.mean(center * center, axis=-1, keepdims=True)
    inverse = lax.rsqrt(spread + EPS)
    return (center * inverse, inverse)


def norm_back(grad_normed, normed, inverse):
    return inverse * (
        grad_normed
        - jnp.mean(grad_normed, axis=-1, keepdims=True)
        - normed * jnp.mean(grad_normed * normed, axis=-1, keepdims=True)
    )


def rotate_half(values):
    lane = lax.broadcasted_iota(jnp.int32, values.shape, 1)
    ahead = pltpu.roll(values, LANES - HD // 2, 1)
    behind = pltpu.roll(values, HD // 2, 1)
    return jnp.where(lane % HD < HD // 2, -ahead, behind)


def dot_tt(left, right):
    return lax.dot_general(left, right, (((1,), (1,)), ((), ())), preferred_element_type=f32)


def dot_rows(left, right):
    return lax.dot_general(left, right, (((0,), (0,)), ((), ())), preferred_element_type=f32)


def params():
    return pltpu.CompilerParams(
        dimension_semantics=("arbitrary",), vmem_limit_bytes=VMEM_BYTES
    )


def spread_kernel(first, *refs):
    sems, out_ref = refs[-1], refs[5]
    copies = [
        pltpu.make_async_copy(refs[i], refs[6 + i], sems.at[i]) for i in range(5)
    ]
    for copy in copies:
        copy.start()
    for copy in copies:
        copy.wait()
    w_ref, gain_one_ref, gain_two_ref, doc_ref, place_ref = refs[6:11]
    shard, columns = w_ref.shape
    width = columns // 3
    rows = doc_ref.shape[1]
    square = (shard, shard)
    eye = lax.broadcasted_iota(jnp.int32, square, 0) == lax.broadcasted_iota(jnp.int32, square, 1)

    def upright(ref):
        spread = jnp.where(eye, ref[...].astype(f32), 0.0)
        return jnp.sum(spread, axis=1, keepdims=True).astype(bf16)

    lane = lax.broadcasted_iota(jnp.int32, (shard, LANES), 1)
    gains = jnp.where(
        lane == 0, upright(gain_one_ref), jnp.where(lane == 1, upright(gain_two_ref), bf16(0))
    )
    place = place_ref[...]
    top = jnp.concatenate([doc_ref[...], place >> 6], axis=1).astype(f32)
    low = jnp.concatenate([place & 63, jnp.zeros_like(place)], axis=1).astype(f32)
    row = lax.broadcasted_iota(jnp.int32, (8, 2 * rows), 0)
    places = jnp.where(row == 0, top, jnp.where(row == 1, low, 0.0)).astype(bf16)
    for c, head in enumerate(first):
        for part in range(3):
            at = part * width + head * HD
            out_ref[c, :shard, part * LANES : (part + 1) * LANES] = w_ref[:, at : at + LANES]
        out_ref[c, :shard, 3 * LANES :] = gains
        out_ref[c, shard:, :] = places


def spread(first, w_qkv, gain_one, gain_two, docs, places):
    shard = w_qkv.shape[0]
    operands = (w_qkv, gain_one[None], gain_two[None], docs, places)
    return pl.pallas_call(
        functools.partial(spread_kernel, first),
        in_specs=[pl.BlockSpec(memory_space=pl.ANY)] * 5,
        out_specs=pl.BlockSpec(memory_space=pltpu.VMEM),
        out_shape=jax.ShapeDtypeStruct((len(first), shard + 8, 4 * LANES), bf16),
        scratch_shapes=[pltpu.VMEM(array.shape, array.dtype) for array in operands]
        + [pltpu.SemaphoreType.DMA((5,))],
        compiler_params=pltpu.CompilerParams(vmem_limit_bytes=VMEM_BYTES),
        name="spread",
    )(*operands)


def ready_kernel(masks, at_ref, w_ref, w_out_ref, gains_ref):
    share = w_ref.shape[1]
    for i, mask in enumerate(masks):
        start = pl.multiple_of((at_ref[0] ^ mask) * share, share)
        w_out_ref[pl.ds(start, share), :] = w_ref[i]
    gains_ref[...] = jnp.transpose(w_out_ref[:, 3 * LANES :].astype(f32))[:8]


def ready(masks, at, w_parts):
    count, share, columns = w_parts.shape
    vmem = pl.BlockSpec(memory_space=pltpu.VMEM)
    return pl.pallas_call(
        functools.partial(ready_kernel, masks),
        in_specs=[pl.BlockSpec(memory_space=pltpu.SMEM), vmem],
        out_specs=[vmem, vmem],
        out_shape=[
            jax.ShapeDtypeStruct((count * share, columns), bf16),
            jax.ShapeDtypeStruct((8, count * share), f32),
        ],
        compiler_params=pltpu.CompilerParams(vmem_limit_bytes=VMEM_BYTES),
        name="ready",
    )(at, w_parts)


def project_kernel(count, at_ref, *refs):
    x_refs = refs[:count]
    w_ref, gains_ref, cos_ref, sin_ref = refs[count : count + 4]
    hidden_ref, qkv_ref, turned_ref = refs[-3:]
    x = x_refs[0][...]
    for i in range(1, count):
        x = jnp.where(pl.program_id(0) == i, x_refs[i][...], x)
    x = x.astype(f32)
    normed, _ = norm_rows(x)
    hidden = (normed * gains_ref[:1, :]).astype(bf16)
    hidden_ref[...] = hidden
    joined = jnp.dot(hidden, w_ref[...], preferred_element_type=f32)
    cosine = cos_ref[...]
    sine = sin_ref[...]
    query = joined[:, :LANES]
    keys = joined[:, LANES : 2 * LANES]
    values = joined[:, 2 * LANES :]
    query = (query * cosine + rotate_half(query) * sine).astype(bf16)
    keys = keys * cosine + rotate_half(keys) * sine
    qkv_ref[:, :LANES] = query * bf16(HD**-0.5)
    qkv_ref[:, LANES : 2 * LANES] = keys.astype(bf16)
    qkv_ref[:, 2 * LANES :] = values.astype(bf16)
    turned_ref[:LANES, :] = jnp.transpose(keys).astype(bf16)
    turned_ref[LANES:, :] = jnp.transpose(values).astype(bf16)


def project(at, blocks, w_heads, gains, cosine, sine, total, held):
    rows, width = blocks[0].shape
    count = len(blocks)
    fixed = lambda *shape: pl.BlockSpec(shape, lambda i, at: (0,) * len(shape))
    tall = lambda width: pl.BlockSpec((rows, width), lambda i, at: (at[i], 0))
    shapes = [
        jax.ShapeDtypeStruct((total, width), bf16),
        jax.ShapeDtypeStruct((total, 3 * LANES), bf16),
        jax.ShapeDtypeStruct((2 * LANES, total), bf16),
    ]
    return pl.pallas_call(
        functools.partial(project_kernel, count),
        grid_spec=pltpu.PrefetchScalarGridSpec(
            num_scalar_prefetch=1,
            grid=(count,),
            in_specs=[fixed(rows, width)] * count
            + [fixed(width, 3 * LANES), fixed(8, width), tall(LANES), tall(LANES)]
            + [pl.BlockSpec(memory_space=pl.ANY) for _ in held],
            out_specs=[
                tall(width),
                tall(3 * LANES),
                pl.BlockSpec((2 * LANES, rows), lambda i, at: (0, at[i])),
            ],
        ),
        out_shape=shapes,
        input_output_aliases={count + 5 + i: i for i in range(len(held))},
        compiler_params=params(),
        cost_estimate=pl.CostEstimate(
            flops=2 * count * rows * width * 3 * LANES,
            bytes_accessed=3 * count << 20,
            transcendentals=0,
        ),
        name="project",
    )(at, *blocks, w_heads, gains, cosine, sine, *held)


def gather_rows(units_ref, ref, part):
    lane = lax.broadcasted_iota(jnp.int32, (part, LANES), 1)
    chunks = []
    for unit in range(UNITS):
        start = pl.multiple_of(units_ref[UNITS + unit] * part, part)
        chunk = ref[pl.ds(start, part), :]
        chunks.append(jnp.where(lane // HD == units_ref[unit], chunk, jnp.zeros_like(chunk)))
    return jnp.concatenate(chunks, axis=0)


def slot_rows(units_ref, unit):
    return pl.ds(pl.multiple_of(units_ref[unit] * HD, HD), HD)


def pack(pieces):
    half = pieces[2].shape[1] // 2
    top = jnp.concatenate(pieces[:2], axis=0)
    low = jnp.concatenate([pieces[2][:, :half], pieces[2][:, half:]], axis=0)
    return jnp.concatenate([jnp.transpose(top), jnp.transpose(low)], axis=0).astype(bf16)


def unpack(packed, part):
    values = packed.astype(f32)
    top = jnp.transpose(values[:part])
    low = jnp.transpose(values[part:])
    return [top[:HD], top[HD:], jnp.concatenate([low[:HD], low[HD:]], axis=1)]


def fold(values, reduce):
    rows, wide = values.shape
    return reduce(values.reshape(rows // 8, 8, wide), axis=0)


def tile_span(base_ref, block, at, tile):
    return pl.ds(pl.multiple_of(base_ref[block] * GRAIN + at * tile, GRAIN), tile)


def masked(scores, base_ref, block, at, tile, range_ref):
    key = lax.broadcasted_iota(jnp.int32, scores.shape, 0) + (base_ref[block] * GRAIN + at * tile)
    same = (key >= range_ref[0, :1, :]) & (key < range_ref[0, 1:2, :])
    return jnp.where(same, scores, NEG)


def attend_kernel(tile, base_ref, count_ref, units_ref, q_ref, k_ref, vt_ref, range_ref,
                  low_ref, att_ref, lse_ref, s_ref, acc_ref):
    block = pl.program_id(0)
    wide = s_ref.shape[1]
    part = wide // UNITS
    queries = gather_rows(units_ref, q_ref, part)

    def score(at, top):
        span = tile_span(base_ref, block, at, tile)
        scores = masked(dot_tt(k_ref[span, :], queries), base_ref, block, at, tile, range_ref)
        s_ref[span, :] = scores
        return jnp.maximum(top, fold(scores, jnp.max))

    count = count_ref[block]
    top = lax.fori_loop(0, count, score, jnp.full((8, wide), NEG, f32))
    top = jnp.max(top, axis=0, keepdims=True)

    def weigh(at, carry):
        total, accum = carry
        span = tile_span(base_ref, block, at, tile)
        expo = jnp.exp(s_ref[span, :] - top)
        total = total + fold(expo, jnp.sum)
        accum = accum + jnp.dot(vt_ref[:, span], expo.astype(bf16), preferred_element_type=f32)
        return (total, accum)

    total, accum = lax.fori_loop(
        0, count, weigh, (jnp.zeros((8, wide), f32), jnp.zeros((LANES, wide), f32))
    )
    total = jnp.sum(total, axis=0, keepdims=True)
    lse_ref[0] = top + jnp.log(total)
    acc_ref[...] = accum / total
    pieces = [
        acc_ref[slot_rows(units_ref, unit), unit * part : (unit + 1) * part]
        for unit in range(UNITS)
    ]
    att_ref[0] = jnp.concatenate(pieces, axis=1)
    low_ref[0] = pack(pieces)


def attend(base, tiles, unit_places, qkv, turned, ranges, rows, tile):
    total = qkv.shape[0]
    count = total // rows
    wide = ranges.shape[2]
    each = lambda *shape: pl.BlockSpec((1,) + shape, lambda i, *s: (i, 0, 0))
    return pl.pallas_call(
        functools.partial(attend_kernel, tile),
        grid_spec=pltpu.PrefetchScalarGridSpec(
            num_scalar_prefetch=3,
            grid=(count,),
            in_specs=[
                pl.BlockSpec((rows, LANES), lambda i, *s: (i, 0)),
                pl.BlockSpec((total, LANES), lambda i, *s: (0, 1)),
                pl.BlockSpec((LANES, total), lambda i, *s: (1, 0)),
                each(2, wide),
            ],
            out_specs=[each(wide // 2, LANES), each(HD, wide), each(1, wide)],
            scratch_shapes=[pltpu.VMEM((total, wide), f32), pltpu.VMEM((LANES, wide), f32)],
        ),
        out_shape=[
            jax.ShapeDtypeStruct((count, wide // 2, LANES), bf16),
            jax.ShapeDtypeStruct((count, HD, wide), f32),
            jax.ShapeDtypeStruct((count, 1, wide), f32),
        ],
        compiler_params=params(),
        cost_estimate=pl.CostEstimate(
            flops=4 * count * wide * total * LANES,
            bytes_accessed=8 << 20,
            transcendentals=count * wide * total,
        ),
        name="attend",
    )(base, tiles, unit_places, qkv, qkv, turned, ranges)


def attend_back_kernel(tile, base_ref, count_ref, units_ref, q_ref, k_ref, v_ref, kt_ref, range_ref,
                       grad_ref, att_ref, lse_ref, cos_q_ref, sin_q_ref, cos_hbm, sin_hbm,
                       out_ref, send_ref, dk_ref, dv_ref, acc_ref, gt_ref, full_ref, cos_ref,
                       sin_ref, sems):
    block = pl.program_id(0)
    count = pl.num_programs(0)
    rows = full_ref.shape[1]
    wide = acc_ref.shape[1]
    part = wide // UNITS
    tables = [
        pltpu.make_async_copy(cos_hbm, cos_ref, sems.at[0]),
        pltpu.make_async_copy(sin_hbm, sin_ref, sems.at[1]),
    ]

    @pl.when(block == 0)
    def _():
        for table in tables:
            table.start()
        dk_ref[...] = jnp.zeros(dk_ref.shape, f32)
        dv_ref[...] = jnp.zeros(dv_ref.shape, f32)
        gt_ref[...] = jnp.zeros(gt_ref.shape, bf16)
        full_ref[...] = jnp.zeros(full_ref.shape, f32)

    queries = gather_rows(units_ref, q_ref, part)
    grads = unpack(grad_ref[0], part)
    delta = jnp.sum(jnp.concatenate(grads, axis=1) * att_ref[0], axis=0, keepdims=True)
    for unit, piece in enumerate(grads):
        columns = slice(unit * part, (unit + 1) * part)
        gt_ref[slot_rows(units_ref, unit), columns] = piece.astype(bf16)
    log_sum = lse_ref[0]

    def step(at, grad_query):
        span = tile_span(base_ref, block, at, tile)
        grads_t = gt_ref[...]
        scores = masked(dot_tt(k_ref[span, :], queries), base_ref, block, at, tile, range_ref)
        grad_probs = jnp.dot(v_ref[span, :], grads_t, preferred_element_type=f32)
        probs = jnp.exp(scores - log_sum)
        dv_ref[span, :] += dot_tt(probs.astype(bf16), grads_t)
        grad_scores = (probs * (grad_probs - delta)).astype(bf16)
        dk_ref[span, :] += jnp.dot(grad_scores, queries, preferred_element_type=f32)
        return grad_query + jnp.dot(kt_ref[:, span], grad_scores, preferred_element_type=f32)

    acc_ref[...] = lax.fori_loop(0, count_ref[block], step, jnp.zeros((LANES, wide), f32))
    pieces = []
    for unit in range(UNITS):
        columns = slice(unit * part, (unit + 1) * part)
        piece = acc_ref[slot_rows(units_ref, unit), columns] * HD**-0.5
        turned = piece * sin_q_ref[0, :, columns]
        turned = jnp.concatenate([-turned[HD // 2 :], turned[: HD // 2]], axis=0)
        pieces.append(piece * cos_q_ref[0, :, columns] - turned)
    send_ref[block, : wide // 2, :] = pack(pieces)
    place_units(units_ref, full_ref, pieces, part)
    out_ref[block, :, :LANES] = jnp.transpose(full_ref[...]).astype(bf16)

    @pl.when(block == count - 1)
    def _():
        for table in tables:
            table.wait()

        def finish(at, carry):
            span = pl.ds(pl.multiple_of(at * rows, rows), rows)
            keys = dk_ref[span, :]
            keys = keys * cos_ref[span, :] - rotate_half(keys * sin_ref[span, :])
            keys = keys.astype(bf16)
            values = dv_ref[span, :].astype(bf16)
            out_ref[at, :, LANES : 2 * LANES] = keys
            out_ref[at, :, 2 * LANES :] = values
            send_ref[at, wide // 2 : wide // 2 + rows, :] = keys
            send_ref[at, wide // 2 + rows :, :] = values
            return carry

        lax.fori_loop(0, count, finish, 0)


def place_units(units_ref, full_ref, pieces, part):
    rows = full_ref.shape[1]
    for split in range(rows // part):
        for unit, piece in enumerate(pieces):

            @pl.when(units_ref[UNITS + unit] == split)
            def _():
                columns = slice(split * part, (split + 1) * part)
                full_ref[slot_rows(units_ref, unit), columns] = piece


def attend_back(base, tiles, unit_places, qkv, turned, ranges, grads, att, lse, tables_q, tables,
                rows, tile):
    total = qkv.shape[0]
    count = total // rows
    wide = ranges.shape[2]
    whole = lambda part: pl.BlockSpec((total, LANES), lambda i, *s: (0, part))
    each = lambda *shape: pl.BlockSpec((1,) + shape, lambda i, *s: (i, 0, 0))
    kept = lambda *shape: pl.BlockSpec(shape, lambda i, *s: (0, 0, 0))
    outside = pl.BlockSpec(memory_space=pl.ANY)
    table = pltpu.VMEM((total, LANES), f32)
    return pl.pallas_call(
        functools.partial(attend_back_kernel, tile),
        grid_spec=pltpu.PrefetchScalarGridSpec(
            num_scalar_prefetch=3,
            grid=(count,),
            in_specs=[
                pl.BlockSpec((rows, LANES), lambda i, *s: (i, 0)),
                whole(1),
                whole(2),
                pl.BlockSpec((LANES, total), lambda i, *s: (0, 0)),
                each(2, wide),
                each(wide // 2, LANES),
                each(HD, wide),
                each(1, wide),
                each(HD, wide),
                each(HD, wide),
                outside,
                outside,
            ],
            out_specs=[
                kept(count, rows, 3 * LANES),
                kept(count, wide // 2 + 2 * rows, LANES),
            ],
            scratch_shapes=[
                table,
                table,
                pltpu.VMEM((LANES, wide), f32),
                pltpu.VMEM((LANES, wide), bf16),
                pltpu.VMEM((LANES, rows), f32),
                table,
                table,
                pltpu.SemaphoreType.DMA((2,)),
            ],
        ),
        out_shape=[
            jax.ShapeDtypeStruct((count, rows, 3 * LANES), bf16),
            jax.ShapeDtypeStruct((count, wide // 2 + 2 * rows, LANES), bf16),
        ],
        compiler_params=params(),
        cost_estimate=pl.CostEstimate(
            flops=10 * count * wide * total * LANES,
            bytes_accessed=12 << 20,
            transcendentals=count * wide * total,
        ),
        name="attend_back",
    )(base, tiles, unit_places, qkv, qkv, qkv, turned, ranges, grads, att, lse, *tables_q, *tables)


def lanes_of(slab, at, want):
    slab = slab.astype(f32)
    return slab if at == want else pltpu.roll(slab, HD, 1)


def beside(left, right):
    side = lax.broadcasted_iota(jnp.int32, left.shape, 1) // HD
    return jnp.where(side == 0, left, right).astype(bf16)


def join_packed(parts_ref, heads, splits, part):
    half = part // 2
    tiles = []
    for tile in range(heads // SLOTS):
        blocks = []
        for piece in range(splits):
            for low in range(2):
                sides = []
                for want in range(SLOTS):
                    c, unit = divmod((tile * SLOTS + want) * splits + piece, UNITS)
                    row, at = (low * half, unit) if unit < 2 else (part, low)
                    sides.append(lanes_of(parts_ref[c, row : row + half, :], at, want))
                blocks.append(beside(*sides))
        tiles.append(jnp.concatenate(blocks, axis=0))
    return jnp.concatenate(tiles, axis=1)


def split_packed(values, out_ref, splits, part):
    half = part // 2

    def slab(unit, low, want):
        head, piece = divmod(unit, splits)
        row = piece * part + low * half
        at = head // SLOTS * LANES
        return lanes_of(values[row : row + half, at : at + LANES], head % SLOTS, want)

    for c in range(out_ref.shape[0]):
        unit = UNITS * c
        for low in range(2):
            out_ref[c, low * half : (low + 1) * half, :] = beside(
                slab(unit, low, 0), slab(unit + 1, low, 1)
            )
        out_ref[c, part:, :] = beside(slab(unit + 2, 0, 0), slab(unit + 2, 1, 1))


def join_heads(parts_ref, at, rows, owners):
    side = lax.broadcasted_iota(jnp.int32, (rows, LANES), 1) // HD
    tiles = []
    for tile in range(len(owners) // SLOTS):
        column = jnp.zeros((rows, LANES), f32)
        for half in range(SLOTS):
            for c, slot in owners[tile * SLOTS + half]:
                slab = lanes_of(parts_ref[c, at : at + rows, :], slot, half)
                column = column + jnp.where(side == half, slab, 0.0)
        tiles.append(column.astype(bf16))
    return jnp.concatenate(tiles, axis=1)


def fetch_rows(place_ref, metas, refs, target_ref, at, sems, span=None):
    copies = []
    begin, end = span or (0, refs[0].shape[2])
    for ref, blocks in zip(refs, metas):
        for index, (flip, back) in enumerate(blocks):
            count = ref.shape[1]
            turn = lax.rem(place_ref[1] + place_ref[2] - back, place_ref[2])
            row = (place_ref[0] ^ flip) * place_ref[3] + turn * count
            row = pl.multiple_of(row, count) if count < target_ref.shape[0] else 0
            target = target_ref.at[pl.ds(row, count), pl.ds(at + begin, end - begin)]
            source = ref.at[index, :, pl.ds(begin, end - begin)]
            copies.append(pltpu.make_async_copy(source, target, sems.at[len(copies)]))
            copies[-1].start()
    return copies


def middle_kernel(heads, splits, metas, cut, place_ref, att_ref, tokens_ref, gain_ref, cot_ref,
                  *refs):
    count = len(metas[0]) + len(metas[1])
    sources = refs[:count]
    (output_ref, grad_heads_ref, grad_middle_ref, attended_ref, branch_ref, hidden_ref,
     grad_up_ref, product_ref, w_ref, sems_a, sems_b, sems_c) = refs[count:]
    width = tokens_ref.shape[1]
    units = product_ref.shape[1]
    fetch = functools.partial(fetch_rows, place_ref)
    copies_a = fetch(metas[0], sources[: len(metas[0])], w_ref, 0, sems_a, (0, width))
    copies_b = fetch(metas[0], sources[: len(metas[0])], w_ref, 0, sems_c, (width, cut))
    copies_b += fetch(metas[1], sources[len(metas[0]) :], w_ref, cut, sems_b)
    up = width
    down = width + 2 * units
    gain = gain_ref[1:2, :]
    cot = cot_ref[...]
    part = tokens_ref.shape[0] // splits
    attended = join_packed(att_ref, heads, splits, part)
    attended_ref[...] = attended
    for copy in copies_a:
        copy.wait()
    middle = tokens_ref[...].astype(f32) + jnp.dot(
        attended, w_ref[:, :width], preferred_element_type=f32
    )
    normed, inverse = norm_rows(middle)
    hidden = (normed * gain).astype(bf16)
    hidden_ref[...] = hidden
    for copy in copies_b:
        copy.wait()
    result = middle
    grad_hidden = jnp.zeros(middle.shape, f32)
    for at in range(0, units, CHUNK):
        one = slice(at, at + CHUNK)
        two = slice(units + at, units + at + CHUNK)
        w_one = w_ref[:, up + at : up + at + CHUNK]
        w_two = w_ref[:, up + units + at : up + units + at + CHUNK]
        w_down = w_ref[:, down + at : down + at + CHUNK]
        inner = jnp.dot(hidden, w_one, preferred_element_type=f32)
        gate = jnp.dot(hidden, w_two, preferred_element_type=f32)
        grad_product = jnp.dot(cot, w_down, preferred_element_type=f32)
        cdf = 0.5 * (1.0 + lax.erf(inner * ROOT_HALF))
        gelu_value = inner * cdf
        product = (gelu_value * gate).astype(bf16)
        product_ref[:, one] = product
        slope = cdf + inner * jnp.exp(-0.5 * inner * inner) * INV_ROOT_TWO_PI
        grad_inner = (grad_product * gate * slope).astype(bf16)
        grad_gate = (grad_product * gelu_value).astype(bf16)
        grad_up_ref[:, one] = grad_inner
        grad_up_ref[:, two] = grad_gate
        result = result + dot_tt(product, w_down)
        grad_hidden = grad_hidden + dot_tt(grad_inner, w_one)
        grad_hidden = grad_hidden + dot_tt(grad_gate, w_two)
    output_ref[...] = result.astype(bf16)
    grad_middle = cot.astype(f32) + norm_back(grad_hidden * gain, normed, inverse)
    grad_middle_ref[...] = grad_middle
    grad_branch = grad_middle.astype(bf16)
    branch_ref[...] = grad_branch
    grad_attended = dot_tt(grad_branch, w_ref[:, :width])
    split_packed(grad_attended, grad_heads_ref, splits, part)


def middle_stage(heads, splits, place, att_in, tokens, gains, cot, parts_a, parts_b, units):
    rows, width = tokens.shape
    arrays = [[array for array, _ in parts] for parts in (parts_a, parts_b)]
    metas = [[blocks for _, blocks in parts] for parts in (parts_a, parts_b)]
    vmem = pl.BlockSpec(memory_space=pltpu.VMEM)
    shape = jax.ShapeDtypeStruct
    return pl.pallas_call(
        functools.partial(middle_kernel, heads, splits, metas, arrays[0][0].shape[-1]),
        in_specs=[pl.BlockSpec(memory_space=pltpu.SMEM)]
        + [vmem] * 4
        + [pl.BlockSpec(memory_space=pl.ANY)] * (len(arrays[0]) + len(arrays[1])),
        out_specs=[vmem] * 8,
        out_shape=[
            shape((rows, width), bf16),
            shape(att_in.shape, bf16),
            shape((rows, width), f32),
            shape((rows, width), bf16),
            shape((rows, width), bf16),
            shape((rows, width), bf16),
            shape((rows, 2 * units), bf16),
            shape((rows, units), bf16),
        ],
        scratch_shapes=[pltpu.VMEM((width, 2 * arrays[0][0].shape[-1]), bf16)]
        + [
            pltpu.SemaphoreType.DMA((sum(len(b) for b in blocks),))
            for blocks in (metas[0], metas[1], metas[0])
        ],
        compiler_params=pltpu.CompilerParams(vmem_limit_bytes=VMEM_BYTES),
        cost_estimate=pl.CostEstimate(
            flops=6 * rows * width * (width + 3 * units),
            bytes_accessed=10 << 20,
            transcendentals=2 * rows * units,
        ),
        name="middle_stage",
    )(place, att_in, tokens, gains, cot, *arrays[0], *arrays[1])


def settle_kernel(metas, place_ref, *refs):
    out_ref, sems = refs[-2:]
    for copy in fetch_rows(place_ref, metas, refs[:-2], out_ref, 0, sems):
        copy.wait()


def settle(place, parts, width):
    arrays = [array for array, _ in parts]
    metas = [blocks for _, blocks in parts]
    anywhere = pl.BlockSpec(memory_space=pl.ANY)
    return pl.pallas_call(
        functools.partial(settle_kernel, metas),
        in_specs=[pl.BlockSpec(memory_space=pltpu.SMEM)] + [anywhere] * len(arrays),
        out_specs=pl.BlockSpec(memory_space=pltpu.VMEM),
        out_shape=jax.ShapeDtypeStruct((width, arrays[0].shape[-1]), bf16),
        scratch_shapes=[pltpu.SemaphoreType.DMA((sum(len(b) for b in metas),))],
        compiler_params=pltpu.CompilerParams(vmem_limit_bytes=VMEM_BYTES),
        cost_estimate=pl.CostEstimate(flops=0, bytes_accessed=8 << 20, transcendentals=0),
        name="settle",
    )(place, *arrays)


def finish_kernel(owners, splits, parts_ref, tokens_ref, gain_ref, grad_ref, w_ref, out_ref):
    rows = tokens_ref.shape[0]
    part = rows // splits
    packed = UNITS * part // 2
    joined = jnp.concatenate(
        [
            join_packed(parts_ref, len(owners), splits, part),
            join_heads(parts_ref, packed, rows, owners),
            join_heads(parts_ref, packed + rows, rows, owners),
        ],
        axis=1,
    )
    normed, inverse = norm_rows(tokens_ref[...].astype(f32))
    grad_hidden = dot_tt(joined, w_ref[...])
    back = norm_back(grad_hidden * gain_ref[:1, :], normed, inverse)
    out_ref[...] = (grad_ref[...] + back).astype(bf16)


def finish(owners, splits, joined, tokens, gains, grad_middle, w_joined):
    rows, width = tokens.shape
    vmem = pl.BlockSpec(memory_space=pltpu.VMEM)
    return pl.pallas_call(
        functools.partial(finish_kernel, owners, splits),
        in_specs=[vmem] * 5,
        out_specs=vmem,
        out_shape=jax.ShapeDtypeStruct((rows, width), bf16),
        compiler_params=pltpu.CompilerParams(vmem_limit_bytes=VMEM_BYTES),
        cost_estimate=pl.CostEstimate(
            flops=6 * rows * width * width, bytes_accessed=6 << 20, transcendentals=0
        ),
        name="finish",
    )(joined, tokens, gains, grad_middle, w_joined)


def half_rows(pairs, side, share, refs, lt_ref, emit):
    at = 0
    for pair in range(pairs):
        lt_ref[pair] = jnp.transpose(refs[2 * pair][...])
    for pair in range(pairs):
        right_ref = refs[2 * pair + 1]
        columns = right_ref.shape[1]
        for start in range(0, columns, CHUNK):
            right = right_ref[:, start : start + CHUNK]
            for half in range(lt_ref.shape[1] // share // 2):
                row = pl.multiple_of((2 * half + side) * share, share)
                emit(
                    half,
                    at + start,
                    jnp.dot(lt_ref[pair, pl.ds(row, share), :], right, preferred_element_type=f32),
                )
        at += columns


def pieces_of(cut, at, value):
    end = at + value.shape[1]
    found = []
    if at < cut:
        found.append((0, at, value[:, : min(end, cut) - at]))
    if end > cut:
        found.append((1, max(at, cut) - cut, value[:, max(at, cut) - at :]))
    return found


def gone_grads_kernel(pairs, cut, sides_ref, *refs):
    outs = refs[2 * pairs : 2 * pairs + 2]
    share = outs[0].shape[1]

    def emit(half, at, value):
        for which, start, piece in pieces_of(cut, at, value):
            span = slice(start, start + piece.shape[1])
            outs[which][half, :, span] = piece.astype(bf16)

    half_rows(pairs, 1 - sides_ref[0], share, refs, refs[-1], emit)


def kept_grads_kernel(pairs, cut, sides_ref, *refs):
    sources = refs[2 * pairs : 2 * pairs + 2]
    targets = refs[2 * pairs + 2 : 2 * pairs + 6]
    lt_ref, got_a, got_b, sum_a, sum_b, sems = refs[2 * pairs + 6 :]
    gots = (got_a, got_b)
    copies = [
        pltpu.make_async_copy(source, got, sems.at[i])
        for i, (source, got) in enumerate(zip(sources, gots))
    ]
    for copy in copies:
        copy.start()
    share = got_a.shape[1]
    shard = sum_b.shape[2]
    outer = share // shard // 2
    waits = list(copies)

    def emit(half, at, value):
        while waits:
            waits.pop().wait()
        for which, start, piece in pieces_of(cut, at, value):
            span = slice(start, start + piece.shape[1])
            total = piece + gots[which][half, :, span].astype(f32)
            if which == 0:
                sum_a[sides_ref[1] ^ half, :, span] = total.astype(bf16)
            else:
                for z in range(outer):
                    for x in range(2):
                        row = (z * 2 + x) * shard
                        block = total[row : row + shard].astype(bf16)
                        sum_b[sides_ref[2] ^ x, half * outer + z, :, span] = block

    half_rows(pairs, sides_ref[0], share, refs, lt_ref, emit)
    copies = []
    for i, total in enumerate((sum_a, sum_b)):
        for flip in range(2):
            copies.append(
                pltpu.make_async_copy(total.at[flip], targets[2 * i + flip], sems.at[2 * i + flip])
            )
            copies[-1].start()
    for copy in copies:
        copy.wait()


def weight_grads(kernel, sides, operands, gots, outs, cut, scratch, name):
    vmem = pl.BlockSpec(memory_space=pltpu.VMEM)
    outside = pl.BlockSpec(memory_space=pl.ANY)
    rows, width = operands[0].shape
    columns = sum(array.shape[1] for array in operands[1::2])
    return pl.pallas_call(
        functools.partial(kernel, len(operands) // 2, cut),
        in_specs=[pl.BlockSpec(memory_space=pltpu.SMEM)]
        + [vmem] * len(operands)
        + [outside] * len(gots),
        out_specs=[outside if gots else vmem] * len(outs),
        out_shape=[jax.ShapeDtypeStruct(shape, bf16) for shape in outs],
        scratch_shapes=[pltpu.VMEM((len(operands) // 2, width, rows), bf16)] + scratch,
        compiler_params=pltpu.CompilerParams(vmem_limit_bytes=VMEM_BYTES),
        cost_estimate=pl.CostEstimate(
            flops=rows * width * columns, bytes_accessed=3 * width * columns, transcendentals=0
        ),
        name=name,
    )(sides, *operands, *gots)


def head_grads_kernel(sides_ref, left_ref, right_ref, kept_ref, gone_ref, acc_ref):
    acc_ref[...] = jnp.zeros(acc_ref.shape, f32)
    count, rows, _ = right_ref.shape
    halves, share = kept_ref.shape[:2]

    def step(at, carry):
        span = pl.ds(pl.multiple_of(at * rows, rows), rows)
        left = jnp.transpose(left_ref[span, :])
        acc_ref[...] += jnp.dot(left, right_ref[at], preferred_element_type=f32)
        return carry

    lax.fori_loop(0, count, step, 0)
    for half in range(halves):
        for flip, ref in enumerate((kept_ref, gone_ref)):
            row = pl.multiple_of((2 * half + (sides_ref[0] ^ flip)) * share, share)
            ref[half] = acc_ref[pl.ds(row, share), :].astype(bf16)


def head_grads(fsdp, sides, hidden, grad_joined):
    total, width = hidden.shape
    columns = grad_joined.shape[2]
    vmem = pl.BlockSpec(memory_space=pltpu.VMEM)
    half = jax.ShapeDtypeStruct((fsdp // 2, width // fsdp, columns), bf16)
    return pl.pallas_call(
        head_grads_kernel,
        in_specs=[pl.BlockSpec(memory_space=pltpu.SMEM), vmem, vmem],
        out_specs=[vmem, vmem],
        out_shape=[half, half],
        scratch_shapes=[pltpu.VMEM((width, columns), f32)],
        compiler_params=pltpu.CompilerParams(vmem_limit_bytes=VMEM_BYTES),
        cost_estimate=pl.CostEstimate(
            flops=2 * total * width * columns,
            bytes_accessed=2 * total * (width + columns),
            transcendentals=0,
        ),
        name="head_grads",
    )(sides, hidden, grad_joined)


def add_halves_kernel(picks, joined, sides_ref, *refs):
    pairs = len(picks)
    outs = refs[2 * pairs :]
    begin = 0
    for i, pick in enumerate(picks):
        kept_ref, got_ref = refs[2 * i], refs[2 * i + 1]
        columns = kept_ref.shape[-1]
        for at in range(kept_ref.shape[0]):
            for flip in range(2):
                side = sides_ref[pick] ^ flip
                total = kept_ref[at, side].astype(f32) + got_ref[at, side].astype(f32)
                if joined:
                    outs[flip][at, :, begin : begin + columns] = total.astype(bf16)
                else:
                    outs[2 * i + flip][at] = total.astype(bf16)
        begin += columns


def add_halves(sides, pairs, joined=False):
    flat = []
    shapes = []
    for kept, got, axis, _ in pairs:
        shape = kept.shape
        shape = (
            math.prod(shape[:axis]), 2, math.prod(shape[axis + 1 : -1]), shape[-1]
        )
        flat += [kept.reshape(shape), got.reshape(shape)]
        shapes += [(shape[0], shape[2], shape[3])] * 2
    if joined:
        columns = sum(shape[2] for shape in shapes) // 2
        shapes = [shapes[0][:2] + (columns,)] * 2
    vmem = pl.BlockSpec(memory_space=pltpu.VMEM)
    size = sum(array.size for array in flat)
    return pl.pallas_call(
        functools.partial(add_halves_kernel, [pair[3] for pair in pairs], joined),
        in_specs=[pl.BlockSpec(memory_space=pltpu.SMEM)] + [vmem] * len(flat),
        out_specs=[vmem] * len(shapes),
        out_shape=[jax.ShapeDtypeStruct(shape, bf16) for shape in shapes],
        compiler_params=pltpu.CompilerParams(vmem_limit_bytes=VMEM_BYTES),
        cost_estimate=pl.CostEstimate(flops=size, bytes_accessed=3 * size, transcendentals=0),
        name="add_halves",
    )(sides, *flat)


def flips(count, bit):
    return [(i, i ^ bit) for i in range(count)]


def gate(*values):
    return lax.optimization_barrier(values)


def program(fsdp, ctx):
    def on_device(tokens, segment_ids, positions, gain_attn, w_qkv, w_out, gain_mlp, w_in, w_down,
                  cotangent):
        rows, width = tokens.shape[1:]
        shard = w_qkv.shape[0]
        share = ctx * shard
        heads = width // HD
        common = math.gcd(heads, ctx)
        splits = ctx // common
        units = heads // common
        part = rows // splits
        total = ctx * rows
        outer = ctx // 2
        first = [min(units * c // splits, heads - SLOTS) for c in range(ctx)]
        owners = [
            [
                (c, slot)
                for c in range(ctx)
                for slot in range(SLOTS)
                if first[c] + slot == head
                and max(units * c, head * splits) < min(units * (c + 1), (head + 1) * splits)
            ]
            for head in range(heads)
        ]
        me = lax.axis_index("ctx")
        mine = lax.axis_index("fsdp")
        sides = jnp.stack([mine % 2, mine // 2 % 2, me % 2, me // 2 % 2, me // 4 % 2])
        sides = sides.astype(jnp.int32)
        place = jnp.stack([mine, me // 2, 0 * me + outer, 0 * me + share]).astype(jnp.int32)
        swap = flips(ctx, 1)
        turn = lambda back: [
            (o * 2 + i, (o + back) % outer * 2 + i) for o in range(outer) for i in range(2)
        ]
        by_y = flips(fsdp, 2)
        by_core = flips(fsdp, 1)
        by_hand = (fsdp, ctx) == (4, 8) and shard % 8 == 0
        tile = KEY_TILE
        cot = cotangent[0]
        packed = jnp.concatenate([w_out, w_in, w_down.T], axis=1)
        columns = packed.shape[1]
        cut = (columns // LANES + 1) // 2 * LANES

        def weave(own, got):
            low = jnp.where(me % 2 == 0, own, got)
            high = jnp.where(me % 2 == 0, got, own)
            return jnp.concatenate([low, high], axis=1)

        def tables(sent):
            infos = sent[:, shard : shard + 2, :].astype(f32)
            docs = infos[:, 0, :rows].astype(jnp.int32)
            spots = (infos[:, 0, rows:] * 64 + infos[:, 1, :rows]).reshape(total, 1)
            half = jnp.arange(LANES) % (HD // 2)
            rates = THETA ** (-2.0 * half.astype(f32) / HD)
            angles = spots * rates[None, :]
            edges = docs.reshape(total // GRAIN, GRAIN)
            lo = jnp.sum((edges[None, :, -1] < docs[:, :1]).astype(jnp.int32), axis=1)
            hi = jnp.sum((edges[None, :, 0] <= docs[:, rows - 1 :]).astype(jnp.int32), axis=1)
            count = (hi - lo + tile // GRAIN - 1) // (tile // GRAIN)
            base = jnp.minimum(lo, total // GRAIN - count * (tile // GRAIN))
            unit = units * me + jnp.arange(units, dtype=jnp.int32)
            first_head = jnp.minimum(units * me // splits, heads - SLOTS)
            unit_places = jnp.concatenate([unit // splits - first_head, unit % splits])
            pick = (unit % splits)[:, None] == jnp.arange(splits, dtype=jnp.int32)[None, :]
            own_part = lambda array: jnp.sum(
                jnp.where(pick[None, :, :, None], array.reshape(ctx, 1, splits, part), 0), axis=2
            ).reshape(ctx, 1, units * part)
            doc_q = own_part(docs)
            spot_q = own_part(spots)
            ids = jnp.arange(IDS + 1, dtype=jnp.int32)
            before = jnp.sum((docs.reshape(1, total) < ids[:, None]).astype(jnp.int32), axis=1)
            is_id = doc_q == ids[None, :-1, None]
            bounds = [
                jnp.sum(jnp.where(is_id, edge[None, :, None], 0), axis=1, keepdims=True)
                for edge in (before[:-1], before[1:])
            ]
            return (
                jnp.cos(angles), jnp.sin(angles), base, count, unit_places.astype(jnp.int32),
                jnp.concatenate(bounds, axis=1), spot_q,
            )

        def query_tables(spot_q):
            half = jnp.arange(HD) % (HD // 2)
            angles = THETA ** (-2.0 * half.astype(f32) / HD)[None, :, None] * spot_q
            return jnp.cos(angles), jnp.sin(angles)

        sent = spread(first, w_qkv, gain_attn, gain_mlp, segment_ids, positions)
        sent = lax.all_to_all(sent, "ctx", 0, 0, tiled=True)
        masks = [0]
        if by_hand:
            own = [tokens[0]]
            near = [jnp.stack(
                [packed[:, :cut], jnp.pad(packed[:, cut:], ((0, 0), (0, 2 * cut - columns)))]
            )]
            own.append(lax.ppermute(own[0], "ctx", turn(1)))
            other = [lax.ppermute(own[0], "ctx", swap)]
            near.append(lax.ppermute(near[0], "ctx", turn(1)))
            own[1], other[0], near[1], sent = gate(own[1], other[0], near[1], sent)

        w_parts = sent[:, :shard, :].reshape(1, share, 4 * LANES)
        bit = fsdp // 2
        while bit:
            got = lax.ppermute(w_parts, "fsdp", flips(fsdp, bit))
            w_parts = jnp.concatenate([w_parts, got], axis=0)
            masks += [mask ^ bit for mask in masks]
            bit //= 2
        known = tables(sent)
        if by_hand:
            own.append(lax.ppermute(own[1], "ctx", turn(1)))
            other.append(lax.ppermute(own[1], "ctx", swap))
            near.append(lax.ppermute(near[1], "ctx", turn(1)))
            low_a = jnp.stack([near[0][0], near[1][0]])
            low_b = jnp.stack([near[0][1], near[1][1]])
            own[2], other[1], near[2], low_a, low_b, w_parts, known = gate(
                own[2], other[1], near[2], low_a, low_b, w_parts, known
            )
        cosine, sine, base, count, unit_places, ranges, spot_q = known

        w_heads, gains = ready(masks, mine.astype(jnp.int32).reshape(1), w_parts)

        def project_some(blocks, places, held):
            at = jnp.stack(places).astype(jnp.int32)
            return project(at, blocks, w_heads, gains, cosine, sine, total, held)

        def came_from(step, flip):
            return (me // 2 + outer - step) % outer * 2 + (me % 2 + flip) % 2

        if by_hand:
            own.append(lax.ppermute(own[2], "ctx", turn(1)))
            other.append(lax.ppermute(own[2], "ctx", swap))
            near.append(lax.ppermute(near[2], "ctx", turn(1)))
            next_a = lax.ppermute(low_a, "ctx", swap)
            next_b = lax.ppermute(low_b, "fsdp", by_y)
            held = []
            for step in range(2):
                held = project_some(
                    [own[step], other[step]], [came_from(step, 0), came_from(step, 1)], held
                )
            own[3], other[2], near[3], next_a, next_b, held, late = gate(
                own[3], other[2], near[3], next_a, next_b, held, w_qkv
            )

            other.append(lax.ppermute(own[3], "ctx", swap))
            high_a = jnp.stack([near[2][0], near[3][0]])
            high_b = jnp.stack([near[2][1], near[3][1]])
            past_a = lax.ppermute(high_a, "ctx", swap)
            past_b = lax.ppermute(high_b, "fsdp", by_y)
            held = project_some(
                [own[2], other[2], own[3]],
                [came_from(2, 0), came_from(2, 1), came_from(3, 0)], held,
            )
            ring_c = [late, lax.ppermute(late, "ctx", turn(1))]
            other[3], past_a, past_b, held, ring_c = gate(other[3], past_a, past_b, held, ring_c)
            ring_c = jnp.stack(ring_c)
            ring_c = [ring_c, lax.ppermute(ring_c, "ctx", turn(2))]

            pair_a = jnp.concatenate([weave(low_a, next_a), weave(high_a, past_a)])
            pair_b = jnp.concatenate([low_b, next_b, high_b, past_b])
            far_a = lax.ppermute(pair_a, "fsdp", by_y)
            far_b = lax.ppermute(pair_b, "ctx", swap)
            held = project_some([other[3]], [came_from(3, 1)], held)
        else:
            blocks = lax.all_gather(tokens[0], "ctx", axis=0, tiled=True)
            blocks = blocks.reshape(ctx, rows, width)
            held = []
            for c in range(0, ctx, 2):
                held = project_some(
                    [blocks[c], blocks[c + 1]], [jnp.int32(c), jnp.int32(c + 1)], held
                )
        hidden_one, qkv, turned = held
        att_low, att, lse = attend(
            base, count, unit_places, qkv, turned, ranges, rows, tile
        )
        if by_hand:
            att_low, far_a, far_b, ring_c, spot_q = gate(att_low, far_a, far_b, ring_c, spot_q)
            tables_q = query_tables(spot_q)
            pair_b = weave(pair_b, far_b)
            arrays = [pair_a, far_a, lax.ppermute(pair_a, "fsdp", by_core),
                      lax.ppermute(far_a, "fsdp", by_core),
                      pair_b, lax.ppermute(pair_b, "fsdp", by_core)]
            metas_a = [[(flip + 2 * far, back) for back in range(outer)]
                       for flip in range(2) for far in range(2)]
            metas_b = [[(flip + 2 * near, back) for near in (0, 1) for back in (0, 1)]
                       + [(flip + 2 * near, back) for near in (0, 1) for back in (2, 3)]
                       for flip in range(2)]
            att_in = lax.all_to_all(att_low, "ctx", 0, 0, tiled=True)
            pair_c = jnp.concatenate(ring_c)
            att_in, arrays, pair_c, tables_q = gate(att_in, arrays, pair_c, tables_q)
            near_c = lax.ppermute(pair_c, "ctx", swap)
        else:
            att_in = lax.all_to_all(att_low, "ctx", 0, 0, tiled=True)
            tables_q = query_tables(spot_q)
            every = lax.all_gather(packed, AXES, axis=0, tiled=True)
            arrays = [every[None, :, :cut], every[None, :, cut:]]
            metas_a = metas_b = [[(0, 0)]]
            place = jnp.stack([0 * me, 0 * me, 0 * me + 1, 0 * me]).astype(jnp.int32)
            w_joined = lax.all_gather(w_qkv, AXES, axis=0, tiled=True)
        parts_a = list(zip(arrays, metas_a))
        parts_b = list(zip(arrays[len(metas_a) :], metas_b))

        output, grad_heads, grad_middle, attended, grad_branch, hidden_two, grad_up, product = (
            middle_stage(
                heads, splits, place, att_in, tokens[0], gains, cot, parts_a, parts_b,
                w_down.shape[0],
            )
        )
        operands = [attended, grad_branch, hidden_two, grad_up, cot, product]
        if by_hand:
            grad_heads, operands, near_c = gate(grad_heads, operands, near_c)
            pair_c = weave(pair_c, near_c)
            far_c = lax.ppermute(pair_c, "fsdp", by_y)
        grad_heads = lax.all_to_all(grad_heads, "ctx", 0, 0, tiled=True)
        if by_hand:
            rest = columns - cut
            gone_a, gone_b = weight_grads(
                gone_grads_kernel, sides, operands, [], [(2, share, cut), (2, share, rest)], cut,
                [], "gone_grads",
            )
            got_a = lax.ppermute(gone_a, "fsdp", by_core)
            got_b = lax.ppermute(gone_b, "fsdp", by_core)
            mine_a, other_a, mine_b, other_b = weight_grads(
                kept_grads_kernel, sides, operands, [got_a, got_b],
                [(share, cut)] * 2 + [(2 * outer, shard, rest)] * 2, cut,
                [
                    pltpu.VMEM((2, share, cut), bf16),
                    pltpu.VMEM((2, share, rest), bf16),
                    pltpu.VMEM((2, share, cut), bf16),
                    pltpu.VMEM((2, 2 * outer, shard, rest), bf16),
                    pltpu.SemaphoreType.DMA((4,)),
                ],
                "kept_grads",
            )
            grad_heads, mine_a, other_a, mine_b, other_b = gate(
                grad_heads, mine_a, other_a, mine_b, other_b
            )
            got_a = lax.ppermute(other_a, "fsdp", by_y)
            got_b = lax.ppermute(other_b, "ctx", swap)
        else:
            grad_packed = jnp.concatenate(
                [dot_rows(left, right) for left, right in zip(operands[::2], operands[1::2])],
                axis=1,
            ).astype(bf16)
            grad_packed = lax.psum_scatter(grad_packed, "fsdp", scatter_dimension=0, tiled=True)
            grad_packed = lax.psum_scatter(grad_packed, "ctx", scatter_dimension=0, tiled=True)
            grad_packed = grad_packed.astype(f32)

        grad_joined, grad_sent = attend_back(
            base, count, unit_places, qkv, turned, ranges, grad_heads, att, lse, tables_q,
            (cosine, sine), rows, tile,
        )
        if by_hand:
            grad_joined, grad_sent, mine_a, got_a, mine_b, got_b, pair_c, far_c = gate(
                grad_joined, grad_sent, mine_a, got_a, mine_b, got_b, pair_c, far_c
            )
            joined_in = lax.all_to_all(grad_sent, "ctx", 0, 0, tiled=True)
            arrays = [pair_c, far_c, lax.ppermute(pair_c, "fsdp", by_core),
                      lax.ppermute(far_c, "fsdp", by_core)]
            by_x = lambda array: array.reshape(outer, 2, shard, array.shape[-1])
            mine_a, other_a, mine_b, other_b = add_halves(
                sides,
                [(by_x(mine_a), by_x(got_a), 1, 2),
                 (mine_b.reshape(2, share // 2, rest), got_b.reshape(2, share // 2, rest), 0, 1)],
            )
            sides_late, other_a, other_b = gate(sides, other_a, other_b)
            got_a = lax.ppermute(other_a, "ctx", swap)
            got_b = lax.ppermute(other_b, "fsdp", by_y)
            kept_cols, gone_cols = head_grads(fsdp, sides_late, hidden_one, grad_joined)
            got_cols = lax.ppermute(gone_cols, "fsdp", by_core)
            mine_a, got_a, mine_b, got_b, kept_cols, got_cols, arrays = gate(
                mine_a, got_a, mine_b, got_b, kept_cols, got_cols, arrays
            )
            w_joined = settle(place, list(zip(arrays, metas_a)), width)
            pairs = lambda array: array.reshape(outer // 2, 2, shard, array.shape[-1])
            kept, gone = add_halves(
                sides,
                [(pairs(mine_a), pairs(got_a), 1, 3), (pairs(mine_b), pairs(got_b), 1, 3)],
                joined=True,
            )
            got = lax.ppermute(gone, "ctx", flips(ctx, 2))
            kept_cols, gone_cols = add_halves(sides, [(kept_cols, got_cols, 0, 1)])
            got_cols = lax.ppermute(gone_cols, "fsdp", by_y)
            joined_in, kept, got, kept_cols, got_cols, w_joined = gate(
                joined_in, kept, got, kept_cols, got_cols, w_joined
            )
            kept, gone = add_halves(sides, [(kept, got, 0, 4)])
            got = lax.ppermute(gone, "ctx", flips(ctx, 4))
            grad_packed = kept[0].astype(f32) + got[0].astype(f32)
            grad_cols = (kept_cols[0].astype(f32) + got_cols[0].astype(f32)).astype(bf16)
            grad_cols, _ = gate(grad_cols, gone)
        else:
            joined_in = lax.all_to_all(grad_sent, "ctx", 0, 0, tiled=True)
            grad_cols = dot_rows(hidden_one, grad_joined.reshape(total, 3 * LANES)).astype(bf16)
            grad_cols = lax.psum_scatter(grad_cols, "fsdp", scatter_dimension=0, tiled=True)
        input_grad = finish(owners, splits, joined_in, tokens[0], gains, grad_middle, w_joined)
        grad_cols = grad_cols.reshape(ctx, shard, 3 * LANES)
        grad_cols = lax.all_to_all(grad_cols, "ctx", 0, 0, tiled=True).astype(f32)

        sum_w_out = grad_packed[:, :width]
        sum_w_in = grad_packed[:, width : width + w_in.shape[1]]
        sum_w_down = grad_packed[:, width + w_in.shape[1] :].T
        sum_gain_mlp = jnp.sum(w_in.astype(f32) * sum_w_in, axis=1) / gain_mlp.astype(f32)
        pieces = []
        for third in range(3):
            for head in range(heads):
                column = 0.0
                for c, slot in owners[head]:
                    at = third * LANES + slot * HD
                    column = column + grad_cols[c, :, at : at + HD]
                pieces.append(column)
        sum_w_qkv = jnp.concatenate(pieces, axis=1)
        sum_gain_attn = jnp.sum(w_qkv.astype(f32) * sum_w_qkv, axis=1) / gain_attn.astype(f32)
        return (
            output[None],
            input_grad[None],
            sum_gain_attn,
            sum_w_qkv,
            sum_w_out,
            sum_gain_mlp,
            sum_w_in,
            sum_w_down,
        )

    return on_device


def solution(mesh):
    rows = P(AXES, None)
    tokens = P("fsdp", "ctx", None)
    return jax.shard_map(
        program(mesh.shape["fsdp"], mesh.shape["ctx"]),
        mesh=mesh,
        in_specs=(
            tokens,
            P("fsdp", "ctx"),
            P("fsdp", "ctx"),
            P(AXES),
            rows,
            rows,
            P(AXES),
            rows,
            P(None, AXES),
            tokens,
        ),
        out_specs=(tokens, tokens, P(AXES), rows, rows, P(AXES), rows, P(None, AXES)),
        check_vma=False,
    )
```

```python
import functools
import math

import jax
import jax.numpy as jnp
from jax import lax
from jax.experimental import pallas as pl
from jax.experimental.pallas import tpu as pltpu
from jax.sharding import PartitionSpec as P

HD = 64
SLOTS = 2
LANES = SLOTS * HD
UNITS = 3
IDS = 16
GRAIN = 128
KEY_TILE = 512
CHUNK = 384
EPS = 1e-05
THETA = 160000.0
NEG = -1e30
ROOT_HALF = 0.7071067811865476
INV_ROOT_TWO_PI = 0.3989422804014327
VMEM_BYTES = 58 * 1024 * 1024
AXES = ("fsdp", "ctx")

f32 = jnp.float32
bf16 = jnp.bfloat16


def norm_rows(values):
    center = values - jnp.mean(values, axis=-1, keepdims=True)
    spread = jnp.mean(center * center, axis=-1, keepdims=True)
    inverse = lax.rsqrt(spread + EPS)
    return (center * inverse, inverse)


def norm_back(grad_normed, normed, inverse):
    return inverse * (
        grad_normed
        - jnp.mean(grad_normed, axis=-1, keepdims=True)
        - normed * jnp.mean(grad_normed * normed, axis=-1, keepdims=True)
    )


def rotate_half(values):
    lane = lax.broadcasted_iota(jnp.int32, values.shape, 1)
    ahead = pltpu.roll(values, LANES - HD // 2, 1)
    behind = pltpu.roll(values, HD // 2, 1)
    return jnp.where(lane % HD < HD // 2, -ahead, behind)


def dot_tt(left, right):
    return lax.dot_general(left, right, (((1,), (1,)), ((), ())), preferred_element_type=f32)


def dot_rows(left, right):
    return lax.dot_general(left, right, (((0,), (0,)), ((), ())), preferred_element_type=f32)


def params():
    return pltpu.CompilerParams(
        dimension_semantics=("arbitrary",), vmem_limit_bytes=VMEM_BYTES
    )


def spread_kernel(first, *refs):
    sems, out_ref = refs[-1], refs[5]
    copies = [
        pltpu.make_async_copy(refs[i], refs[6 + i], sems.at[i]) for i in range(5)
    ]
    for copy in copies:
        copy.start()
    for copy in copies:
        copy.wait()
    w_ref, gain_one_ref, gain_two_ref, doc_ref, place_ref = refs[6:11]
    shard, columns = w_ref.shape
    width = columns // 3
    rows = doc_ref.shape[1]
    square = (shard, shard)
    eye = lax.broadcasted_iota(jnp.int32, square, 0) == lax.broadcasted_iota(jnp.int32, square, 1)

    def upright(ref):
        spread = jnp.where(eye, ref[...].astype(f32), 0.0)
        return jnp.sum(spread, axis=1, keepdims=True).astype(bf16)

    lane = lax.broadcasted_iota(jnp.int32, (shard, LANES), 1)
    gains = jnp.where(
        lane == 0, upright(gain_one_ref), jnp.where(lane == 1, upright(gain_two_ref), bf16(0))
    )
    place = place_ref[...]
    top = jnp.concatenate([doc_ref[...], place >> 6], axis=1).astype(f32)
    low = jnp.concatenate([place & 63, jnp.zeros_like(place)], axis=1).astype(f32)
    row = lax.broadcasted_iota(jnp.int32, (8, 2 * rows), 0)
    places = jnp.where(row == 0, top, jnp.where(row == 1, low, 0.0)).astype(bf16)
    for c, head in enumerate(first):
        for part in range(3):
            at = part * width + head * HD
            out_ref[c, :shard, part * LANES : (part + 1) * LANES] = w_ref[:, at : at + LANES]
        out_ref[c, :shard, 3 * LANES :] = gains
        out_ref[c, shard:, :] = places


def spread(first, w_qkv, gain_one, gain_two, docs, places):
    shard = w_qkv.shape[0]
    operands = (w_qkv, gain_one[None], gain_two[None], docs, places)
    return pl.pallas_call(
        functools.partial(spread_kernel, first),
        in_specs=[pl.BlockSpec(memory_space=pl.ANY)] * 5,
        out_specs=pl.BlockSpec(memory_space=pltpu.VMEM),
        out_shape=jax.ShapeDtypeStruct((len(first), shard + 8, 4 * LANES), bf16),
        scratch_shapes=[pltpu.VMEM(array.shape, array.dtype) for array in operands]
        + [pltpu.SemaphoreType.DMA((5,))],
        compiler_params=pltpu.CompilerParams(vmem_limit_bytes=VMEM_BYTES),
        name="spread",
    )(*operands)


def ready_kernel(masks, at_ref, w_ref, w_out_ref, gains_ref):
    share = w_ref.shape[1]
    for i, mask in enumerate(masks):
        start = pl.multiple_of((at_ref[0] ^ mask) * share, share)
        w_out_ref[pl.ds(start, share), :] = w_ref[i]
    gains_ref[...] = jnp.transpose(w_out_ref[:, 3 * LANES :].astype(f32))[:8]


def ready(masks, at, w_parts):
    count, share, columns = w_parts.shape
    vmem = pl.BlockSpec(memory_space=pltpu.VMEM)
    return pl.pallas_call(
        functools.partial(ready_kernel, masks),
        in_specs=[pl.BlockSpec(memory_space=pltpu.SMEM), vmem],
        out_specs=[vmem, vmem],
        out_shape=[
            jax.ShapeDtypeStruct((count * share, columns), bf16),
            jax.ShapeDtypeStruct((8, count * share), f32),
        ],
        compiler_params=pltpu.CompilerParams(vmem_limit_bytes=VMEM_BYTES),
        name="ready",
    )(at, w_parts)


def project_kernel(count, at_ref, *refs):
    x_refs = refs[:count]
    w_ref, gains_ref, cos_ref, sin_ref = refs[count : count + 4]
    hidden_ref, qkv_ref, turned_ref = refs[-3:]
    x = x_refs[0][...]
    for i in range(1, count):
        x = jnp.where(pl.program_id(0) == i, x_refs[i][...], x)
    x = x.astype(f32)
    normed, _ = norm_rows(x)
    hidden = (normed * gains_ref[:1, :]).astype(bf16)
    hidden_ref[...] = hidden
    joined = jnp.dot(hidden, w_ref[...], preferred_element_type=f32)
    cosine = cos_ref[...]
    sine = sin_ref[...]
    query = joined[:, :LANES]
    keys = joined[:, LANES : 2 * LANES]
    values = joined[:, 2 * LANES :]
    query = (query * cosine + rotate_half(query) * sine).astype(bf16)
    keys = keys * cosine + rotate_half(keys) * sine
    qkv_ref[:, :LANES] = query * bf16(HD**-0.5)
    qkv_ref[:, LANES : 2 * LANES] = keys.astype(bf16)
    qkv_ref[:, 2 * LANES :] = values.astype(bf16)
    turned_ref[:LANES, :] = jnp.transpose(keys).astype(bf16)
    turned_ref[LANES:, :] = jnp.transpose(values).astype(bf16)


def project(at, blocks, w_heads, gains, cosine, sine, total, held):
    rows, width = blocks[0].shape
    count = len(blocks)
    fixed = lambda *shape: pl.BlockSpec(shape, lambda i, at: (0,) * len(shape))
    tall = lambda width: pl.BlockSpec((rows, width), lambda i, at: (at[i], 0))
    shapes = [
        jax.ShapeDtypeStruct((total, width), bf16),
        jax.ShapeDtypeStruct((total, 3 * LANES), bf16),
        jax.ShapeDtypeStruct((2 * LANES, total), bf16),
    ]
    return pl.pallas_call(
        functools.partial(project_kernel, count),
        grid_spec=pltpu.PrefetchScalarGridSpec(
            num_scalar_prefetch=1,
            grid=(count,),
            in_specs=[fixed(rows, width)] * count
            + [fixed(width, 3 * LANES), fixed(8, width), tall(LANES), tall(LANES)]
            + [pl.BlockSpec(memory_space=pl.ANY) for _ in held],
            out_specs=[
                tall(width),
                tall(3 * LANES),
                pl.BlockSpec((2 * LANES, rows), lambda i, at: (0, at[i])),
            ],
        ),
        out_shape=shapes,
        input_output_aliases={count + 5 + i: i for i in range(len(held))},
        compiler_params=params(),
        cost_estimate=pl.CostEstimate(
            flops=2 * count * rows * width * 3 * LANES,
            bytes_accessed=3 * count << 20,
            transcendentals=0,
        ),
        name="project",
    )(at, *blocks, w_heads, gains, cosine, sine, *held)


def gather_rows(units_ref, ref, part):
    lane = lax.broadcasted_iota(jnp.int32, (part, LANES), 1)
    chunks = []
    for unit in range(UNITS):
        start = pl.multiple_of(units_ref[UNITS + unit] * part, part)
        chunk = ref[pl.ds(start, part), :]
        chunks.append(jnp.where(lane // HD == units_ref[unit], chunk, jnp.zeros_like(chunk)))
    return jnp.concatenate(chunks, axis=0)


def slot_rows(units_ref, unit):
    return pl.ds(pl.multiple_of(units_ref[unit] * HD, HD), HD)


def pack(pieces):
    half = pieces[2].shape[1] // 2
    top = jnp.concatenate(pieces[:2], axis=0)
    low = jnp.concatenate([pieces[2][:, :half], pieces[2][:, half:]], axis=0)
    return jnp.concatenate([jnp.transpose(top), jnp.transpose(low)], axis=0).astype(bf16)


def unpack(packed, part):
    values = packed.astype(f32)
    top = jnp.transpose(values[:part])
    low = jnp.transpose(values[part:])
    return [top[:HD], top[HD:], jnp.concatenate([low[:HD], low[HD:]], axis=1)]


def fold(values, reduce):
    rows, wide = values.shape
    return reduce(values.reshape(rows // 8, 8, wide), axis=0)


def tile_span(base_ref, block, at, tile):
    return pl.ds(pl.multiple_of(base_ref[block] * GRAIN + at * tile, GRAIN), tile)


def masked(scores, base_ref, block, at, tile, range_ref):
    key = lax.broadcasted_iota(jnp.int32, scores.shape, 0) + (base_ref[block] * GRAIN + at * tile)
    same = (key >= range_ref[0, :1, :]) & (key < range_ref[0, 1:2, :])
    return jnp.where(same, scores, NEG)


def attend_kernel(tile, base_ref, count_ref, units_ref, q_ref, k_ref, vt_ref, range_ref,
                  low_ref, att_ref, lse_ref, s_ref, acc_ref):
    block = pl.program_id(0)
    wide = s_ref.shape[1]
    part = wide // UNITS
    queries = gather_rows(units_ref, q_ref, part)

    def score(at, top):
        span = tile_span(base_ref, block, at, tile)
        scores = masked(dot_tt(k_ref[span, :], queries), base_ref, block, at, tile, range_ref)
        s_ref[span, :] = scores
        return jnp.maximum(top, fold(scores, jnp.max))

    count = count_ref[block]
    top = lax.fori_loop(0, count, score, jnp.full((8, wide), NEG, f32))
    top = jnp.max(top, axis=0, keepdims=True)

    def weigh(at, carry):
        total, accum = carry
        span = tile_span(base_ref, block, at, tile)
        expo = jnp.exp(s_ref[span, :] - top)
        total = total + fold(expo, jnp.sum)
        accum = accum + jnp.dot(vt_ref[:, span], expo.astype(bf16), preferred_element_type=f32)
        return (total, accum)

    total, accum = lax.fori_loop(
        0, count, weigh, (jnp.zeros((8, wide), f32), jnp.zeros((LANES, wide), f32))
    )
    total = jnp.sum(total, axis=0, keepdims=True)
    lse_ref[0] = top + jnp.log(total)
    acc_ref[...] = accum / total
    pieces = [
        acc_ref[slot_rows(units_ref, unit), unit * part : (unit + 1) * part]
        for unit in range(UNITS)
    ]
    att_ref[0] = jnp.concatenate(pieces, axis=1)
    low_ref[0] = pack(pieces)


def attend(base, tiles, unit_places, qkv, turned, ranges, rows, tile):
    total = qkv.shape[0]
    count = total // rows
    wide = ranges.shape[2]
    each = lambda *shape: pl.BlockSpec((1,) + shape, lambda i, *s: (i, 0, 0))
    return pl.pallas_call(
        functools.partial(attend_kernel, tile),
        grid_spec=pltpu.PrefetchScalarGridSpec(
            num_scalar_prefetch=3,
            grid=(count,),
            in_specs=[
                pl.BlockSpec((rows, LANES), lambda i, *s: (i, 0)),
                pl.BlockSpec((total, LANES), lambda i, *s: (0, 1)),
                pl.BlockSpec((LANES, total), lambda i, *s: (1, 0)),
                each(2, wide),
            ],
            out_specs=[each(wide // 2, LANES), each(HD, wide), each(1, wide)],
            scratch_shapes=[pltpu.VMEM((total, wide), f32), pltpu.VMEM((LANES, wide), f32)],
        ),
        out_shape=[
            jax.ShapeDtypeStruct((count, wide // 2, LANES), bf16),
            jax.ShapeDtypeStruct((count, HD, wide), f32),
            jax.ShapeDtypeStruct((count, 1, wide), f32),
        ],
        compiler_params=params(),
        cost_estimate=pl.CostEstimate(
            flops=4 * count * wide * total * LANES,
            bytes_accessed=8 << 20,
            transcendentals=count * wide * total,
        ),
        name="attend",
    )(base, tiles, unit_places, qkv, qkv, turned, ranges)


def attend_back_kernel(tile, base_ref, count_ref, units_ref, q_ref, k_ref, v_ref, kt_ref, range_ref,
                       grad_ref, att_ref, lse_ref, cos_q_ref, sin_q_ref, cos_hbm, sin_hbm,
                       out_ref, send_ref, dk_ref, dv_ref, acc_ref, gt_ref, full_ref, cos_ref,
                       sin_ref, sems):
    block = pl.program_id(0)
    count = pl.num_programs(0)
    rows = full_ref.shape[1]
    wide = acc_ref.shape[1]
    part = wide // UNITS
    tables = [
        pltpu.make_async_copy(cos_hbm, cos_ref, sems.at[0]),
        pltpu.make_async_copy(sin_hbm, sin_ref, sems.at[1]),
    ]

    @pl.when(block == 0)
    def _():
        for table in tables:
            table.start()
        dk_ref[...] = jnp.zeros(dk_ref.shape, f32)
        dv_ref[...] = jnp.zeros(dv_ref.shape, f32)
        gt_ref[...] = jnp.zeros(gt_ref.shape, bf16)
        full_ref[...] = jnp.zeros(full_ref.shape, f32)

    queries = gather_rows(units_ref, q_ref, part)
    grads = unpack(grad_ref[0], part)
    delta = jnp.sum(jnp.concatenate(grads, axis=1) * att_ref[0], axis=0, keepdims=True)
    for unit, piece in enumerate(grads):
        columns = slice(unit * part, (unit + 1) * part)
        gt_ref[slot_rows(units_ref, unit), columns] = piece.astype(bf16)
    log_sum = lse_ref[0]

    def step(at, grad_query):
        span = tile_span(base_ref, block, at, tile)
        grads_t = gt_ref[...]
        scores = masked(dot_tt(k_ref[span, :], queries), base_ref, block, at, tile, range_ref)
        grad_probs = jnp.dot(v_ref[span, :], grads_t, preferred_element_type=f32)
        probs = jnp.exp(scores - log_sum)
        dv_ref[span, :] += dot_tt(probs.astype(bf16), grads_t)
        grad_scores = (probs * (grad_probs - delta)).astype(bf16)
        dk_ref[span, :] += jnp.dot(grad_scores, queries, preferred_element_type=f32)
        return grad_query + jnp.dot(kt_ref[:, span], grad_scores, preferred_element_type=f32)

    acc_ref[...] = lax.fori_loop(0, count_ref[block], step, jnp.zeros((LANES, wide), f32))
    pieces = []
    for unit in range(UNITS):
        columns = slice(unit * part, (unit + 1) * part)
        piece = acc_ref[slot_rows(units_ref, unit), columns] * HD**-0.5
        turned = piece * sin_q_ref[0, :, columns]
        turned = jnp.concatenate([-turned[HD // 2 :], turned[: HD // 2]], axis=0)
        pieces.append(piece * cos_q_ref[0, :, columns] - turned)
    send_ref[block, : wide // 2, :] = pack(pieces)
    place_units(units_ref, full_ref, pieces, part)
    out_ref[block, :, :LANES] = jnp.transpose(full_ref[...]).astype(bf16)

    @pl.when(block == count - 1)
    def _():
        for table in tables:
            table.wait()

        def finish(at, carry):
            span = pl.ds(pl.multiple_of(at * rows, rows), rows)
            keys = dk_ref[span, :]
            keys = keys * cos_ref[span, :] - rotate_half(keys * sin_ref[span, :])
            keys = keys.astype(bf16)
            values = dv_ref[span, :].astype(bf16)
            out_ref[at, :, LANES : 2 * LANES] = keys
            out_ref[at, :, 2 * LANES :] = values
            send_ref[at, wide // 2 : wide // 2 + rows, :] = keys
            send_ref[at, wide // 2 + rows :, :] = values
            return carry

        lax.fori_loop(0, count, finish, 0)


def place_units(units_ref, full_ref, pieces, part):
    rows = full_ref.shape[1]
    for split in range(rows // part):
        for unit, piece in enumerate(pieces):

            @pl.when(units_ref[UNITS + unit] == split)
            def _():
                columns = slice(split * part, (split + 1) * part)
                full_ref[slot_rows(units_ref, unit), columns] = piece


def attend_back(base, tiles, unit_places, qkv, turned, ranges, grads, att, lse, tables_q, tables,
                rows, tile):
    total = qkv.shape[0]
    count = total // rows
    wide = ranges.shape[2]
    whole = lambda part: pl.BlockSpec((total, LANES), lambda i, *s: (0, part))
    each = lambda *shape: pl.BlockSpec((1,) + shape, lambda i, *s: (i, 0, 0))
    kept = lambda *shape: pl.BlockSpec(shape, lambda i, *s: (0, 0, 0))
    outside = pl.BlockSpec(memory_space=pl.ANY)
    table = pltpu.VMEM((total, LANES), f32)
    return pl.pallas_call(
        functools.partial(attend_back_kernel, tile),
        grid_spec=pltpu.PrefetchScalarGridSpec(
            num_scalar_prefetch=3,
            grid=(count,),
            in_specs=[
                pl.BlockSpec((rows, LANES), lambda i, *s: (i, 0)),
                whole(1),
                whole(2),
                pl.BlockSpec((LANES, total), lambda i, *s: (0, 0)),
                each(2, wide),
                each(wide // 2, LANES),
                each(HD, wide),
                each(1, wide),
                each(HD, wide),
                each(HD, wide),
                outside,
                outside,
            ],
            out_specs=[
                kept(count, rows, 3 * LANES),
                kept(count, wide // 2 + 2 * rows, LANES),
            ],
            scratch_shapes=[
                table,
                table,
                pltpu.VMEM((LANES, wide), f32),
                pltpu.VMEM((LANES, wide), bf16),
                pltpu.VMEM((LANES, rows), f32),
                table,
                table,
                pltpu.SemaphoreType.DMA((2,)),
            ],
        ),
        out_shape=[
            jax.ShapeDtypeStruct((count, rows, 3 * LANES), bf16),
            jax.ShapeDtypeStruct((count, wide // 2 + 2 * rows, LANES), bf16),
        ],
        compiler_params=params(),
        cost_estimate=pl.CostEstimate(
            flops=10 * count * wide * total * LANES,
            bytes_accessed=12 << 20,
            transcendentals=count * wide * total,
        ),
        name="attend_back",
    )(base, tiles, unit_places, qkv, qkv, qkv, turned, ranges, grads, att, lse, *tables_q, *tables)


def lanes_of(slab, at, want):
    slab = slab.astype(f32)
    return slab if at == want else pltpu.roll(slab, HD, 1)


def beside(left, right):
    side = lax.broadcasted_iota(jnp.int32, left.shape, 1) // HD
    return jnp.where(side == 0, left, right).astype(bf16)


def join_packed(parts_ref, heads, splits, part):
    half = part // 2
    tiles = []
    for tile in range(heads // SLOTS):
        blocks = []
        for piece in range(splits):
            for low in range(2):
                sides = []
                for want in range(SLOTS):
                    c, unit = divmod((tile * SLOTS + want) * splits + piece, UNITS)
                    row, at = (low * half, unit) if unit < 2 else (part, low)
                    sides.append(lanes_of(parts_ref[c, row : row + half, :], at, want))
                blocks.append(beside(*sides))
        tiles.append(jnp.concatenate(blocks, axis=0))
    return jnp.concatenate(tiles, axis=1)


def split_packed(values, out_ref, splits, part):
    half = part // 2

    def slab(unit, low, want):
        head, piece = divmod(unit, splits)
        row = piece * part + low * half
        at = head // SLOTS * LANES
        return lanes_of(values[row : row + half, at : at + LANES], head % SLOTS, want)

    for c in range(out_ref.shape[0]):
        unit = UNITS * c
        for low in range(2):
            out_ref[c, low * half : (low + 1) * half, :] = beside(
                slab(unit, low, 0), slab(unit + 1, low, 1)
            )
        out_ref[c, part:, :] = beside(slab(unit + 2, 0, 0), slab(unit + 2, 1, 1))


def join_heads(parts_ref, at, rows, owners):
    side = lax.broadcasted_iota(jnp.int32, (rows, LANES), 1) // HD
    tiles = []
    for tile in range(len(owners) // SLOTS):
        column = jnp.zeros((rows, LANES), f32)
        for half in range(SLOTS):
            for c, slot in owners[tile * SLOTS + half]:
                slab = lanes_of(parts_ref[c, at : at + rows, :], slot, half)
                column = column + jnp.where(side == half, slab, 0.0)
        tiles.append(column.astype(bf16))
    return jnp.concatenate(tiles, axis=1)


def fetch_rows(place_ref, metas, refs, target_ref, at, sems, span=None):
    copies = []
    begin, end = span or (0, refs[0].shape[2])
    for ref, blocks in zip(refs, metas):
        for index, (flip, back) in enumerate(blocks):
            count = ref.shape[1]
            turn = lax.rem(place_ref[1] + place_ref[2] - back, place_ref[2])
            row = (place_ref[0] ^ flip) * place_ref[3] + turn * count
            row = pl.multiple_of(row, count) if count < target_ref.shape[0] else 0
            target = target_ref.at[pl.ds(row, count), pl.ds(at + begin, end - begin)]
            source = ref.at[index, :, pl.ds(begin, end - begin)]
            copies.append(pltpu.make_async_copy(source, target, sems.at[len(copies)]))
            copies[-1].start()
    return copies


def middle_kernel(heads, splits, metas, cut, place_ref, att_ref, tokens_ref, gain_ref, cot_ref,
                  *refs):
    count = len(metas[0]) + len(metas[1])
    sources = refs[:count]
    (output_ref, grad_heads_ref, grad_middle_ref, attended_ref, branch_ref, hidden_ref,
     grad_up_ref, product_ref, w_ref, sems_a, sems_b, sems_c) = refs[count:]
    width = tokens_ref.shape[1]
    units = product_ref.shape[1]
    fetch = functools.partial(fetch_rows, place_ref)
    copies_a = fetch(metas[0], sources[: len(metas[0])], w_ref, 0, sems_a, (0, width))
    copies_b = fetch(metas[0], sources[: len(metas[0])], w_ref, 0, sems_c, (width, cut))
    copies_b += fetch(metas[1], sources[len(metas[0]) :], w_ref, cut, sems_b)
    up = width
    down = width + 2 * units
    gain = gain_ref[1:2, :]
    cot = cot_ref[...]
    part = tokens_ref.shape[0] // splits
    attended = join_packed(att_ref, heads, splits, part)
    attended_ref[...] = attended
    for copy in copies_a:
        copy.wait()
    middle = tokens_ref[...].astype(f32) + jnp.dot(
        attended, w_ref[:, :width], preferred_element_type=f32
    )
    normed, inverse = norm_rows(middle)
    hidden = (normed * gain).astype(bf16)
    hidden_ref[...] = hidden
    for copy in copies_b:
        copy.wait()
    result = middle
    grad_hidden = jnp.zeros(middle.shape, f32)
    for at in range(0, units, CHUNK):
        one = slice(at, at + CHUNK)
        two = slice(units + at, units + at + CHUNK)
        w_one = w_ref[:, up + at : up + at + CHUNK]
        w_two = w_ref[:, up + units + at : up + units + at + CHUNK]
        w_down = w_ref[:, down + at : down + at + CHUNK]
        inner = jnp.dot(hidden, w_one, preferred_element_type=f32)
        gate = jnp.dot(hidden, w_two, preferred_element_type=f32)
        grad_product = jnp.dot(cot, w_down, preferred_element_type=f32)
        cdf = 0.5 * (1.0 + lax.erf(inner * ROOT_HALF))
        gelu_value = inner * cdf
        product = (gelu_value * gate).astype(bf16)
        product_ref[:, one] = product
        slope = cdf + inner * jnp.exp(-0.5 * inner * inner) * INV_ROOT_TWO_PI
        grad_inner = (grad_product * gate * slope).astype(bf16)
        grad_gate = (grad_product * gelu_value).astype(bf16)
        grad_up_ref[:, one] = grad_inner
        grad_up_ref[:, two] = grad_gate
        result = result + dot_tt(product, w_down)
        grad_hidden = grad_hidden + dot_tt(grad_inner, w_one)
        grad_hidden = grad_hidden + dot_tt(grad_gate, w_two)
    output_ref[...] = result.astype(bf16)
    grad_middle = cot.astype(f32) + norm_back(grad_hidden * gain, normed, inverse)
    grad_middle_ref[...] = grad_middle
    grad_branch = grad_middle.astype(bf16)
    branch_ref[...] = grad_branch
    grad_attended = dot_tt(grad_branch, w_ref[:, :width])
    split_packed(grad_attended, grad_heads_ref, splits, part)


def middle_stage(heads, splits, place, att_in, tokens, gains, cot, parts_a, parts_b, units):
    rows, width = tokens.shape
    arrays = [[array for array, _ in parts] for parts in (parts_a, parts_b)]
    metas = [[blocks for _, blocks in parts] for parts in (parts_a, parts_b)]
    vmem = pl.BlockSpec(memory_space=pltpu.VMEM)
    shape = jax.ShapeDtypeStruct
    return pl.pallas_call(
        functools.partial(middle_kernel, heads, splits, metas, arrays[0][0].shape[-1]),
        in_specs=[pl.BlockSpec(memory_space=pltpu.SMEM)]
        + [vmem] * 4
        + [pl.BlockSpec(memory_space=pl.ANY)] * (len(arrays[0]) + len(arrays[1])),
        out_specs=[vmem] * 8,
        out_shape=[
            shape((rows, width), bf16),
            shape(att_in.shape, bf16),
            shape((rows, width), f32),
            shape((rows, width), bf16),
            shape((rows, width), bf16),
            shape((rows, width), bf16),
            shape((rows, 2 * units), bf16),
            shape((rows, units), bf16),
        ],
        scratch_shapes=[pltpu.VMEM((width, 2 * arrays[0][0].shape[-1]), bf16)]
        + [
            pltpu.SemaphoreType.DMA((sum(len(b) for b in blocks),))
            for blocks in (metas[0], metas[1], metas[0])
        ],
        compiler_params=pltpu.CompilerParams(vmem_limit_bytes=VMEM_BYTES),
        cost_estimate=pl.CostEstimate(
            flops=6 * rows * width * (width + 3 * units),
            bytes_accessed=10 << 20,
            transcendentals=2 * rows * units,
        ),
        name="middle_stage",
    )(place, att_in, tokens, gains, cot, *arrays[0], *arrays[1])


def settle_kernel(metas, place_ref, *refs):
    out_ref, sems = refs[-2:]
    for copy in fetch_rows(place_ref, metas, refs[:-2], out_ref, 0, sems):
        copy.wait()


def settle(place, parts, width):
    arrays = [array for array, _ in parts]
    metas = [blocks for _, blocks in parts]
    anywhere = pl.BlockSpec(memory_space=pl.ANY)
    return pl.pallas_call(
        functools.partial(settle_kernel, metas),
        in_specs=[pl.BlockSpec(memory_space=pltpu.SMEM)] + [anywhere] * len(arrays),
        out_specs=pl.BlockSpec(memory_space=pltpu.VMEM),
        out_shape=jax.ShapeDtypeStruct((width, arrays[0].shape[-1]), bf16),
        scratch_shapes=[pltpu.SemaphoreType.DMA((sum(len(b) for b in metas),))],
        compiler_params=pltpu.CompilerParams(vmem_limit_bytes=VMEM_BYTES),
        cost_estimate=pl.CostEstimate(flops=0, bytes_accessed=8 << 20, transcendentals=0),
        name="settle",
    )(place, *arrays)


def finish_kernel(owners, splits, parts_ref, tokens_ref, gain_ref, grad_ref, w_ref, out_ref):
    rows = tokens_ref.shape[0]
    part = rows // splits
    packed = UNITS * part // 2
    joined = jnp.concatenate(
        [
            join_packed(parts_ref, len(owners), splits, part),
            join_heads(parts_ref, packed, rows, owners),
            join_heads(parts_ref, packed + rows, rows, owners),
        ],
        axis=1,
    )
    normed, inverse = norm_rows(tokens_ref[...].astype(f32))
    grad_hidden = dot_tt(joined, w_ref[...])
    back = norm_back(grad_hidden * gain_ref[:1, :], normed, inverse)
    out_ref[...] = (grad_ref[...] + back).astype(bf16)


def finish(owners, splits, joined, tokens, gains, grad_middle, w_joined):
    rows, width = tokens.shape
    vmem = pl.BlockSpec(memory_space=pltpu.VMEM)
    return pl.pallas_call(
        functools.partial(finish_kernel, owners, splits),
        in_specs=[vmem] * 5,
        out_specs=vmem,
        out_shape=jax.ShapeDtypeStruct((rows, width), bf16),
        compiler_params=pltpu.CompilerParams(vmem_limit_bytes=VMEM_BYTES),
        cost_estimate=pl.CostEstimate(
            flops=6 * rows * width * width, bytes_accessed=6 << 20, transcendentals=0
        ),
        name="finish",
    )(joined, tokens, gains, grad_middle, w_joined)


def half_rows(pairs, side, share, refs, lt_ref, emit):
    at = 0
    for pair in range(pairs):
        lt_ref[pair] = jnp.transpose(refs[2 * pair][...])
    for pair in range(pairs):
        right_ref = refs[2 * pair + 1]
        columns = right_ref.shape[1]
        for start in range(0, columns, CHUNK):
            right = right_ref[:, start : start + CHUNK]
            for half in range(lt_ref.shape[1] // share // 2):
                row = pl.multiple_of((2 * half + side) * share, share)
                emit(
                    half,
                    at + start,
                    jnp.dot(lt_ref[pair, pl.ds(row, share), :], right, preferred_element_type=f32),
                )
        at += columns


def pieces_of(cut, at, value):
    end = at + value.shape[1]
    found = []
    if at < cut:
        found.append((0, at, value[:, : min(end, cut) - at]))
    if end > cut:
        found.append((1, max(at, cut) - cut, value[:, max(at, cut) - at :]))
    return found


def gone_grads_kernel(pairs, cut, sides_ref, *refs):
    outs = refs[2 * pairs : 2 * pairs + 2]
    share = outs[0].shape[1]

    def emit(half, at, value):
        for which, start, piece in pieces_of(cut, at, value):
            span = slice(start, start + piece.shape[1])
            outs[which][half, :, span] = piece.astype(bf16)

    half_rows(pairs, 1 - sides_ref[0], share, refs, refs[-1], emit)


def kept_grads_kernel(pairs, cut, sides_ref, *refs):
    sources = refs[2 * pairs : 2 * pairs + 2]
    targets = refs[2 * pairs + 2 : 2 * pairs + 6]
    lt_ref, got_a, got_b, sum_a, sum_b, sems = refs[2 * pairs + 6 :]
    gots = (got_a, got_b)
    copies = [
        pltpu.make_async_copy(source, got, sems.at[i])
        for i, (source, got) in enumerate(zip(sources, gots))
    ]
    for copy in copies:
        copy.start()
    share = got_a.shape[1]
    shard = sum_b.shape[2]
    outer = share // shard // 2
    waits = list(copies)

    def emit(half, at, value):
        while waits:
            waits.pop().wait()
        for which, start, piece in pieces_of(cut, at, value):
            span = slice(start, start + piece.shape[1])
            total = piece + gots[which][half, :, span].astype(f32)
            if which == 0:
                sum_a[sides_ref[1] ^ half, :, span] = total.astype(bf16)
            else:
                for z in range(outer):
                    for x in range(2):
                        row = (z * 2 + x) * shard
                        block = total[row : row + shard].astype(bf16)
                        sum_b[sides_ref[2] ^ x, half * outer + z, :, span] = block

    half_rows(pairs, sides_ref[0], share, refs, lt_ref, emit)
    copies = []
    for i, total in enumerate((sum_a, sum_b)):
        for flip in range(2):
            copies.append(
                pltpu.make_async_copy(total.at[flip], targets[2 * i + flip], sems.at[2 * i + flip])
            )
            copies[-1].start()
    for copy in copies:
        copy.wait()


def weight_grads(kernel, sides, operands, gots, outs, cut, scratch, name):
    vmem = pl.BlockSpec(memory_space=pltpu.VMEM)
    outside = pl.BlockSpec(memory_space=pl.ANY)
    rows, width = operands[0].shape
    columns = sum(array.shape[1] for array in operands[1::2])
    return pl.pallas_call(
        functools.partial(kernel, len(operands) // 2, cut),
        in_specs=[pl.BlockSpec(memory_space=pltpu.SMEM)]
        + [vmem] * len(operands)
        + [outside] * len(gots),
        out_specs=[outside if gots else vmem] * len(outs),
        out_shape=[jax.ShapeDtypeStruct(shape, bf16) for shape in outs],
        scratch_shapes=[pltpu.VMEM((len(operands) // 2, width, rows), bf16)] + scratch,
        compiler_params=pltpu.CompilerParams(vmem_limit_bytes=VMEM_BYTES),
        cost_estimate=pl.CostEstimate(
            flops=rows * width * columns, bytes_accessed=3 * width * columns, transcendentals=0
        ),
        name=name,
    )(sides, *operands, *gots)


def head_grads_kernel(sides_ref, left_ref, right_ref, kept_ref, gone_ref, acc_ref):
    acc_ref[...] = jnp.zeros(acc_ref.shape, f32)
    count, rows, _ = right_ref.shape
    halves, share = kept_ref.shape[:2]

    def step(at, carry):
        span = pl.ds(pl.multiple_of(at * rows, rows), rows)
        left = jnp.transpose(left_ref[span, :])
        acc_ref[...] += jnp.dot(left, right_ref[at], preferred_element_type=f32)
        return carry

    lax.fori_loop(0, count, step, 0)
    for half in range(halves):
        for flip, ref in enumerate((kept_ref, gone_ref)):
            row = pl.multiple_of((2 * half + (sides_ref[0] ^ flip)) * share, share)
            ref[half] = acc_ref[pl.ds(row, share), :].astype(bf16)


def head_grads(fsdp, sides, hidden, grad_joined):
    total, width = hidden.shape
    columns = grad_joined.shape[2]
    vmem = pl.BlockSpec(memory_space=pltpu.VMEM)
    half = jax.ShapeDtypeStruct((fsdp // 2, width // fsdp, columns), bf16)
    return pl.pallas_call(
        head_grads_kernel,
        in_specs=[pl.BlockSpec(memory_space=pltpu.SMEM), vmem, vmem],
        out_specs=[vmem, vmem],
        out_shape=[half, half],
        scratch_shapes=[pltpu.VMEM((width, columns), f32)],
        compiler_params=pltpu.CompilerParams(vmem_limit_bytes=VMEM_BYTES),
        cost_estimate=pl.CostEstimate(
            flops=2 * total * width * columns,
            bytes_accessed=2 * total * (width + columns),
            transcendentals=0,
        ),
        name="head_grads",
    )(sides, hidden, grad_joined)


def add_halves_kernel(picks, joined, sides_ref, *refs):
    pairs = len(picks)
    outs = refs[2 * pairs :]
    begin = 0
    for i, pick in enumerate(picks):
        kept_ref, got_ref = refs[2 * i], refs[2 * i + 1]
        columns = kept_ref.shape[-1]
        for at in range(kept_ref.shape[0]):
            for flip in range(2):
                side = sides_ref[pick] ^ flip
                total = kept_ref[at, side].astype(f32) + got_ref[at, side].astype(f32)
                if joined:
                    outs[flip][at, :, begin : begin + columns] = total.astype(bf16)
                else:
                    outs[2 * i + flip][at] = total.astype(bf16)
        begin += columns


def add_halves(sides, pairs, joined=False):
    flat = []
    shapes = []
    for kept, got, axis, _ in pairs:
        shape = kept.shape
        shape = (
            math.prod(shape[:axis]), 2, math.prod(shape[axis + 1 : -1]), shape[-1]
        )
        flat += [kept.reshape(shape), got.reshape(shape)]
        shapes += [(shape[0], shape[2], shape[3])] * 2
    if joined:
        columns = sum(shape[2] for shape in shapes) // 2
        shapes = [shapes[0][:2] + (columns,)] * 2
    vmem = pl.BlockSpec(memory_space=pltpu.VMEM)
    size = sum(array.size for array in flat)
    return pl.pallas_call(
        functools.partial(add_halves_kernel, [pair[3] for pair in pairs], joined),
        in_specs=[pl.BlockSpec(memory_space=pltpu.SMEM)] + [vmem] * len(flat),
        out_specs=[vmem] * len(shapes),
        out_shape=[jax.ShapeDtypeStruct(shape, bf16) for shape in shapes],
        compiler_params=pltpu.CompilerParams(vmem_limit_bytes=VMEM_BYTES),
        cost_estimate=pl.CostEstimate(flops=size, bytes_accessed=3 * size, transcendentals=0),
        name="add_halves",
    )(sides, *flat)


def flips(count, bit):
    return [(i, i ^ bit) for i in range(count)]


def gate(*values):
    return lax.optimization_barrier(values)


def program(fsdp, ctx):
    def on_device(tokens, segment_ids, positions, gain_attn, w_qkv, w_out, gain_mlp, w_in, w_down,
                  cotangent):
        rows, width = tokens.shape[1:]
        shard = w_qkv.shape[0]
        share = ctx * shard
        heads = width // HD
        common = math.gcd(heads, ctx)
        splits = ctx // common
        units = heads // common
        part = rows // splits
        total = ctx * rows
        outer = ctx // 2
        first = [min(units * c // splits, heads - SLOTS) for c in range(ctx)]
        owners = [
            [
                (c, slot)
                for c in range(ctx)
                for slot in range(SLOTS)
                if first[c] + slot == head
                and max(units * c, head * splits) < min(units * (c + 1), (head + 1) * splits)
            ]
            for head in range(heads)
        ]
        me = lax.axis_index("ctx")
        mine = lax.axis_index("fsdp")
        sides = jnp.stack([mine % 2, mine // 2 % 2, me % 2, me // 2 % 2, me // 4 % 2])
        sides = sides.astype(jnp.int32)
        place = jnp.stack([mine, me // 2, 0 * me + outer, 0 * me + share]).astype(jnp.int32)
        swap = flips(ctx, 1)
        turn = lambda back: [
            (o * 2 + i, (o + back) % outer * 2 + i) for o in range(outer) for i in range(2)
        ]
        by_y = flips(fsdp, 2)
        by_core = flips(fsdp, 1)
        by_hand = (fsdp, ctx) == (4, 8) and shard % 8 == 0
        tile = KEY_TILE
        cot = cotangent[0]
        packed = jnp.concatenate([w_out, w_in, w_down.T], axis=1)
        columns = packed.shape[1]
        cut = (columns // LANES + 1) // 2 * LANES

        def weave(own, got):
            low = jnp.where(me % 2 == 0, own, got)
            high = jnp.where(me % 2 == 0, got, own)
            return jnp.concatenate([low, high], axis=1)

        def tables(sent):
            infos = sent[:, shard : shard + 2, :].astype(f32)
            docs = infos[:, 0, :rows].astype(jnp.int32)
            spots = (infos[:, 0, rows:] * 64 + infos[:, 1, :rows]).reshape(total, 1)
            half = jnp.arange(LANES) % (HD // 2)
            rates = THETA ** (-2.0 * half.astype(f32) / HD)
            angles = spots * rates[None, :]
            edges = docs.reshape(total // GRAIN, GRAIN)
            lo = jnp.sum((edges[None, :, -1] < docs[:, :1]).astype(jnp.int32), axis=1)
            hi = jnp.sum((edges[None, :, 0] <= docs[:, rows - 1 :]).astype(jnp.int32), axis=1)
            count = (hi - lo + tile // GRAIN - 1) // (tile // GRAIN)
            base = jnp.minimum(lo, total // GRAIN - count * (tile // GRAIN))
            unit = units * me + jnp.arange(units, dtype=jnp.int32)
            first_head = jnp.minimum(units * me // splits, heads - SLOTS)
            unit_places = jnp.concatenate([unit // splits - first_head, unit % splits])
            pick = (unit % splits)[:, None] == jnp.arange(splits, dtype=jnp.int32)[None, :]
            own_part = lambda array: jnp.sum(
                jnp.where(pick[None, :, :, None], array.reshape(ctx, 1, splits, part), 0), axis=2
            ).reshape(ctx, 1, units * part)
            doc_q = own_part(docs)
            spot_q = own_part(spots)
            ids = jnp.arange(IDS + 1, dtype=jnp.int32)
            before = jnp.sum((docs.reshape(1, total) < ids[:, None]).astype(jnp.int32), axis=1)
            is_id = doc_q == ids[None, :-1, None]
            bounds = [
                jnp.sum(jnp.where(is_id, edge[None, :, None], 0), axis=1, keepdims=True)
                for edge in (before[:-1], before[1:])
            ]
            return (
                jnp.cos(angles), jnp.sin(angles), base, count, unit_places.astype(jnp.int32),
                jnp.concatenate(bounds, axis=1), spot_q,
            )

        def query_tables(spot_q):
            half = jnp.arange(HD) % (HD // 2)
            angles = THETA ** (-2.0 * half.astype(f32) / HD)[None, :, None] * spot_q
            return jnp.cos(angles), jnp.sin(angles)

        sent = spread(first, w_qkv, gain_attn, gain_mlp, segment_ids, positions)
        sent = lax.all_to_all(sent, "ctx", 0, 0, tiled=True)
        masks = [0]
        if by_hand:
            own = [tokens[0]]
            near = [jnp.stack(
                [packed[:, :cut], jnp.pad(packed[:, cut:], ((0, 0), (0, 2 * cut - columns)))]
            )]
            own.append(lax.ppermute(own[0], "ctx", turn(1)))
            other = [lax.ppermute(own[0], "ctx", swap)]
            near.append(lax.ppermute(near[0], "ctx", turn(1)))
            own[1], other[0], near[1], sent = gate(own[1], other[0], near[1], sent)

        w_parts = sent[:, :shard, :].reshape(1, share, 4 * LANES)
        bit = fsdp // 2
        while bit:
            got = lax.ppermute(w_parts, "fsdp", flips(fsdp, bit))
            w_parts = jnp.concatenate([w_parts, got], axis=0)
            masks += [mask ^ bit for mask in masks]
            bit //= 2
        known = tables(sent)
        if by_hand:
            own.append(lax.ppermute(own[1], "ctx", turn(1)))
            other.append(lax.ppermute(own[1], "ctx", swap))
            near.append(lax.ppermute(near[1], "ctx", turn(1)))
            low_a = jnp.stack([near[0][0], near[1][0]])
            low_b = jnp.stack([near[0][1], near[1][1]])
            own[2], other[1], near[2], low_a, low_b, w_parts, known = gate(
                own[2], other[1], near[2], low_a, low_b, w_parts, known
            )
        cosine, sine, base, count, unit_places, ranges, spot_q = known

        w_heads, gains = ready(masks, mine.astype(jnp.int32).reshape(1), w_parts)

        def project_some(blocks, places, held):
            at = jnp.stack(places).astype(jnp.int32)
            return project(at, blocks, w_heads, gains, cosine, sine, total, held)

        def came_from(step, flip):
            return (me // 2 + outer - step) % outer * 2 + (me % 2 + flip) % 2

        if by_hand:
            own.append(lax.ppermute(own[2], "ctx", turn(1)))
            other.append(lax.ppermute(own[2], "ctx", swap))
            near.append(lax.ppermute(near[2], "ctx", turn(1)))
            next_a = lax.ppermute(low_a, "ctx", swap)
            next_b = lax.ppermute(low_b, "fsdp", by_y)
            held = []
            for step in range(2):
                held = project_some(
                    [own[step], other[step]], [came_from(step, 0), came_from(step, 1)], held
                )
            own[3], other[2], near[3], next_a, next_b, held, late = gate(
                own[3], other[2], near[3], next_a, next_b, held, w_qkv
            )

            other.append(lax.ppermute(own[3], "ctx", swap))
            high_a = jnp.stack([near[2][0], near[3][0]])
            high_b = jnp.stack([near[2][1], near[3][1]])
            past_a = lax.ppermute(high_a, "ctx", swap)
            past_b = lax.ppermute(high_b, "fsdp", by_y)
            held = project_some(
                [own[2], other[2], own[3]],
                [came_from(2, 0), came_from(2, 1), came_from(3, 0)], held,
            )
            ring_c = [late, lax.ppermute(late, "ctx", turn(1))]
            other[3], past_a, past_b, held, ring_c = gate(other[3], past_a, past_b, held, ring_c)
            ring_c = jnp.stack(ring_c)
            ring_c = [ring_c, lax.ppermute(ring_c, "ctx", turn(2))]

            pair_a = jnp.concatenate([weave(low_a, next_a), weave(high_a, past_a)])
            pair_b = jnp.concatenate([low_b, next_b, high_b, past_b])
            far_a = lax.ppermute(pair_a, "fsdp", by_y)
            far_b = lax.ppermute(pair_b, "ctx", swap)
            held = project_some([other[3]], [came_from(3, 1)], held)
        else:
            blocks = lax.all_gather(tokens[0], "ctx", axis=0, tiled=True)
            blocks = blocks.reshape(ctx, rows, width)
            held = []
            for c in range(0, ctx, 2):
                held = project_some(
                    [blocks[c], blocks[c + 1]], [jnp.int32(c), jnp.int32(c + 1)], held
                )
        hidden_one, qkv, turned = held
        att_low, att, lse = attend(
            base, count, unit_places, qkv, turned, ranges, rows, tile
        )
        if by_hand:
            att_low, far_a, far_b, ring_c, spot_q = gate(att_low, far_a, far_b, ring_c, spot_q)
            tables_q = query_tables(spot_q)
            pair_b = weave(pair_b, far_b)
            arrays = [pair_a, far_a, lax.ppermute(pair_a, "fsdp", by_core),
                      lax.ppermute(far_a, "fsdp", by_core),
                      pair_b, lax.ppermute(pair_b, "fsdp", by_core)]
            metas_a = [[(flip + 2 * far, back) for back in range(outer)]
                       for flip in range(2) for far in range(2)]
            metas_b = [[(flip + 2 * near, back) for near in (0, 1) for back in (0, 1)]
                       + [(flip + 2 * near, back) for near in (0, 1) for back in (2, 3)]
                       for flip in range(2)]
            att_in = lax.all_to_all(att_low, "ctx", 0, 0, tiled=True)
            pair_c = jnp.concatenate(ring_c)
            att_in, arrays, pair_c, tables_q = gate(att_in, arrays, pair_c, tables_q)
            near_c = lax.ppermute(pair_c, "ctx", swap)
        else:
            att_in = lax.all_to_all(att_low, "ctx", 0, 0, tiled=True)
            tables_q = query_tables(spot_q)
            every = lax.all_gather(packed, AXES, axis=0, tiled=True)
            arrays = [every[None, :, :cut], every[None, :, cut:]]
            metas_a = metas_b = [[(0, 0)]]
            place = jnp.stack([0 * me, 0 * me, 0 * me + 1, 0 * me]).astype(jnp.int32)
            w_joined = lax.all_gather(w_qkv, AXES, axis=0, tiled=True)
        parts_a = list(zip(arrays, metas_a))
        parts_b = list(zip(arrays[len(metas_a) :], metas_b))

        output, grad_heads, grad_middle, attended, grad_branch, hidden_two, grad_up, product = (
            middle_stage(
                heads, splits, place, att_in, tokens[0], gains, cot, parts_a, parts_b,
                w_down.shape[0],
            )
        )
        operands = [attended, grad_branch, hidden_two, grad_up, cot, product]
        if by_hand:
            grad_heads, operands, near_c = gate(grad_heads, operands, near_c)
            pair_c = weave(pair_c, near_c)
            far_c = lax.ppermute(pair_c, "fsdp", by_y)
        grad_heads = lax.all_to_all(grad_heads, "ctx", 0, 0, tiled=True)
        if by_hand:
            grad_cut = columns // LANES // 2 * LANES
            rest = columns - grad_cut
            gone_a, gone_b = weight_grads(
                gone_grads_kernel, sides, operands, [], [(2, share, grad_cut), (2, share, rest)],
                grad_cut, [], "gone_grads",
            )
            got_a = lax.ppermute(gone_a, "fsdp", by_core)
            got_b = lax.ppermute(gone_b, "fsdp", by_core)
            mine_a, other_a, mine_b, other_b = weight_grads(
                kept_grads_kernel, sides, operands, [got_a, got_b],
                [(share, grad_cut)] * 2 + [(2 * outer, shard, rest)] * 2, grad_cut,
                [
                    pltpu.VMEM((2, share, grad_cut), bf16),
                    pltpu.VMEM((2, share, rest), bf16),
                    pltpu.VMEM((2, share, grad_cut), bf16),
                    pltpu.VMEM((2, 2 * outer, shard, rest), bf16),
                    pltpu.SemaphoreType.DMA((4,)),
                ],
                "kept_grads",
            )
            grad_heads, mine_a, other_a, mine_b, other_b = gate(
                grad_heads, mine_a, other_a, mine_b, other_b
            )
            got_a = lax.ppermute(other_a, "fsdp", by_y)
            got_b = lax.ppermute(other_b, "ctx", swap)
        else:
            grad_packed = jnp.concatenate(
                [dot_rows(left, right) for left, right in zip(operands[::2], operands[1::2])],
                axis=1,
            ).astype(bf16)
            grad_packed = lax.psum_scatter(grad_packed, "fsdp", scatter_dimension=0, tiled=True)
            grad_packed = lax.psum_scatter(grad_packed, "ctx", scatter_dimension=0, tiled=True)
            grad_packed = grad_packed.astype(f32)

        grad_joined, grad_sent = attend_back(
            base, count, unit_places, qkv, turned, ranges, grad_heads, att, lse, tables_q,
            (cosine, sine), rows, tile,
        )
        if by_hand:
            grad_joined, grad_sent, mine_a, got_a, mine_b, got_b, pair_c, far_c = gate(
                grad_joined, grad_sent, mine_a, got_a, mine_b, got_b, pair_c, far_c
            )
            joined_in = lax.all_to_all(grad_sent, "ctx", 0, 0, tiled=True)
            arrays = [pair_c, far_c, lax.ppermute(pair_c, "fsdp", by_core),
                      lax.ppermute(far_c, "fsdp", by_core)]
            by_x = lambda array: array.reshape(outer, 2, shard, array.shape[-1])
            mine_a, other_a, mine_b, other_b = add_halves(
                sides,
                [(by_x(mine_a), by_x(got_a), 1, 2),
                 (mine_b.reshape(2, share // 2, rest), got_b.reshape(2, share // 2, rest), 0, 1)],
            )
            sides_late, other_a, other_b = gate(sides, other_a, other_b)
            got_a = lax.ppermute(other_a, "ctx", swap)
            got_b = lax.ppermute(other_b, "fsdp", by_y)
            kept_cols, gone_cols = head_grads(fsdp, sides_late, hidden_one, grad_joined)
            got_cols = lax.ppermute(gone_cols, "fsdp", by_core)
            mine_a, got_a, mine_b, got_b, kept_cols, got_cols, arrays = gate(
                mine_a, got_a, mine_b, got_b, kept_cols, got_cols, arrays
            )
            w_joined = settle(place, list(zip(arrays, metas_a)), width)
            pairs = lambda array: array.reshape(outer // 2, 2, shard, array.shape[-1])
            kept, gone = add_halves(
                sides,
                [(pairs(mine_a), pairs(got_a), 1, 3), (pairs(mine_b), pairs(got_b), 1, 3)],
                joined=True,
            )
            got = lax.ppermute(gone, "ctx", flips(ctx, 2))
            kept_cols, gone_cols = add_halves(sides, [(kept_cols, got_cols, 0, 1)])
            got_cols = lax.ppermute(gone_cols, "fsdp", by_y)
            joined_in, kept, got, kept_cols, got_cols, w_joined = gate(
                joined_in, kept, got, kept_cols, got_cols, w_joined
            )
            kept, gone = add_halves(sides, [(kept, got, 0, 4)])
            got = lax.ppermute(gone, "ctx", flips(ctx, 4))
            grad_packed = kept[0].astype(f32) + got[0].astype(f32)
            grad_cols = (kept_cols[0].astype(f32) + got_cols[0].astype(f32)).astype(bf16)
            grad_cols, _ = gate(grad_cols, gone)
        else:
            joined_in = lax.all_to_all(grad_sent, "ctx", 0, 0, tiled=True)
            grad_cols = dot_rows(hidden_one, grad_joined.reshape(total, 3 * LANES)).astype(bf16)
            grad_cols = lax.psum_scatter(grad_cols, "fsdp", scatter_dimension=0, tiled=True)
        input_grad = finish(owners, splits, joined_in, tokens[0], gains, grad_middle, w_joined)
        grad_cols = grad_cols.reshape(ctx, shard, 3 * LANES)
        grad_cols = lax.all_to_all(grad_cols, "ctx", 0, 0, tiled=True).astype(f32)

        sum_w_out = grad_packed[:, :width]
        sum_w_in = grad_packed[:, width : width + w_in.shape[1]]
        sum_w_down = grad_packed[:, width + w_in.shape[1] :].T
        sum_gain_mlp = jnp.sum(w_in.astype(f32) * sum_w_in, axis=1) / gain_mlp.astype(f32)
        pieces = []
        for third in range(3):
            for head in range(heads):
                column = 0.0
                for c, slot in owners[head]:
                    at = third * LANES + slot * HD
                    column = column + grad_cols[c, :, at : at + HD]
                pieces.append(column)
        sum_w_qkv = jnp.concatenate(pieces, axis=1)
        sum_gain_attn = jnp.sum(w_qkv.astype(f32) * sum_w_qkv, axis=1) / gain_attn.astype(f32)
        return (
            output[None],
            input_grad[None],
            sum_gain_attn,
            sum_w_qkv,
            sum_w_out,
            sum_gain_mlp,
            sum_w_in,
            sum_w_down,
        )

    return on_device


def solution(mesh):
    rows = P(AXES, None)
    tokens = P("fsdp", "ctx", None)
    return jax.shard_map(
        program(mesh.shape["fsdp"], mesh.shape["ctx"]),
        mesh=mesh,
        in_specs=(
            tokens,
            P("fsdp", "ctx"),
            P("fsdp", "ctx"),
            P(AXES),
            rows,
            rows,
            P(AXES),
            rows,
            P(None, AXES),
            tokens,
        ),
        out_specs=(tokens, tokens, P(AXES), rows, rows, P(AXES), rows, P(None, AXES)),
        check_vma=False,
    )
```

```python
import functools
import math

import jax
import jax.numpy as jnp
from jax import lax
from jax.experimental import pallas as pl
from jax.experimental.pallas import tpu as pltpu
from jax.sharding import PartitionSpec as P

HD = 64
SLOTS = 2
LANES = SLOTS * HD
UNITS = 3
IDS = 16
GRAIN = 128
KEY_TILE = 512
CHUNK = 384
EPS = 1e-05
THETA = 160000.0
NEG = -1e30
ROOT_HALF = 0.7071067811865476
INV_ROOT_TWO_PI = 0.3989422804014327
VMEM_BYTES = 58 * 1024 * 1024
AXES = ("fsdp", "ctx")

f32 = jnp.float32
bf16 = jnp.bfloat16


def norm_rows(values):
    center = values - jnp.mean(values, axis=-1, keepdims=True)
    spread = jnp.mean(center * center, axis=-1, keepdims=True)
    inverse = lax.rsqrt(spread + EPS)
    return (center * inverse, inverse)


def norm_back(grad_normed, normed, inverse):
    return inverse * (
        grad_normed
        - jnp.mean(grad_normed, axis=-1, keepdims=True)
        - normed * jnp.mean(grad_normed * normed, axis=-1, keepdims=True)
    )


def rotate_half(values):
    lane = lax.broadcasted_iota(jnp.int32, values.shape, 1)
    ahead = pltpu.roll(values, LANES - HD // 2, 1)
    behind = pltpu.roll(values, HD // 2, 1)
    return jnp.where(lane % HD < HD // 2, -ahead, behind)


def dot_tt(left, right):
    return lax.dot_general(left, right, (((1,), (1,)), ((), ())), preferred_element_type=f32)


def dot_rows(left, right):
    return lax.dot_general(left, right, (((0,), (0,)), ((), ())), preferred_element_type=f32)


def params():
    return pltpu.CompilerParams(
        dimension_semantics=("arbitrary",), vmem_limit_bytes=VMEM_BYTES
    )


def spread_kernel(first, *refs):
    sems, out_ref = refs[-1], refs[5]
    copies = [
        pltpu.make_async_copy(refs[i], refs[6 + i], sems.at[i]) for i in range(5)
    ]
    for copy in copies:
        copy.start()
    for copy in copies:
        copy.wait()
    w_ref, gain_one_ref, gain_two_ref, doc_ref, place_ref = refs[6:11]
    shard, columns = w_ref.shape
    width = columns // 3
    rows = doc_ref.shape[1]
    square = (shard, shard)
    eye = lax.broadcasted_iota(jnp.int32, square, 0) == lax.broadcasted_iota(jnp.int32, square, 1)

    def upright(ref):
        spread = jnp.where(eye, ref[...].astype(f32), 0.0)
        return jnp.sum(spread, axis=1, keepdims=True).astype(bf16)

    lane = lax.broadcasted_iota(jnp.int32, (shard, LANES), 1)
    gains = jnp.where(
        lane == 0, upright(gain_one_ref), jnp.where(lane == 1, upright(gain_two_ref), bf16(0))
    )
    place = place_ref[...]
    top = jnp.concatenate([doc_ref[...], place >> 6], axis=1).astype(f32)
    low = jnp.concatenate([place & 63, jnp.zeros_like(place)], axis=1).astype(f32)
    row = lax.broadcasted_iota(jnp.int32, (8, 2 * rows), 0)
    places = jnp.where(row == 0, top, jnp.where(row == 1, low, 0.0)).astype(bf16)
    for c, head in enumerate(first):
        for part in range(3):
            at = part * width + head * HD
            out_ref[c, :shard, part * LANES : (part + 1) * LANES] = w_ref[:, at : at + LANES]
        out_ref[c, :shard, 3 * LANES :] = gains
        out_ref[c, shard:, :] = places


def spread(first, w_qkv, gain_one, gain_two, docs, places):
    shard = w_qkv.shape[0]
    operands = (w_qkv, gain_one[None], gain_two[None], docs, places)
    return pl.pallas_call(
        functools.partial(spread_kernel, first),
        in_specs=[pl.BlockSpec(memory_space=pl.ANY)] * 5,
        out_specs=pl.BlockSpec(memory_space=pltpu.VMEM),
        out_shape=jax.ShapeDtypeStruct((len(first), shard + 8, 4 * LANES), bf16),
        scratch_shapes=[pltpu.VMEM(array.shape, array.dtype) for array in operands]
        + [pltpu.SemaphoreType.DMA((5,))],
        compiler_params=pltpu.CompilerParams(vmem_limit_bytes=VMEM_BYTES),
        name="spread",
    )(*operands)


def ready_kernel(masks, at_ref, w_ref, w_out_ref, gains_ref):
    share = w_ref.shape[1]
    for i, mask in enumerate(masks):
        start = pl.multiple_of((at_ref[0] ^ mask) * share, share)
        w_out_ref[pl.ds(start, share), :] = w_ref[i]
    gains_ref[...] = jnp.transpose(w_out_ref[:, 3 * LANES :].astype(f32))[:8]


def ready(masks, at, w_parts):
    count, share, columns = w_parts.shape
    vmem = pl.BlockSpec(memory_space=pltpu.VMEM)
    return pl.pallas_call(
        functools.partial(ready_kernel, masks),
        in_specs=[pl.BlockSpec(memory_space=pltpu.SMEM), vmem],
        out_specs=[vmem, vmem],
        out_shape=[
            jax.ShapeDtypeStruct((count * share, columns), bf16),
            jax.ShapeDtypeStruct((8, count * share), f32),
        ],
        compiler_params=pltpu.CompilerParams(vmem_limit_bytes=VMEM_BYTES),
        name="ready",
    )(at, w_parts)


def project_kernel(count, at_ref, *refs):
    x_refs = refs[:count]
    w_ref, gains_ref, cos_ref, sin_ref = refs[count : count + 4]
    hidden_ref, qkv_ref, turned_ref = refs[-3:]
    x = x_refs[0][...]
    for i in range(1, count):
        x = jnp.where(pl.program_id(0) == i, x_refs[i][...], x)
    x = x.astype(f32)
    normed, _ = norm_rows(x)
    hidden = (normed * gains_ref[:1, :]).astype(bf16)
    hidden_ref[...] = hidden
    joined = jnp.dot(hidden, w_ref[...], preferred_element_type=f32)
    cosine = cos_ref[...]
    sine = sin_ref[...]
    query = joined[:, :LANES]
    keys = joined[:, LANES : 2 * LANES]
    values = joined[:, 2 * LANES :]
    query = (query * cosine + rotate_half(query) * sine).astype(bf16)
    keys = keys * cosine + rotate_half(keys) * sine
    qkv_ref[:, :LANES] = query * bf16(HD**-0.5)
    qkv_ref[:, LANES : 2 * LANES] = keys.astype(bf16)
    qkv_ref[:, 2 * LANES :] = values.astype(bf16)
    turned_ref[:LANES, :] = jnp.transpose(keys).astype(bf16)
    turned_ref[LANES:, :] = jnp.transpose(values).astype(bf16)


def project(at, blocks, w_heads, gains, cosine, sine, total, held):
    rows, width = blocks[0].shape
    count = len(blocks)
    fixed = lambda *shape: pl.BlockSpec(shape, lambda i, at: (0,) * len(shape))
    tall = lambda width: pl.BlockSpec((rows, width), lambda i, at: (at[i], 0))
    shapes = [
        jax.ShapeDtypeStruct((total, width), bf16),
        jax.ShapeDtypeStruct((total, 3 * LANES), bf16),
        jax.ShapeDtypeStruct((2 * LANES, total), bf16),
    ]
    return pl.pallas_call(
        functools.partial(project_kernel, count),
        grid_spec=pltpu.PrefetchScalarGridSpec(
            num_scalar_prefetch=1,
            grid=(count,),
            in_specs=[fixed(rows, width)] * count
            + [fixed(width, 3 * LANES), fixed(8, width), tall(LANES), tall(LANES)]
            + [pl.BlockSpec(memory_space=pl.ANY) for _ in held],
            out_specs=[
                tall(width),
                tall(3 * LANES),
                pl.BlockSpec((2 * LANES, rows), lambda i, at: (0, at[i])),
            ],
        ),
        out_shape=shapes,
        input_output_aliases={count + 5 + i: i for i in range(len(held))},
        compiler_params=params(),
        cost_estimate=pl.CostEstimate(
            flops=2 * count * rows * width * 3 * LANES,
            bytes_accessed=3 * count << 20,
            transcendentals=0,
        ),
        name="project",
    )(at, *blocks, w_heads, gains, cosine, sine, *held)


def unit_rows(units_ref, ref, unit, first, part):
    lane = lax.broadcasted_iota(jnp.int32, (part, LANES), 1)
    start = pl.multiple_of(first + units_ref[UNITS + unit] * part, part)
    chunk = ref[pl.ds(start, part), :]
    return jnp.where(lane // HD == units_ref[unit], chunk, jnp.zeros_like(chunk))


def jobs(step, part):
    every = slice(0, UNITS * part)
    return [
        (2 * step + at, [(at, unit) for unit in range(UNITS)], [(at, every)]) for at in range(2)
    ]


def row_of(ref, row, where):
    return jnp.concatenate([ref[at, row : row + 1, columns] for at, columns in where], axis=1)


def slot_rows(units_ref, unit):
    return pl.ds(pl.multiple_of(units_ref[unit] * HD, HD), HD)


def pack(pieces):
    half = pieces[2].shape[1] // 2
    top = jnp.concatenate(pieces[:2], axis=0)
    low = jnp.concatenate([pieces[2][:, :half], pieces[2][:, half:]], axis=0)
    return jnp.concatenate([jnp.transpose(top), jnp.transpose(low)], axis=0).astype(bf16)


def unpack(packed, part):
    values = packed.astype(f32)
    top = jnp.transpose(values[:part])
    low = jnp.transpose(values[part:])
    return [top[:HD], top[HD:], jnp.concatenate([low[:HD], low[HD:]], axis=1)]


def fold(values, reduce):
    rows, wide = values.shape
    return reduce(values.reshape(rows // 8, 8, wide), axis=0)


def tile_span(first, at, tile):
    return pl.ds(pl.multiple_of(first + at * tile, GRAIN), tile)


def masked(scores, first, at, tile, low, high):
    key = lax.broadcasted_iota(jnp.int32, scores.shape, 0) + (first + at * tile)
    return jnp.where((key >= low) & (key < high), scores, NEG)


def attend_kernel(tile, base_ref, count_ref, units_ref, q_ref, k_ref, vt_ref, range_ref,
                  low_ref, att_ref, lse_ref, s_ref, acc_ref):
    wide = s_ref.shape[1]
    part = wide // UNITS
    rows = q_ref.shape[0] // 2
    pieces = {}
    for job, places, where in jobs(pl.program_id(0), part):
        queries = jnp.concatenate(
            [unit_rows(units_ref, q_ref, unit, at * rows, part) for at, unit in places], axis=0
        )
        low = row_of(range_ref, 0, where)
        high = row_of(range_ref, 1, where)
        first = base_ref[job] * GRAIN
        count = count_ref[job]

        def score(at, top):
            span = tile_span(first, at, tile)
            scores = masked(dot_tt(k_ref[span, :], queries), first, at, tile, low, high)
            s_ref[span, :] = scores
            return jnp.maximum(top, fold(scores, jnp.max))

        top = lax.fori_loop(0, count, score, jnp.full((8, wide), NEG, f32))
        top = jnp.max(top, axis=0, keepdims=True)

        def weigh(at, carry):
            total, accum = carry
            span = tile_span(first, at, tile)
            expo = jnp.exp(s_ref[span, :] - top)
            total = total + fold(expo, jnp.sum)
            accum = accum + jnp.dot(vt_ref[:, span], expo.astype(bf16), preferred_element_type=f32)
            return (total, accum)

        total, accum = lax.fori_loop(
            0, count, weigh, (jnp.zeros((8, wide), f32), jnp.zeros((LANES, wide), f32))
        )
        total = jnp.sum(total, axis=0, keepdims=True)
        log_sum = top + jnp.log(total)
        acc_ref[...] = accum / total
        for i, (at, unit) in enumerate(places):
            source = slice(i * part, (i + 1) * part)
            target = slice(unit * part, (unit + 1) * part)
            lse_ref[at, :, target] = log_sum[:, source]
            pieces[at, unit] = acc_ref[slot_rows(units_ref, unit), source]
            att_ref[at, :, target] = pieces[at, unit]
    for at in range(2):
        low_ref[at] = pack([pieces[at, unit] for unit in range(UNITS)])


def attend(base, tiles, unit_places, qkv, turned, ranges, rows, tile):
    total = qkv.shape[0]
    count = total // rows
    wide = ranges.shape[2]
    two = lambda *shape: pl.BlockSpec((2,) + shape, lambda i, *s: (i, 0, 0))
    return pl.pallas_call(
        functools.partial(attend_kernel, tile),
        grid_spec=pltpu.PrefetchScalarGridSpec(
            num_scalar_prefetch=3,
            grid=(count // 2,),
            in_specs=[
                pl.BlockSpec((2 * rows, LANES), lambda i, *s: (i, 0)),
                pl.BlockSpec((total, LANES), lambda i, *s: (0, 1)),
                pl.BlockSpec((LANES, total), lambda i, *s: (1, 0)),
                two(2, wide),
            ],
            out_specs=[two(wide // 2, LANES), two(HD, wide), two(1, wide)],
            scratch_shapes=[
                pltpu.VMEM((total, wide), f32),
                pltpu.VMEM((LANES, wide), f32),
            ],
        ),
        out_shape=[
            jax.ShapeDtypeStruct((count, wide // 2, LANES), bf16),
            jax.ShapeDtypeStruct((count, HD, wide), f32),
            jax.ShapeDtypeStruct((count, 1, wide), f32),
        ],
        compiler_params=params(),
        cost_estimate=pl.CostEstimate(
            flops=4 * count * wide * total * LANES,
            bytes_accessed=8 << 20,
            transcendentals=count * wide * total,
        ),
        name="attend",
    )(base, tiles, unit_places, qkv, qkv, turned, ranges)


def attend_back_kernel(tile, base_ref, count_ref, units_ref, q_ref, k_ref, v_ref, kt_ref, range_ref,
                       grad_ref, att_ref, lse_ref, cos_q_ref, sin_q_ref, cos_hbm, sin_hbm,
                       out_ref, send_ref, dk_ref, dv_ref, acc_ref, gt_ref, full_ref, cos_ref,
                       sin_ref, sems):
    step = pl.program_id(0)
    steps = pl.num_programs(0)
    rows = full_ref.shape[1]
    wide = acc_ref.shape[1]
    part = wide // UNITS
    packed = UNITS * part // 2
    tables = [
        pltpu.make_async_copy(cos_hbm, cos_ref, sems.at[0]),
        pltpu.make_async_copy(sin_hbm, sin_ref, sems.at[1]),
    ]

    @pl.when(step == 0)
    def _():
        for table in tables:
            table.start()
        dk_ref[...] = jnp.zeros(dk_ref.shape, f32)
        dv_ref[...] = jnp.zeros(dv_ref.shape, f32)
        full_ref[...] = jnp.zeros(full_ref.shape, f32)

    grads = [unpack(grad_ref[at], part) for at in range(2)]
    deltas = [
        jnp.sum(jnp.concatenate(grads[at], axis=1) * att_ref[at], axis=0, keepdims=True)
        for at in range(2)
    ]
    pieces = {}
    for job, places, where in jobs(step, part):
        queries = jnp.concatenate(
            [unit_rows(units_ref, q_ref, unit, at * rows, part) for at, unit in places], axis=0
        )
        low = row_of(range_ref, 0, where)
        high = row_of(range_ref, 1, where)
        log_sum = row_of(lse_ref, 0, where)
        delta = jnp.concatenate([deltas[at][:, columns] for at, columns in where], axis=1)
        first = base_ref[job] * GRAIN
        gt_ref[...] = jnp.zeros(gt_ref.shape, bf16)
        for i, (at, unit) in enumerate(places):
            columns = slice(i * part, (i + 1) * part)
            gt_ref[slot_rows(units_ref, unit), columns] = grads[at][unit].astype(bf16)

        def one_tile(at, grad_query):
            span = tile_span(first, at, tile)
            grads_t = gt_ref[...]
            scores = masked(dot_tt(k_ref[span, :], queries), first, at, tile, low, high)
            grad_probs = jnp.dot(v_ref[span, :], grads_t, preferred_element_type=f32)
            probs = jnp.exp(scores - log_sum)
            dv_ref[span, :] += dot_tt(probs.astype(bf16), grads_t)
            grad_scores = (probs * (grad_probs - delta)).astype(bf16)
            dk_ref[span, :] += jnp.dot(grad_scores, queries, preferred_element_type=f32)
            return grad_query + jnp.dot(kt_ref[:, span], grad_scores, preferred_element_type=f32)

        acc_ref[...] = lax.fori_loop(
            0, count_ref[job], one_tile, jnp.zeros((LANES, wide), f32)
        )
        for i, (at, unit) in enumerate(places):
            source = slice(i * part, (i + 1) * part)
            target = slice(unit * part, (unit + 1) * part)
            piece = acc_ref[slot_rows(units_ref, unit), source] * HD**-0.5
            turned = piece * sin_q_ref[at, :, target]
            turned = jnp.concatenate([-turned[HD // 2 :], turned[: HD // 2]], axis=0)
            pieces[at, unit] = piece * cos_q_ref[at, :, target] - turned
    for at in range(2):
        found = [pieces[at, unit] for unit in range(UNITS)]
        send_ref[2 * step + at, :packed, :] = pack(found)
        place_units(units_ref, full_ref, found, part)
        out_ref[2 * step + at, :, :LANES] = jnp.transpose(full_ref[...]).astype(bf16)

    @pl.when(step == steps - 1)
    def _():
        for table in tables:
            table.wait()

        def finish(at, carry):
            span = pl.ds(pl.multiple_of(at * rows, rows), rows)
            keys = dk_ref[span, :]
            keys = keys * cos_ref[span, :] - rotate_half(keys * sin_ref[span, :])
            keys = keys.astype(bf16)
            values = dv_ref[span, :].astype(bf16)
            out_ref[at, :, LANES : 2 * LANES] = keys
            out_ref[at, :, 2 * LANES :] = values
            send_ref[at, packed : packed + rows, :] = keys
            send_ref[at, packed + rows :, :] = values
            return carry

        lax.fori_loop(0, 2 * steps, finish, 0)


def place_units(units_ref, full_ref, pieces, part):
    rows = full_ref.shape[1]
    for split in range(rows // part):
        for unit, piece in enumerate(pieces):

            @pl.when(units_ref[UNITS + unit] == split)
            def _():
                columns = slice(split * part, (split + 1) * part)
                full_ref[slot_rows(units_ref, unit), columns] = piece


def attend_back(base, tiles, unit_places, qkv, turned, ranges, grads, att, lse, tables_q, tables,
                rows, tile):
    total = qkv.shape[0]
    count = total // rows
    wide = ranges.shape[2]
    whole = lambda part: pl.BlockSpec((total, LANES), lambda i, *s: (0, part))
    two = lambda *shape: pl.BlockSpec((2,) + shape, lambda i, *s: (i, 0, 0))
    kept = lambda *shape: pl.BlockSpec(shape, lambda i, *s: (0, 0, 0))
    outside = pl.BlockSpec(memory_space=pl.ANY)
    table = pltpu.VMEM((total, LANES), f32)
    return pl.pallas_call(
        functools.partial(attend_back_kernel, tile),
        grid_spec=pltpu.PrefetchScalarGridSpec(
            num_scalar_prefetch=3,
            grid=(count // 2,),
            in_specs=[
                pl.BlockSpec((2 * rows, LANES), lambda i, *s: (i, 0)),
                whole(1),
                whole(2),
                pl.BlockSpec((LANES, total), lambda i, *s: (0, 0)),
                two(2, wide),
                two(wide // 2, LANES),
                two(HD, wide),
                two(1, wide),
                two(HD, wide),
                two(HD, wide),
                outside,
                outside,
            ],
            out_specs=[
                kept(count, rows, 3 * LANES),
                kept(count, wide // 2 + 2 * rows, LANES),
            ],
            scratch_shapes=[
                table,
                table,
                pltpu.VMEM((LANES, wide), f32),
                pltpu.VMEM((LANES, wide), bf16),
                pltpu.VMEM((LANES, rows), f32),
                table,
                table,
                pltpu.SemaphoreType.DMA((2,)),
            ],
        ),
        out_shape=[
            jax.ShapeDtypeStruct((count, rows, 3 * LANES), bf16),
            jax.ShapeDtypeStruct((count, wide // 2 + 2 * rows, LANES), bf16),
        ],
        compiler_params=params(),
        cost_estimate=pl.CostEstimate(
            flops=10 * count * wide * total * LANES,
            bytes_accessed=12 << 20,
            transcendentals=count * wide * total,
        ),
        name="attend_back",
    )(base, tiles, unit_places, qkv, qkv, qkv, turned, ranges, grads, att, lse, *tables_q, *tables)


def lanes_of(slab, at, want):
    slab = slab.astype(f32)
    return slab if at == want else pltpu.roll(slab, HD, 1)


def beside(left, right):
    side = lax.broadcasted_iota(jnp.int32, left.shape, 1) // HD
    return jnp.where(side == 0, left, right).astype(bf16)


def join_packed(parts_ref, heads, splits, part):
    half = part // 2
    tiles = []
    for tile in range(heads // SLOTS):
        blocks = []
        for piece in range(splits):
            for low in range(2):
                sides = []
                for want in range(SLOTS):
                    c, unit = divmod((tile * SLOTS + want) * splits + piece, UNITS)
                    row, at = (low * half, unit) if unit < 2 else (part, low)
                    sides.append(lanes_of(parts_ref[c, row : row + half, :], at, want))
                blocks.append(beside(*sides))
        tiles.append(jnp.concatenate(blocks, axis=0))
    return jnp.concatenate(tiles, axis=1)


def split_packed(values, out_ref, splits, part):
    half = part // 2

    def slab(unit, low, want):
        head, piece = divmod(unit, splits)
        row = piece * part + low * half
        at = head // SLOTS * LANES
        return lanes_of(values[row : row + half, at : at + LANES], head % SLOTS, want)

    for c in range(out_ref.shape[0]):
        unit = UNITS * c
        for low in range(2):
            out_ref[c, low * half : (low + 1) * half, :] = beside(
                slab(unit, low, 0), slab(unit + 1, low, 1)
            )
        out_ref[c, part:, :] = beside(slab(unit + 2, 0, 0), slab(unit + 2, 1, 1))


def join_heads(parts_ref, at, rows, owners):
    side = lax.broadcasted_iota(jnp.int32, (rows, LANES), 1) // HD
    tiles = []
    for tile in range(len(owners) // SLOTS):
        column = jnp.zeros((rows, LANES), f32)
        for half in range(SLOTS):
            for c, slot in owners[tile * SLOTS + half]:
                slab = lanes_of(parts_ref[c, at : at + rows, :], slot, half)
                column = column + jnp.where(side == half, slab, 0.0)
        tiles.append(column.astype(bf16))
    return jnp.concatenate(tiles, axis=1)


def fetch_rows(place_ref, metas, refs, target_ref, at, sems, span=None):
    copies = []
    begin, end = span or (0, refs[0].shape[2])
    for ref, blocks in zip(refs, metas):
        for index, (flip, back) in enumerate(blocks):
            count = ref.shape[1]
            turn = lax.rem(place_ref[1] + place_ref[2] - back, place_ref[2])
            row = (place_ref[0] ^ flip) * place_ref[3] + turn * count
            row = pl.multiple_of(row, count) if count < target_ref.shape[0] else 0
            target = target_ref.at[pl.ds(row, count), pl.ds(at + begin, end - begin)]
            source = ref.at[index, :, pl.ds(begin, end - begin)]
            copies.append(pltpu.make_async_copy(source, target, sems.at[len(copies)]))
            copies[-1].start()
    return copies


def middle_kernel(heads, splits, metas, cut, place_ref, att_ref, tokens_ref, gain_ref, cot_ref,
                  *refs):
    count = len(metas[0]) + len(metas[1])
    sources = refs[:count]
    (output_ref, grad_heads_ref, grad_middle_ref, attended_ref, branch_ref, hidden_ref,
     grad_up_ref, product_ref, w_ref, sems_a, sems_b, sems_c) = refs[count:]
    width = tokens_ref.shape[1]
    units = product_ref.shape[1]
    fetch = functools.partial(fetch_rows, place_ref)
    copies_a = fetch(metas[0], sources[: len(metas[0])], w_ref, 0, sems_a, (0, width))
    copies_b = fetch(metas[0], sources[: len(metas[0])], w_ref, 0, sems_c, (width, cut))
    copies_b += fetch(metas[1], sources[len(metas[0]) :], w_ref, cut, sems_b)
    up = width
    down = width + 2 * units
    gain = gain_ref[1:2, :]
    cot = cot_ref[...]
    part = tokens_ref.shape[0] // splits
    attended = join_packed(att_ref, heads, splits, part)
    attended_ref[...] = attended
    for copy in copies_a:
        copy.wait()
    middle = tokens_ref[...].astype(f32) + jnp.dot(
        attended, w_ref[:, :width], preferred_element_type=f32
    )
    normed, inverse = norm_rows(middle)
    hidden = (normed * gain).astype(bf16)
    hidden_ref[...] = hidden
    for copy in copies_b:
        copy.wait()
    result = middle
    grad_hidden = jnp.zeros(middle.shape, f32)
    for at in range(0, units, CHUNK):
        one = slice(at, at + CHUNK)
        two = slice(units + at, units + at + CHUNK)
        w_one = w_ref[:, up + at : up + at + CHUNK]
        w_two = w_ref[:, up + units + at : up + units + at + CHUNK]
        w_down = w_ref[:, down + at : down + at + CHUNK]
        inner = jnp.dot(hidden, w_one, preferred_element_type=f32)
        gate = jnp.dot(hidden, w_two, preferred_element_type=f32)
        grad_product = jnp.dot(cot, w_down, preferred_element_type=f32)
        cdf = 0.5 * (1.0 + lax.erf(inner * ROOT_HALF))
        gelu_value = inner * cdf
        product = (gelu_value * gate).astype(bf16)
        product_ref[:, one] = product
        slope = cdf + inner * jnp.exp(-0.5 * inner * inner) * INV_ROOT_TWO_PI
        grad_inner = (grad_product * gate * slope).astype(bf16)
        grad_gate = (grad_product * gelu_value).astype(bf16)
        grad_up_ref[:, one] = grad_inner
        grad_up_ref[:, two] = grad_gate
        result = result + dot_tt(product, w_down)
        grad_hidden = grad_hidden + dot_tt(grad_inner, w_one)
        grad_hidden = grad_hidden + dot_tt(grad_gate, w_two)
    output_ref[...] = result.astype(bf16)
    grad_middle = cot.astype(f32) + norm_back(grad_hidden * gain, normed, inverse)
    grad_middle_ref[...] = grad_middle
    grad_branch = grad_middle.astype(bf16)
    branch_ref[...] = grad_branch
    grad_attended = dot_tt(grad_branch, w_ref[:, :width])
    split_packed(grad_attended, grad_heads_ref, splits, part)


def middle_stage(heads, splits, place, att_in, tokens, gains, cot, parts_a, parts_b, units):
    rows, width = tokens.shape
    arrays = [[array for array, _ in parts] for parts in (parts_a, parts_b)]
    metas = [[blocks for _, blocks in parts] for parts in (parts_a, parts_b)]
    vmem = pl.BlockSpec(memory_space=pltpu.VMEM)
    shape = jax.ShapeDtypeStruct
    return pl.pallas_call(
        functools.partial(middle_kernel, heads, splits, metas, arrays[0][0].shape[-1]),
        in_specs=[pl.BlockSpec(memory_space=pltpu.SMEM)]
        + [vmem] * 4
        + [pl.BlockSpec(memory_space=pl.ANY)] * (len(arrays[0]) + len(arrays[1])),
        out_specs=[vmem] * 8,
        out_shape=[
            shape((rows, width), bf16),
            shape(att_in.shape, bf16),
            shape((rows, width), f32),
            shape((rows, width), bf16),
            shape((rows, width), bf16),
            shape((rows, width), bf16),
            shape((rows, 2 * units), bf16),
            shape((rows, units), bf16),
        ],
        scratch_shapes=[pltpu.VMEM((width, 2 * arrays[0][0].shape[-1]), bf16)]
        + [
            pltpu.SemaphoreType.DMA((sum(len(b) for b in blocks),))
            for blocks in (metas[0], metas[1], metas[0])
        ],
        compiler_params=pltpu.CompilerParams(vmem_limit_bytes=VMEM_BYTES),
        cost_estimate=pl.CostEstimate(
            flops=6 * rows * width * (width + 3 * units),
            bytes_accessed=10 << 20,
            transcendentals=2 * rows * units,
        ),
        name="middle_stage",
    )(place, att_in, tokens, gains, cot, *arrays[0], *arrays[1])


def settle_kernel(metas, place_ref, *refs):
    out_ref, sems = refs[-2:]
    for copy in fetch_rows(place_ref, metas, refs[:-2], out_ref, 0, sems):
        copy.wait()


def settle(place, parts, width):
    arrays = [array for array, _ in parts]
    metas = [blocks for _, blocks in parts]
    anywhere = pl.BlockSpec(memory_space=pl.ANY)
    return pl.pallas_call(
        functools.partial(settle_kernel, metas),
        in_specs=[pl.BlockSpec(memory_space=pltpu.SMEM)] + [anywhere] * len(arrays),
        out_specs=pl.BlockSpec(memory_space=pltpu.VMEM),
        out_shape=jax.ShapeDtypeStruct((width, arrays[0].shape[-1]), bf16),
        scratch_shapes=[pltpu.SemaphoreType.DMA((sum(len(b) for b in metas),))],
        compiler_params=pltpu.CompilerParams(vmem_limit_bytes=VMEM_BYTES),
        cost_estimate=pl.CostEstimate(flops=0, bytes_accessed=8 << 20, transcendentals=0),
        name="settle",
    )(place, *arrays)


def finish_kernel(owners, splits, parts_ref, tokens_ref, gain_ref, grad_ref, w_ref, out_ref):
    rows = tokens_ref.shape[0]
    part = rows // splits
    packed = UNITS * part // 2
    joined = jnp.concatenate(
        [
            join_packed(parts_ref, len(owners), splits, part),
            join_heads(parts_ref, packed, rows, owners),
            join_heads(parts_ref, packed + rows, rows, owners),
        ],
        axis=1,
    )
    normed, inverse = norm_rows(tokens_ref[...].astype(f32))
    grad_hidden = dot_tt(joined, w_ref[...])
    back = norm_back(grad_hidden * gain_ref[:1, :], normed, inverse)
    out_ref[...] = (grad_ref[...] + back).astype(bf16)


def finish(owners, splits, joined, tokens, gains, grad_middle, w_joined):
    rows, width = tokens.shape
    vmem = pl.BlockSpec(memory_space=pltpu.VMEM)
    return pl.pallas_call(
        functools.partial(finish_kernel, owners, splits),
        in_specs=[vmem] * 5,
        out_specs=vmem,
        out_shape=jax.ShapeDtypeStruct((rows, width), bf16),
        compiler_params=pltpu.CompilerParams(vmem_limit_bytes=VMEM_BYTES),
        cost_estimate=pl.CostEstimate(
            flops=6 * rows * width * width, bytes_accessed=6 << 20, transcendentals=0
        ),
        name="finish",
    )(joined, tokens, gains, grad_middle, w_joined)


def half_rows(pairs, side, share, refs, lt_ref, emit):
    at = 0
    for pair in range(pairs):
        lt_ref[pair] = jnp.transpose(refs[2 * pair][...])
    for pair in range(pairs):
        right_ref = refs[2 * pair + 1]
        columns = right_ref.shape[1]
        for start in range(0, columns, CHUNK):
            right = right_ref[:, start : start + CHUNK]
            for half in range(lt_ref.shape[1] // share // 2):
                row = pl.multiple_of((2 * half + side) * share, share)
                emit(
                    half,
                    at + start,
                    jnp.dot(lt_ref[pair, pl.ds(row, share), :], right, preferred_element_type=f32),
                )
        at += columns


def pieces_of(cut, at, value):
    end = at + value.shape[1]
    found = []
    if at < cut:
        found.append((0, at, value[:, : min(end, cut) - at]))
    if end > cut:
        found.append((1, max(at, cut) - cut, value[:, max(at, cut) - at :]))
    return found


def gone_grads_kernel(pairs, cut, sides_ref, *refs):
    outs = refs[2 * pairs : 2 * pairs + 2]
    share = outs[0].shape[1]

    def emit(half, at, value):
        for which, start, piece in pieces_of(cut, at, value):
            span = slice(start, start + piece.shape[1])
            outs[which][half, :, span] = piece.astype(bf16)

    half_rows(pairs, 1 - sides_ref[0], share, refs, refs[-1], emit)


def kept_grads_kernel(pairs, cut, sides_ref, *refs):
    sources = refs[2 * pairs : 2 * pairs + 2]
    targets = refs[2 * pairs + 2 : 2 * pairs + 6]
    lt_ref, got_a, got_b, sum_a, sum_b, sems = refs[2 * pairs + 6 :]
    gots = (got_a, got_b)
    copies = [
        pltpu.make_async_copy(source, got, sems.at[i])
        for i, (source, got) in enumerate(zip(sources, gots))
    ]
    for copy in copies:
        copy.start()
    share = got_a.shape[1]
    shard = sum_b.shape[2]
    outer = share // shard // 2
    waits = list(copies)

    def emit(half, at, value):
        while waits:
            waits.pop().wait()
        for which, start, piece in pieces_of(cut, at, value):
            span = slice(start, start + piece.shape[1])
            total = piece + gots[which][half, :, span].astype(f32)
            if which == 0:
                sum_a[sides_ref[1] ^ half, :, span] = total.astype(bf16)
            else:
                for z in range(outer):
                    for x in range(2):
                        row = (z * 2 + x) * shard
                        block = total[row : row + shard].astype(bf16)
                        sum_b[sides_ref[2] ^ x, half * outer + z, :, span] = block

    half_rows(pairs, sides_ref[0], share, refs, lt_ref, emit)
    copies = []
    for i, total in enumerate((sum_a, sum_b)):
        for flip in range(2):
            copies.append(
                pltpu.make_async_copy(total.at[flip], targets[2 * i + flip], sems.at[2 * i + flip])
            )
            copies[-1].start()
    for copy in copies:
        copy.wait()


def weight_grads(kernel, sides, operands, gots, outs, cut, scratch, name):
    vmem = pl.BlockSpec(memory_space=pltpu.VMEM)
    outside = pl.BlockSpec(memory_space=pl.ANY)
    rows, width = operands[0].shape
    columns = sum(array.shape[1] for array in operands[1::2])
    return pl.pallas_call(
        functools.partial(kernel, len(operands) // 2, cut),
        in_specs=[pl.BlockSpec(memory_space=pltpu.SMEM)]
        + [vmem] * len(operands)
        + [outside] * len(gots),
        out_specs=[outside if gots else vmem] * len(outs),
        out_shape=[jax.ShapeDtypeStruct(shape, bf16) for shape in outs],
        scratch_shapes=[pltpu.VMEM((len(operands) // 2, width, rows), bf16)] + scratch,
        compiler_params=pltpu.CompilerParams(vmem_limit_bytes=VMEM_BYTES),
        cost_estimate=pl.CostEstimate(
            flops=rows * width * columns, bytes_accessed=3 * width * columns, transcendentals=0
        ),
        name=name,
    )(sides, *operands, *gots)


def head_grads_kernel(sides_ref, left_ref, right_ref, kept_ref, gone_ref, acc_ref):
    acc_ref[...] = jnp.zeros(acc_ref.shape, f32)
    count, rows, _ = right_ref.shape
    halves, share = kept_ref.shape[:2]

    def step(at, carry):
        span = pl.ds(pl.multiple_of(at * rows, rows), rows)
        left = jnp.transpose(left_ref[span, :])
        acc_ref[...] += jnp.dot(left, right_ref[at], preferred_element_type=f32)
        return carry

    lax.fori_loop(0, count, step, 0)
    for half in range(halves):
        for flip, ref in enumerate((kept_ref, gone_ref)):
            row = pl.multiple_of((2 * half + (sides_ref[0] ^ flip)) * share, share)
            ref[half] = acc_ref[pl.ds(row, share), :].astype(bf16)


def head_grads(fsdp, sides, hidden, grad_joined):
    total, width = hidden.shape
    columns = grad_joined.shape[2]
    vmem = pl.BlockSpec(memory_space=pltpu.VMEM)
    half = jax.ShapeDtypeStruct((fsdp // 2, width // fsdp, columns), bf16)
    return pl.pallas_call(
        head_grads_kernel,
        in_specs=[pl.BlockSpec(memory_space=pltpu.SMEM), vmem, vmem],
        out_specs=[vmem, vmem],
        out_shape=[half, half],
        scratch_shapes=[pltpu.VMEM((width, columns), f32)],
        compiler_params=pltpu.CompilerParams(vmem_limit_bytes=VMEM_BYTES),
        cost_estimate=pl.CostEstimate(
            flops=2 * total * width * columns,
            bytes_accessed=2 * total * (width + columns),
            transcendentals=0,
        ),
        name="head_grads",
    )(sides, hidden, grad_joined)


def add_halves_kernel(picks, joined, sides_ref, *refs):
    pairs = len(picks)
    outs = refs[2 * pairs :]
    begin = 0
    for i, pick in enumerate(picks):
        kept_ref, got_ref = refs[2 * i], refs[2 * i + 1]
        columns = kept_ref.shape[-1]
        for at in range(kept_ref.shape[0]):
            for flip in range(2):
                side = sides_ref[pick] ^ flip
                total = kept_ref[at, side].astype(f32) + got_ref[at, side].astype(f32)
                if joined:
                    outs[flip][at, :, begin : begin + columns] = total.astype(bf16)
                else:
                    outs[2 * i + flip][at] = total.astype(bf16)
        begin += columns


def add_halves(sides, pairs, joined=False):
    flat = []
    shapes = []
    for kept, got, axis, _ in pairs:
        shape = kept.shape
        shape = (
            math.prod(shape[:axis]), 2, math.prod(shape[axis + 1 : -1]), shape[-1]
        )
        flat += [kept.reshape(shape), got.reshape(shape)]
        shapes += [(shape[0], shape[2], shape[3])] * 2
    if joined:
        columns = sum(shape[2] for shape in shapes) // 2
        shapes = [shapes[0][:2] + (columns,)] * 2
    vmem = pl.BlockSpec(memory_space=pltpu.VMEM)
    size = sum(array.size for array in flat)
    return pl.pallas_call(
        functools.partial(add_halves_kernel, [pair[3] for pair in pairs], joined),
        in_specs=[pl.BlockSpec(memory_space=pltpu.SMEM)] + [vmem] * len(flat),
        out_specs=[vmem] * len(shapes),
        out_shape=[jax.ShapeDtypeStruct(shape, bf16) for shape in shapes],
        compiler_params=pltpu.CompilerParams(vmem_limit_bytes=VMEM_BYTES),
        cost_estimate=pl.CostEstimate(flops=size, bytes_accessed=3 * size, transcendentals=0),
        name="add_halves",
    )(sides, *flat)


def flips(count, bit):
    return [(i, i ^ bit) for i in range(count)]


def gate(*values):
    return lax.optimization_barrier(values)


def program(fsdp, ctx):
    def on_device(tokens, segment_ids, positions, gain_attn, w_qkv, w_out, gain_mlp, w_in, w_down,
                  cotangent):
        rows, width = tokens.shape[1:]
        shard = w_qkv.shape[0]
        share = ctx * shard
        heads = width // HD
        common = math.gcd(heads, ctx)
        splits = ctx // common
        units = heads // common
        part = rows // splits
        total = ctx * rows
        outer = ctx // 2
        first = [min(units * c // splits, heads - SLOTS) for c in range(ctx)]
        owners = [
            [
                (c, slot)
                for c in range(ctx)
                for slot in range(SLOTS)
                if first[c] + slot == head
                and max(units * c, head * splits) < min(units * (c + 1), (head + 1) * splits)
            ]
            for head in range(heads)
        ]
        me = lax.axis_index("ctx")
        mine = lax.axis_index("fsdp")
        sides = jnp.stack([mine % 2, mine // 2 % 2, me % 2, me // 2 % 2, me // 4 % 2])
        sides = sides.astype(jnp.int32)
        place = jnp.stack([mine, me // 2, 0 * me + outer, 0 * me + share]).astype(jnp.int32)
        swap = flips(ctx, 1)
        turn = lambda back: [
            (o * 2 + i, (o + back) % outer * 2 + i) for o in range(outer) for i in range(2)
        ]
        by_y = flips(fsdp, 2)
        by_core = flips(fsdp, 1)
        by_hand = (fsdp, ctx) == (4, 8) and shard % 8 == 0
        tile = KEY_TILE
        cot = cotangent[0]
        packed = jnp.concatenate([w_out, w_in, w_down.T], axis=1)
        columns = packed.shape[1]
        cut = (columns // LANES + 1) // 2 * LANES

        def weave(own, got):
            low = jnp.where(me % 2 == 0, own, got)
            high = jnp.where(me % 2 == 0, got, own)
            return jnp.concatenate([low, high], axis=1)

        def tables(sent):
            infos = sent[:, shard : shard + 2, :].astype(f32)
            docs = infos[:, 0, :rows].astype(jnp.int32)
            spots = (infos[:, 0, rows:] * 64 + infos[:, 1, :rows]).reshape(total, 1)
            half = jnp.arange(LANES) % (HD // 2)
            rates = THETA ** (-2.0 * half.astype(f32) / HD)
            angles = spots * rates[None, :]
            edges = docs.reshape(total // GRAIN, GRAIN)
            lo = jnp.sum((edges[None, :, -1] < docs[:, :1]).astype(jnp.int32), axis=1)
            hi = jnp.sum((edges[None, :, 0] <= docs[:, rows - 1 :]).astype(jnp.int32), axis=1)
            count = (hi - lo + tile // GRAIN - 1) // (tile // GRAIN)
            base = jnp.minimum(lo, total // GRAIN - count * (tile // GRAIN))
            unit = units * me + jnp.arange(units, dtype=jnp.int32)
            first_head = jnp.minimum(units * me // splits, heads - SLOTS)
            unit_places = jnp.concatenate([unit // splits - first_head, unit % splits])
            pick = (unit % splits)[:, None] == jnp.arange(splits, dtype=jnp.int32)[None, :]
            own_part = lambda array: jnp.sum(
                jnp.where(pick[None, :, :, None], array.reshape(ctx, 1, splits, part), 0), axis=2
            ).reshape(ctx, 1, units * part)
            doc_q = own_part(docs)
            spot_q = own_part(spots)
            ids = jnp.arange(IDS + 1, dtype=jnp.int32)
            before = jnp.sum((docs.reshape(1, total) < ids[:, None]).astype(jnp.int32), axis=1)
            is_id = doc_q == ids[None, :-1, None]
            bounds = [
                jnp.sum(jnp.where(is_id, edge[None, :, None], 0), axis=1, keepdims=True)
                for edge in (before[:-1], before[1:])
            ]
            return (
                jnp.cos(angles), jnp.sin(angles), base, count, unit_places.astype(jnp.int32),
                jnp.concatenate(bounds, axis=1), spot_q,
            )

        def query_tables(spot_q):
            half = jnp.arange(HD) % (HD // 2)
            angles = THETA ** (-2.0 * half.astype(f32) / HD)[None, :, None] * spot_q
            return jnp.cos(angles), jnp.sin(angles)

        sent = spread(first, w_qkv, gain_attn, gain_mlp, segment_ids, positions)
        sent = lax.all_to_all(sent, "ctx", 0, 0, tiled=True)
        masks = [0]
        if by_hand:
            own = [tokens[0]]
            near = [jnp.stack(
                [packed[:, :cut], jnp.pad(packed[:, cut:], ((0, 0), (0, 2 * cut - columns)))]
            )]
            own.append(lax.ppermute(own[0], "ctx", turn(1)))
            other = [lax.ppermute(own[0], "ctx", swap)]
            near.append(lax.ppermute(near[0], "ctx", turn(1)))
            own[1], other[0], near[1], sent = gate(own[1], other[0], near[1], sent)

        w_parts = sent[:, :shard, :].reshape(1, share, 4 * LANES)
        bit = fsdp // 2
        while bit:
            got = lax.ppermute(w_parts, "fsdp", flips(fsdp, bit))
            w_parts = jnp.concatenate([w_parts, got], axis=0)
            masks += [mask ^ bit for mask in masks]
            bit //= 2
        known = tables(sent)
        if by_hand:
            own.append(lax.ppermute(own[1], "ctx", turn(1)))
            other.append(lax.ppermute(own[1], "ctx", swap))
            near.append(lax.ppermute(near[1], "ctx", turn(1)))
            low_a = jnp.stack([near[0][0], near[1][0]])
            low_b = jnp.stack([near[0][1], near[1][1]])
            own[2], other[1], near[2], low_a, low_b, w_parts, known = gate(
                own[2], other[1], near[2], low_a, low_b, w_parts, known
            )
        cosine, sine, base, count, unit_places, ranges, spot_q = known

        w_heads, gains = ready(masks, mine.astype(jnp.int32).reshape(1), w_parts)

        def project_some(blocks, places, held):
            at = jnp.stack(places).astype(jnp.int32)
            return project(at, blocks, w_heads, gains, cosine, sine, total, held)

        def came_from(step, flip):
            return (me // 2 + outer - step) % outer * 2 + (me % 2 + flip) % 2

        if by_hand:
            own.append(lax.ppermute(own[2], "ctx", turn(1)))
            other.append(lax.ppermute(own[2], "ctx", swap))
            near.append(lax.ppermute(near[2], "ctx", turn(1)))
            next_a = lax.ppermute(low_a, "ctx", swap)
            next_b = lax.ppermute(low_b, "fsdp", by_y)
            held = []
            for step in range(2):
                held = project_some(
                    [own[step], other[step]], [came_from(step, 0), came_from(step, 1)], held
                )
            own[3], other[2], near[3], next_a, next_b, held, late = gate(
                own[3], other[2], near[3], next_a, next_b, held, w_qkv
            )

            other.append(lax.ppermute(own[3], "ctx", swap))
            high_a = jnp.stack([near[2][0], near[3][0]])
            high_b = jnp.stack([near[2][1], near[3][1]])
            past_a = lax.ppermute(high_a, "ctx", swap)
            past_b = lax.ppermute(high_b, "fsdp", by_y)
            held = project_some(
                [own[2], other[2], own[3]],
                [came_from(2, 0), came_from(2, 1), came_from(3, 0)], held,
            )
            ring_c = [late, lax.ppermute(late, "ctx", turn(1))]
            other[3], past_a, past_b, held, ring_c = gate(other[3], past_a, past_b, held, ring_c)
            ring_c = jnp.stack(ring_c)
            ring_c = [ring_c, lax.ppermute(ring_c, "ctx", turn(2))]

            pair_a = jnp.concatenate([weave(low_a, next_a), weave(high_a, past_a)])
            pair_b = jnp.concatenate([low_b, next_b, high_b, past_b])
            far_a = lax.ppermute(pair_a, "fsdp", by_y)
            far_b = lax.ppermute(pair_b, "ctx", swap)
            held = project_some([other[3]], [came_from(3, 1)], held)
        else:
            blocks = lax.all_gather(tokens[0], "ctx", axis=0, tiled=True)
            blocks = blocks.reshape(ctx, rows, width)
            held = []
            for c in range(0, ctx, 2):
                held = project_some(
                    [blocks[c], blocks[c + 1]], [jnp.int32(c), jnp.int32(c + 1)], held
                )
        hidden_one, qkv, turned = held
        att_low, att, lse = attend(
            base, count, unit_places, qkv, turned, ranges, rows, tile
        )
        if by_hand:
            att_low, far_a, far_b, ring_c, spot_q = gate(att_low, far_a, far_b, ring_c, spot_q)
            tables_q = query_tables(spot_q)
            pair_b = weave(pair_b, far_b)
            arrays = [pair_a, far_a, lax.ppermute(pair_a, "fsdp", by_core),
                      lax.ppermute(far_a, "fsdp", by_core),
                      pair_b, lax.ppermute(pair_b, "fsdp", by_core)]
            metas_a = [[(flip + 2 * far, back) for back in range(outer)]
                       for flip in range(2) for far in range(2)]
            metas_b = [[(flip + 2 * near, back) for near in (0, 1) for back in (0, 1)]
                       + [(flip + 2 * near, back) for near in (0, 1) for back in (2, 3)]
                       for flip in range(2)]
            att_in = lax.all_to_all(att_low, "ctx", 0, 0, tiled=True)
            pair_c = jnp.concatenate(ring_c)
            att_in, arrays, pair_c, tables_q = gate(att_in, arrays, pair_c, tables_q)
            near_c = lax.ppermute(pair_c, "ctx", swap)
        else:
            att_in = lax.all_to_all(att_low, "ctx", 0, 0, tiled=True)
            tables_q = query_tables(spot_q)
            every = lax.all_gather(packed, AXES, axis=0, tiled=True)
            arrays = [every[None, :, :cut], every[None, :, cut:]]
            metas_a = metas_b = [[(0, 0)]]
            place = jnp.stack([0 * me, 0 * me, 0 * me + 1, 0 * me]).astype(jnp.int32)
            w_joined = lax.all_gather(w_qkv, AXES, axis=0, tiled=True)
        parts_a = list(zip(arrays, metas_a))
        parts_b = list(zip(arrays[len(metas_a) :], metas_b))

        output, grad_heads, grad_middle, attended, grad_branch, hidden_two, grad_up, product = (
            middle_stage(
                heads, splits, place, att_in, tokens[0], gains, cot, parts_a, parts_b,
                w_down.shape[0],
            )
        )
        operands = [attended, grad_branch, hidden_two, grad_up, cot, product]
        if by_hand:
            grad_heads, operands, near_c = gate(grad_heads, operands, near_c)
            pair_c = weave(pair_c, near_c)
            far_c = lax.ppermute(pair_c, "fsdp", by_y)
        grad_heads = lax.all_to_all(grad_heads, "ctx", 0, 0, tiled=True)
        if by_hand:
            grad_cut = columns // LANES * 5 // 11 * LANES
            rest = columns - grad_cut
            gone_a, gone_b = weight_grads(
                gone_grads_kernel, sides, operands, [], [(2, share, grad_cut), (2, share, rest)],
                grad_cut, [], "gone_grads",
            )
            got_a = lax.ppermute(gone_a, "fsdp", by_core)
            got_b = lax.ppermute(gone_b, "fsdp", by_core)
            mine_a, other_a, mine_b, other_b = weight_grads(
                kept_grads_kernel, sides, operands, [got_a, got_b],
                [(share, grad_cut)] * 2 + [(2 * outer, shard, rest)] * 2, grad_cut,
                [
                    pltpu.VMEM((2, share, grad_cut), bf16),
                    pltpu.VMEM((2, share, rest), bf16),
                    pltpu.VMEM((2, share, grad_cut), bf16),
                    pltpu.VMEM((2, 2 * outer, shard, rest), bf16),
                    pltpu.SemaphoreType.DMA((4,)),
                ],
                "kept_grads",
            )
            grad_heads, mine_a, other_a, mine_b, other_b = gate(
                grad_heads, mine_a, other_a, mine_b, other_b
            )
            got_a = lax.ppermute(other_a, "fsdp", by_y)
            got_b = lax.ppermute(other_b, "ctx", swap)
        else:
            grad_packed = jnp.concatenate(
                [dot_rows(left, right) for left, right in zip(operands[::2], operands[1::2])],
                axis=1,
            ).astype(bf16)
            grad_packed = lax.psum_scatter(grad_packed, "fsdp", scatter_dimension=0, tiled=True)
            grad_packed = lax.psum_scatter(grad_packed, "ctx", scatter_dimension=0, tiled=True)
            grad_packed = grad_packed.astype(f32)

        grad_joined, grad_sent = attend_back(
            base, count, unit_places, qkv, turned, ranges, grad_heads, att, lse, tables_q,
            (cosine, sine), rows, tile,
        )
        if by_hand:
            grad_joined, grad_sent, mine_a, got_a, mine_b, got_b, pair_c, far_c = gate(
                grad_joined, grad_sent, mine_a, got_a, mine_b, got_b, pair_c, far_c
            )
            joined_in = lax.all_to_all(grad_sent, "ctx", 0, 0, tiled=True)
            arrays = [pair_c, far_c, lax.ppermute(pair_c, "fsdp", by_core),
                      lax.ppermute(far_c, "fsdp", by_core)]
            by_x = lambda array: array.reshape(outer, 2, shard, array.shape[-1])
            mine_a, other_a, mine_b, other_b = add_halves(
                sides,
                [(by_x(mine_a), by_x(got_a), 1, 2),
                 (mine_b.reshape(2, share // 2, rest), got_b.reshape(2, share // 2, rest), 0, 1)],
            )
            sides_late, other_a, other_b = gate(sides, other_a, other_b)
            got_a = lax.ppermute(other_a, "ctx", swap)
            got_b = lax.ppermute(other_b, "fsdp", by_y)
            kept_cols, gone_cols = head_grads(fsdp, sides_late, hidden_one, grad_joined)
            got_cols = lax.ppermute(gone_cols, "fsdp", by_core)
            mine_a, got_a, mine_b, got_b, kept_cols, got_cols, arrays = gate(
                mine_a, got_a, mine_b, got_b, kept_cols, got_cols, arrays
            )
            w_joined = settle(place, list(zip(arrays, metas_a)), width)
            pairs = lambda array: array.reshape(outer // 2, 2, shard, array.shape[-1])
            kept, gone = add_halves(
                sides,
                [(pairs(mine_a), pairs(got_a), 1, 3), (pairs(mine_b), pairs(got_b), 1, 3)],
                joined=True,
            )
            got = lax.ppermute(gone, "ctx", flips(ctx, 2))
            kept_cols, gone_cols = add_halves(sides, [(kept_cols, got_cols, 0, 1)])
            got_cols = lax.ppermute(gone_cols, "fsdp", by_y)
            joined_in, kept, got, kept_cols, got_cols, w_joined = gate(
                joined_in, kept, got, kept_cols, got_cols, w_joined
            )
            kept, gone = add_halves(sides, [(kept, got, 0, 4)])
            got = lax.ppermute(gone, "ctx", flips(ctx, 4))
            grad_packed = kept[0].astype(f32) + got[0].astype(f32)
            grad_cols = (kept_cols[0].astype(f32) + got_cols[0].astype(f32)).astype(bf16)
            grad_cols, _ = gate(grad_cols, gone)
        else:
            joined_in = lax.all_to_all(grad_sent, "ctx", 0, 0, tiled=True)
            grad_cols = dot_rows(hidden_one, grad_joined.reshape(total, 3 * LANES)).astype(bf16)
            grad_cols = lax.psum_scatter(grad_cols, "fsdp", scatter_dimension=0, tiled=True)
        input_grad = finish(owners, splits, joined_in, tokens[0], gains, grad_middle, w_joined)
        grad_cols = grad_cols.reshape(ctx, shard, 3 * LANES)
        grad_cols = lax.all_to_all(grad_cols, "ctx", 0, 0, tiled=True).astype(f32)

        sum_w_out = grad_packed[:, :width]
        sum_w_in = grad_packed[:, width : width + w_in.shape[1]]
        sum_w_down = grad_packed[:, width + w_in.shape[1] :].T
        sum_gain_mlp = jnp.sum(w_in.astype(f32) * sum_w_in, axis=1) / gain_mlp.astype(f32)
        pieces = []
        for third in range(3):
            for head in range(heads):
                column = 0.0
                for c, slot in owners[head]:
                    at = third * LANES + slot * HD
                    column = column + grad_cols[c, :, at : at + HD]
                pieces.append(column)
        sum_w_qkv = jnp.concatenate(pieces, axis=1)
        sum_gain_attn = jnp.sum(w_qkv.astype(f32) * sum_w_qkv, axis=1) / gain_attn.astype(f32)
        return (
            output[None],
            input_grad[None],
            sum_gain_attn,
            sum_w_qkv,
            sum_w_out,
            sum_gain_mlp,
            sum_w_in,
            sum_w_down,
        )

    return on_device


def solution(mesh):
    rows = P(AXES, None)
    tokens = P("fsdp", "ctx", None)
    return jax.shard_map(
        program(mesh.shape["fsdp"], mesh.shape["ctx"]),
        mesh=mesh,
        in_specs=(
            tokens,
            P("fsdp", "ctx"),
            P("fsdp", "ctx"),
            P(AXES),
            rows,
            rows,
            P(AXES),
            rows,
            P(None, AXES),
            tokens,
        ),
        out_specs=(tokens, tokens, P(AXES), rows, rows, P(AXES), rows, P(None, AXES)),
        check_vma=False,
    )
```

```python
import functools
import math

import jax
import jax.numpy as jnp
from jax import lax
from jax.experimental import pallas as pl
from jax.experimental.pallas import tpu as pltpu
from jax.sharding import PartitionSpec as P

HD = 64
SLOTS = 2
LANES = SLOTS * HD
UNITS = 3
IDS = 16
GRAIN = 128
KEY_TILE = 512
CHUNK = 384
MIDDLE_CHUNK = 1152
EPS = 1e-05
THETA = 160000.0
NEG = -1e30
ROOT_HALF = 0.7071067811865476
INV_ROOT_TWO_PI = 0.3989422804014327
VMEM_BYTES = 58 * 1024 * 1024
AXES = ("fsdp", "ctx")

f32 = jnp.float32
bf16 = jnp.bfloat16


def norm_rows(values):
    center = values - jnp.mean(values, axis=-1, keepdims=True)
    spread = jnp.mean(center * center, axis=-1, keepdims=True)
    inverse = lax.rsqrt(spread + EPS)
    return (center * inverse, inverse)


def norm_back(grad_normed, normed, inverse):
    return inverse * (
        grad_normed
        - jnp.mean(grad_normed, axis=-1, keepdims=True)
        - normed * jnp.mean(grad_normed * normed, axis=-1, keepdims=True)
    )


def rotate_half(values):
    lane = lax.broadcasted_iota(jnp.int32, values.shape, 1)
    ahead = pltpu.roll(values, LANES - HD // 2, 1)
    behind = pltpu.roll(values, HD // 2, 1)
    return jnp.where(lane % HD < HD // 2, -ahead, behind)


def dot_tt(left, right):
    return lax.dot_general(left, right, (((1,), (1,)), ((), ())), preferred_element_type=f32)


def dot_rows(left, right):
    return lax.dot_general(left, right, (((0,), (0,)), ((), ())), preferred_element_type=f32)


def params():
    return pltpu.CompilerParams(
        dimension_semantics=("arbitrary",), vmem_limit_bytes=VMEM_BYTES
    )


def spread_kernel(first, *refs):
    sems, out_ref = refs[-1], refs[5]
    copies = [
        pltpu.make_async_copy(refs[i], refs[6 + i], sems.at[i]) for i in range(5)
    ]
    for copy in copies:
        copy.start()
    for copy in copies:
        copy.wait()
    w_ref, gain_one_ref, gain_two_ref, doc_ref, place_ref = refs[6:11]
    shard, columns = w_ref.shape
    width = columns // 3
    rows = doc_ref.shape[1]
    square = (shard, shard)
    eye = lax.broadcasted_iota(jnp.int32, square, 0) == lax.broadcasted_iota(jnp.int32, square, 1)

    def upright(ref):
        spread = jnp.where(eye, ref[...].astype(f32), 0.0)
        return jnp.sum(spread, axis=1, keepdims=True).astype(bf16)

    lane = lax.broadcasted_iota(jnp.int32, (shard, LANES), 1)
    gains = jnp.where(
        lane == 0, upright(gain_one_ref), jnp.where(lane == 1, upright(gain_two_ref), bf16(0))
    )
    place = place_ref[...]
    top = jnp.concatenate([doc_ref[...], place >> 6], axis=1).astype(f32)
    low = jnp.concatenate([place & 63, jnp.zeros_like(place)], axis=1).astype(f32)
    row = lax.broadcasted_iota(jnp.int32, (8, 2 * rows), 0)
    places = jnp.where(row == 0, top, jnp.where(row == 1, low, 0.0)).astype(bf16)
    for c, head in enumerate(first):
        for part in range(3):
            at = part * width + head * HD
            out_ref[c, :shard, part * LANES : (part + 1) * LANES] = w_ref[:, at : at + LANES]
        out_ref[c, :shard, 3 * LANES :] = gains
        out_ref[c, shard:, :] = places


def spread(first, w_qkv, gain_one, gain_two, docs, places):
    shard = w_qkv.shape[0]
    operands = (w_qkv, gain_one[None], gain_two[None], docs, places)
    return pl.pallas_call(
        functools.partial(spread_kernel, first),
        in_specs=[pl.BlockSpec(memory_space=pl.ANY)] * 5,
        out_specs=pl.BlockSpec(memory_space=pltpu.VMEM),
        out_shape=jax.ShapeDtypeStruct((len(first), shard + 8, 4 * LANES), bf16),
        scratch_shapes=[pltpu.VMEM(array.shape, array.dtype) for array in operands]
        + [pltpu.SemaphoreType.DMA((5,))],
        compiler_params=pltpu.CompilerParams(vmem_limit_bytes=VMEM_BYTES),
        name="spread",
    )(*operands)


def ready_kernel(masks, at_ref, w_ref, w_out_ref, gains_ref):
    share = w_ref.shape[1]
    for i, mask in enumerate(masks):
        start = pl.multiple_of((at_ref[0] ^ mask) * share, share)
        w_out_ref[pl.ds(start, share), :] = w_ref[i]
    gains_ref[...] = jnp.transpose(w_out_ref[:, 3 * LANES :].astype(f32))[:8]


def ready(masks, at, w_parts):
    count, share, columns = w_parts.shape
    vmem = pl.BlockSpec(memory_space=pltpu.VMEM)
    return pl.pallas_call(
        functools.partial(ready_kernel, masks),
        in_specs=[pl.BlockSpec(memory_space=pltpu.SMEM), vmem],
        out_specs=[vmem, vmem],
        out_shape=[
            jax.ShapeDtypeStruct((count * share, columns), bf16),
            jax.ShapeDtypeStruct((8, count * share), f32),
        ],
        compiler_params=pltpu.CompilerParams(vmem_limit_bytes=VMEM_BYTES),
        name="ready",
    )(at, w_parts)


def project_kernel(count, at_ref, *refs):
    x_refs = refs[:count]
    w_ref, gains_ref, cos_ref, sin_ref = refs[count : count + 4]
    hidden_ref, qkv_ref, turned_ref = refs[-3:]
    x = x_refs[0][...]
    for i in range(1, count):
        x = jnp.where(pl.program_id(0) == i, x_refs[i][...], x)
    x = x.astype(f32)
    normed, _ = norm_rows(x)
    hidden = (normed * gains_ref[:1, :]).astype(bf16)
    hidden_ref[...] = hidden
    joined = jnp.dot(hidden, w_ref[...], preferred_element_type=f32)
    cosine = cos_ref[...]
    sine = sin_ref[...]
    query = joined[:, :LANES]
    keys = joined[:, LANES : 2 * LANES]
    values = joined[:, 2 * LANES :]
    query = (query * cosine + rotate_half(query) * sine).astype(bf16)
    keys = keys * cosine + rotate_half(keys) * sine
    qkv_ref[:, :LANES] = query * bf16(HD**-0.5)
    qkv_ref[:, LANES : 2 * LANES] = keys.astype(bf16)
    qkv_ref[:, 2 * LANES :] = values.astype(bf16)
    turned_ref[:LANES, :] = jnp.transpose(keys).astype(bf16)
    turned_ref[LANES:, :] = jnp.transpose(values).astype(bf16)


def project(at, blocks, w_heads, gains, cosine, sine, total, held):
    rows, width = blocks[0].shape
    count = len(blocks)
    fixed = lambda *shape: pl.BlockSpec(shape, lambda i, at: (0,) * len(shape))
    tall = lambda width: pl.BlockSpec((rows, width), lambda i, at: (at[i], 0))
    shapes = [
        jax.ShapeDtypeStruct((total, width), bf16),
        jax.ShapeDtypeStruct((total, 3 * LANES), bf16),
        jax.ShapeDtypeStruct((2 * LANES, total), bf16),
    ]
    return pl.pallas_call(
        functools.partial(project_kernel, count),
        grid_spec=pltpu.PrefetchScalarGridSpec(
            num_scalar_prefetch=1,
            grid=(count,),
            in_specs=[fixed(rows, width)] * count
            + [fixed(width, 3 * LANES), fixed(8, width), tall(LANES), tall(LANES)]
            + [pl.BlockSpec(memory_space=pl.ANY) for _ in held],
            out_specs=[
                tall(width),
                tall(3 * LANES),
                pl.BlockSpec((2 * LANES, rows), lambda i, at: (0, at[i])),
            ],
        ),
        out_shape=shapes,
        input_output_aliases={count + 5 + i: i for i in range(len(held))},
        compiler_params=params(),
        cost_estimate=pl.CostEstimate(
            flops=2 * count * rows * width * 3 * LANES,
            bytes_accessed=3 * count << 20,
            transcendentals=0,
        ),
        name="project",
    )(at, *blocks, w_heads, gains, cosine, sine, *held)


def unit_rows(units_ref, ref, unit, first, part):
    lane = lax.broadcasted_iota(jnp.int32, (part, LANES), 1)
    start = pl.multiple_of(first + units_ref[UNITS + unit] * part, part)
    chunk = ref[pl.ds(start, part), :]
    return jnp.where(lane // HD == units_ref[unit], chunk, jnp.zeros_like(chunk))


def jobs(step, part):
    every = slice(0, UNITS * part)
    return [
        (2 * step + at, [(at, unit) for unit in range(UNITS)], [(at, every)]) for at in range(2)
    ]


def row_of(ref, row, where):
    return jnp.concatenate([ref[at, row : row + 1, columns] for at, columns in where], axis=1)


def slot_rows(units_ref, unit):
    return pl.ds(pl.multiple_of(units_ref[unit] * HD, HD), HD)


def pack(pieces):
    half = pieces[2].shape[1] // 2
    top = jnp.concatenate(pieces[:2], axis=0)
    low = jnp.concatenate([pieces[2][:, :half], pieces[2][:, half:]], axis=0)
    return jnp.concatenate([jnp.transpose(top), jnp.transpose(low)], axis=0).astype(bf16)


def unpack(packed, part):
    values = packed.astype(f32)
    top = jnp.transpose(values[:part])
    low = jnp.transpose(values[part:])
    return [top[:HD], top[HD:], jnp.concatenate([low[:HD], low[HD:]], axis=1)]


def fold(values, reduce):
    rows, wide = values.shape
    return reduce(values.reshape(rows // 8, 8, wide), axis=0)


def tile_span(first, at, tile):
    return pl.ds(pl.multiple_of(first + at * tile, GRAIN), tile)


def masked(scores, first, at, tile, low, high):
    key = lax.broadcasted_iota(jnp.int32, scores.shape, 0) + (first + at * tile)
    return jnp.where((key >= low) & (key < high), scores, NEG)


def attend_kernel(tile, base_ref, count_ref, units_ref, q_ref, k_ref, vt_ref, range_ref,
                  low_ref, att_ref, lse_ref, s_ref, acc_ref):
    wide = s_ref.shape[1]
    part = wide // UNITS
    rows = q_ref.shape[0] // 2
    pieces = {}
    for job, places, where in jobs(pl.program_id(0), part):
        queries = jnp.concatenate(
            [unit_rows(units_ref, q_ref, unit, at * rows, part) for at, unit in places], axis=0
        )
        low = row_of(range_ref, 0, where)
        high = row_of(range_ref, 1, where)
        first = base_ref[job] * GRAIN
        count = count_ref[job]

        def score(at, top):
            span = tile_span(first, at, tile)
            scores = masked(dot_tt(k_ref[span, :], queries), first, at, tile, low, high)
            s_ref[span, :] = scores
            return jnp.maximum(top, fold(scores, jnp.max))

        top = lax.fori_loop(0, count, score, jnp.full((8, wide), NEG, f32))
        top = jnp.max(top, axis=0, keepdims=True)

        def weigh(at, carry):
            total, accum = carry
            span = tile_span(first, at, tile)
            expo = jnp.exp(s_ref[span, :] - top)
            total = total + fold(expo, jnp.sum)
            accum = accum + jnp.dot(vt_ref[:, span], expo.astype(bf16), preferred_element_type=f32)
            return (total, accum)

        total, accum = lax.fori_loop(
            0, count, weigh, (jnp.zeros((8, wide), f32), jnp.zeros((LANES, wide), f32))
        )
        total = jnp.sum(total, axis=0, keepdims=True)
        log_sum = top + jnp.log(total)
        acc_ref[...] = accum / total
        for i, (at, unit) in enumerate(places):
            source = slice(i * part, (i + 1) * part)
            target = slice(unit * part, (unit + 1) * part)
            lse_ref[at, :, target] = log_sum[:, source]
            pieces[at, unit] = acc_ref[slot_rows(units_ref, unit), source]
            att_ref[at, :, target] = pieces[at, unit]
    for at in range(2):
        low_ref[at] = pack([pieces[at, unit] for unit in range(UNITS)])


def attend(base, tiles, unit_places, qkv, turned, ranges, rows, tile):
    total = qkv.shape[0]
    count = total // rows
    wide = ranges.shape[2]
    two = lambda *shape: pl.BlockSpec((2,) + shape, lambda i, *s: (i, 0, 0))
    return pl.pallas_call(
        functools.partial(attend_kernel, tile),
        grid_spec=pltpu.PrefetchScalarGridSpec(
            num_scalar_prefetch=3,
            grid=(count // 2,),
            in_specs=[
                pl.BlockSpec((2 * rows, LANES), lambda i, *s: (i, 0)),
                pl.BlockSpec((total, LANES), lambda i, *s: (0, 1)),
                pl.BlockSpec((LANES, total), lambda i, *s: (1, 0)),
                two(2, wide),
            ],
            out_specs=[two(wide // 2, LANES), two(HD, wide), two(1, wide)],
            scratch_shapes=[
                pltpu.VMEM((total, wide), f32),
                pltpu.VMEM((LANES, wide), f32),
            ],
        ),
        out_shape=[
            jax.ShapeDtypeStruct((count, wide // 2, LANES), bf16),
            jax.ShapeDtypeStruct((count, HD, wide), f32),
            jax.ShapeDtypeStruct((count, 1, wide), f32),
        ],
        compiler_params=params(),
        cost_estimate=pl.CostEstimate(
            flops=4 * count * wide * total * LANES,
            bytes_accessed=8 << 20,
            transcendentals=count * wide * total,
        ),
        name="attend",
    )(base, tiles, unit_places, qkv, qkv, turned, ranges)


def attend_back_kernel(tile, base_ref, count_ref, units_ref, q_ref, k_ref, v_ref, kt_ref, range_ref,
                       grad_ref, att_ref, lse_ref, cos_q_ref, sin_q_ref, cos_hbm, sin_hbm,
                       out_ref, send_ref, dk_ref, dv_ref, acc_ref, gt_ref, full_ref, cos_ref,
                       sin_ref, sems):
    step = pl.program_id(0)
    steps = pl.num_programs(0)
    rows = full_ref.shape[1]
    wide = acc_ref.shape[1]
    part = wide // UNITS
    packed = UNITS * part // 2
    tables = [
        pltpu.make_async_copy(cos_hbm, cos_ref, sems.at[0]),
        pltpu.make_async_copy(sin_hbm, sin_ref, sems.at[1]),
    ]

    @pl.when(step == 0)
    def _():
        for table in tables:
            table.start()
        dk_ref[...] = jnp.zeros(dk_ref.shape, f32)
        dv_ref[...] = jnp.zeros(dv_ref.shape, f32)
        full_ref[...] = jnp.zeros(full_ref.shape, f32)

    grads = [unpack(grad_ref[at], part) for at in range(2)]
    deltas = [
        jnp.sum(jnp.concatenate(grads[at], axis=1) * att_ref[at], axis=0, keepdims=True)
        for at in range(2)
    ]
    pieces = {}
    for job, places, where in jobs(step, part):
        queries = jnp.concatenate(
            [unit_rows(units_ref, q_ref, unit, at * rows, part) for at, unit in places], axis=0
        )
        low = row_of(range_ref, 0, where)
        high = row_of(range_ref, 1, where)
        log_sum = row_of(lse_ref, 0, where)
        delta = jnp.concatenate([deltas[at][:, columns] for at, columns in where], axis=1)
        first = base_ref[job] * GRAIN
        gt_ref[...] = jnp.zeros(gt_ref.shape, bf16)
        for i, (at, unit) in enumerate(places):
            columns = slice(i * part, (i + 1) * part)
            gt_ref[slot_rows(units_ref, unit), columns] = grads[at][unit].astype(bf16)

        def one_tile(at, grad_query):
            span = tile_span(first, at, tile)
            grads_t = gt_ref[...]
            scores = masked(dot_tt(k_ref[span, :], queries), first, at, tile, low, high)
            grad_probs = jnp.dot(v_ref[span, :], grads_t, preferred_element_type=f32)
            probs = jnp.exp(scores - log_sum)
            dv_ref[span, :] += dot_tt(probs.astype(bf16), grads_t)
            grad_scores = (probs * (grad_probs - delta)).astype(bf16)
            dk_ref[span, :] += jnp.dot(grad_scores, queries, preferred_element_type=f32)
            return grad_query + jnp.dot(kt_ref[:, span], grad_scores, preferred_element_type=f32)

        acc_ref[...] = lax.fori_loop(
            0, count_ref[job], one_tile, jnp.zeros((LANES, wide), f32)
        )
        for i, (at, unit) in enumerate(places):
            source = slice(i * part, (i + 1) * part)
            target = slice(unit * part, (unit + 1) * part)
            piece = acc_ref[slot_rows(units_ref, unit), source] * HD**-0.5
            turned = piece * sin_q_ref[at, :, target]
            turned = jnp.concatenate([-turned[HD // 2 :], turned[: HD // 2]], axis=0)
            pieces[at, unit] = piece * cos_q_ref[at, :, target] - turned
    for at in range(2):
        found = [pieces[at, unit] for unit in range(UNITS)]
        send_ref[2 * step + at, :packed, :] = pack(found)
        place_units(units_ref, full_ref, found, part)
        out_ref[2 * step + at, :, :LANES] = jnp.transpose(full_ref[...]).astype(bf16)

    @pl.when(step == steps - 1)
    def _():
        for table in tables:
            table.wait()

        def finish(at, carry):
            span = pl.ds(pl.multiple_of(at * rows, rows), rows)
            keys = dk_ref[span, :]
            keys = keys * cos_ref[span, :] - rotate_half(keys * sin_ref[span, :])
            keys = keys.astype(bf16)
            values = dv_ref[span, :].astype(bf16)
            out_ref[at, :, LANES : 2 * LANES] = keys
            out_ref[at, :, 2 * LANES :] = values
            send_ref[at, packed : packed + rows, :] = keys
            send_ref[at, packed + rows :, :] = values
            return carry

        lax.fori_loop(0, 2 * steps, finish, 0)


def place_units(units_ref, full_ref, pieces, part):
    rows = full_ref.shape[1]
    for split in range(rows // part):
        for unit, piece in enumerate(pieces):

            @pl.when(units_ref[UNITS + unit] == split)
            def _():
                columns = slice(split * part, (split + 1) * part)
                full_ref[slot_rows(units_ref, unit), columns] = piece


def attend_back(base, tiles, unit_places, qkv, turned, ranges, grads, att, lse, tables_q, tables,
                rows, tile):
    total = qkv.shape[0]
    count = total // rows
    wide = ranges.shape[2]
    whole = lambda part: pl.BlockSpec((total, LANES), lambda i, *s: (0, part))
    two = lambda *shape: pl.BlockSpec((2,) + shape, lambda i, *s: (i, 0, 0))
    kept = lambda *shape: pl.BlockSpec(shape, lambda i, *s: (0, 0, 0))
    outside = pl.BlockSpec(memory_space=pl.ANY)
    table = pltpu.VMEM((total, LANES), f32)
    return pl.pallas_call(
        functools.partial(attend_back_kernel, tile),
        grid_spec=pltpu.PrefetchScalarGridSpec(
            num_scalar_prefetch=3,
            grid=(count // 2,),
            in_specs=[
                pl.BlockSpec((2 * rows, LANES), lambda i, *s: (i, 0)),
                whole(1),
                whole(2),
                pl.BlockSpec((LANES, total), lambda i, *s: (0, 0)),
                two(2, wide),
                two(wide // 2, LANES),
                two(HD, wide),
                two(1, wide),
                two(HD, wide),
                two(HD, wide),
                outside,
                outside,
            ],
            out_specs=[
                kept(count, rows, 3 * LANES),
                kept(count, wide // 2 + 2 * rows, LANES),
            ],
            scratch_shapes=[
                table,
                table,
                pltpu.VMEM((LANES, wide), f32),
                pltpu.VMEM((LANES, wide), bf16),
                pltpu.VMEM((LANES, rows), f32),
                table,
                table,
                pltpu.SemaphoreType.DMA((2,)),
            ],
        ),
        out_shape=[
            jax.ShapeDtypeStruct((count, rows, 3 * LANES), bf16),
            jax.ShapeDtypeStruct((count, wide // 2 + 2 * rows, LANES), bf16),
        ],
        compiler_params=params(),
        cost_estimate=pl.CostEstimate(
            flops=10 * count * wide * total * LANES,
            bytes_accessed=12 << 20,
            transcendentals=count * wide * total,
        ),
        name="attend_back",
    )(base, tiles, unit_places, qkv, qkv, qkv, turned, ranges, grads, att, lse, *tables_q, *tables)


def lanes_of(slab, at, want):
    slab = slab.astype(f32)
    return slab if at == want else pltpu.roll(slab, HD, 1)


def beside(left, right):
    side = lax.broadcasted_iota(jnp.int32, left.shape, 1) // HD
    return jnp.where(side == 0, left, right).astype(bf16)


def join_packed(parts_ref, heads, splits, part):
    half = part // 2
    tiles = []
    for tile in range(heads // SLOTS):
        blocks = []
        for piece in range(splits):
            for low in range(2):
                sides = []
                for want in range(SLOTS):
                    c, unit = divmod((tile * SLOTS + want) * splits + piece, UNITS)
                    row, at = (low * half, unit) if unit < 2 else (part, low)
                    sides.append(lanes_of(parts_ref[c, row : row + half, :], at, want))
                blocks.append(beside(*sides))
        tiles.append(jnp.concatenate(blocks, axis=0))
    return jnp.concatenate(tiles, axis=1)


def split_packed(values, out_ref, splits, part):
    half = part // 2

    def slab(unit, low, want):
        head, piece = divmod(unit, splits)
        row = piece * part + low * half
        at = head // SLOTS * LANES
        return lanes_of(values[row : row + half, at : at + LANES], head % SLOTS, want)

    for c in range(out_ref.shape[0]):
        unit = UNITS * c
        for low in range(2):
            out_ref[c, low * half : (low + 1) * half, :] = beside(
                slab(unit, low, 0), slab(unit + 1, low, 1)
            )
        out_ref[c, part:, :] = beside(slab(unit + 2, 0, 0), slab(unit + 2, 1, 1))


def join_heads(parts_ref, at, rows, owners):
    side = lax.broadcasted_iota(jnp.int32, (rows, LANES), 1) // HD
    tiles = []
    for tile in range(len(owners) // SLOTS):
        column = jnp.zeros((rows, LANES), f32)
        for half in range(SLOTS):
            for c, slot in owners[tile * SLOTS + half]:
                slab = lanes_of(parts_ref[c, at : at + rows, :], slot, half)
                column = column + jnp.where(side == half, slab, 0.0)
        tiles.append(column.astype(bf16))
    return jnp.concatenate(tiles, axis=1)


def fetch_rows(place_ref, metas, refs, target_ref, at, sems, span=None):
    copies = []
    begin, end = span or (0, refs[0].shape[2])
    for ref, blocks in zip(refs, metas):
        for index, (flip, back) in enumerate(blocks):
            count = ref.shape[1]
            turn = lax.rem(place_ref[1] + place_ref[2] - back, place_ref[2])
            row = (place_ref[0] ^ flip) * place_ref[3] + turn * count
            row = pl.multiple_of(row, count) if count < target_ref.shape[0] else 0
            target = target_ref.at[pl.ds(row, count), pl.ds(at + begin, end - begin)]
            source = ref.at[index, :, pl.ds(begin, end - begin)]
            copies.append(pltpu.make_async_copy(source, target, sems.at[len(copies)]))
            copies[-1].start()
    return copies


def middle_kernel(heads, splits, metas, cut, place_ref, att_ref, tokens_ref, gain_ref, cot_ref,
                  *refs):
    count = len(metas[0]) + len(metas[1])
    sources = refs[:count]
    (output_ref, grad_heads_ref, grad_middle_ref, attended_ref, branch_ref, hidden_ref,
     grad_up_ref, product_ref, w_ref, sems_a, sems_b, sems_c) = refs[count:]
    width = tokens_ref.shape[1]
    units = product_ref.shape[1]
    fetch = functools.partial(fetch_rows, place_ref)
    copies_a = fetch(metas[0], sources[: len(metas[0])], w_ref, 0, sems_a, (0, width))
    copies_b = fetch(metas[0], sources[: len(metas[0])], w_ref, 0, sems_c, (width, cut))
    copies_b += fetch(metas[1], sources[len(metas[0]) :], w_ref, cut, sems_b)
    up = width
    down = width + 2 * units
    gain = gain_ref[1:2, :]
    cot = cot_ref[...]
    part = tokens_ref.shape[0] // splits
    attended = join_packed(att_ref, heads, splits, part)
    attended_ref[...] = attended
    for copy in copies_a:
        copy.wait()
    middle = tokens_ref[...].astype(f32) + jnp.dot(
        attended, w_ref[:, :width], preferred_element_type=f32
    )
    normed, inverse = norm_rows(middle)
    hidden = (normed * gain).astype(bf16)
    hidden_ref[...] = hidden
    for copy in copies_b:
        copy.wait()
    result = middle
    grad_hidden = jnp.zeros(middle.shape, f32)
    for at in range(0, units, MIDDLE_CHUNK):
        one = slice(at, at + MIDDLE_CHUNK)
        two = slice(units + at, units + at + MIDDLE_CHUNK)
        w_one = w_ref[:, up + at : up + at + MIDDLE_CHUNK]
        w_two = w_ref[:, up + units + at : up + units + at + MIDDLE_CHUNK]
        w_down = w_ref[:, down + at : down + at + MIDDLE_CHUNK]
        inner = jnp.dot(hidden, w_one, preferred_element_type=f32)
        gate = jnp.dot(hidden, w_two, preferred_element_type=f32)
        grad_product = jnp.dot(cot, w_down, preferred_element_type=f32)
        cdf = 0.5 * (1.0 + lax.erf(inner * ROOT_HALF))
        gelu_value = inner * cdf
        product = (gelu_value * gate).astype(bf16)
        product_ref[:, one] = product
        slope = cdf + inner * jnp.exp(-0.5 * inner * inner) * INV_ROOT_TWO_PI
        grad_inner = (grad_product * gate * slope).astype(bf16)
        grad_gate = (grad_product * gelu_value).astype(bf16)
        grad_up_ref[:, one] = grad_inner
        grad_up_ref[:, two] = grad_gate
        result = result + dot_tt(product, w_down)
        grad_hidden = grad_hidden + dot_tt(grad_inner, w_one)
        grad_hidden = grad_hidden + dot_tt(grad_gate, w_two)
    output_ref[...] = result.astype(bf16)
    grad_middle = cot.astype(f32) + norm_back(grad_hidden * gain, normed, inverse)
    grad_middle_ref[...] = grad_middle
    grad_branch = grad_middle.astype(bf16)
    branch_ref[...] = grad_branch
    grad_attended = dot_tt(grad_branch, w_ref[:, :width])
    split_packed(grad_attended, grad_heads_ref, splits, part)


def middle_stage(heads, splits, place, att_in, tokens, gains, cot, parts_a, parts_b, units):
    rows, width = tokens.shape
    arrays = [[array for array, _ in parts] for parts in (parts_a, parts_b)]
    metas = [[blocks for _, blocks in parts] for parts in (parts_a, parts_b)]
    vmem = pl.BlockSpec(memory_space=pltpu.VMEM)
    shape = jax.ShapeDtypeStruct
    return pl.pallas_call(
        functools.partial(middle_kernel, heads, splits, metas, arrays[0][0].shape[-1]),
        in_specs=[pl.BlockSpec(memory_space=pltpu.SMEM)]
        + [vmem] * 4
        + [pl.BlockSpec(memory_space=pl.ANY)] * (len(arrays[0]) + len(arrays[1])),
        out_specs=[vmem] * 8,
        out_shape=[
            shape((rows, width), bf16),
            shape(att_in.shape, bf16),
            shape((rows, width), f32),
            shape((rows, width), bf16),
            shape((rows, width), bf16),
            shape((rows, width), bf16),
            shape((rows, 2 * units), bf16),
            shape((rows, units), bf16),
        ],
        scratch_shapes=[pltpu.VMEM((width, 2 * arrays[0][0].shape[-1]), bf16)]
        + [
            pltpu.SemaphoreType.DMA((sum(len(b) for b in blocks),))
            for blocks in (metas[0], metas[1], metas[0])
        ],
        compiler_params=pltpu.CompilerParams(vmem_limit_bytes=VMEM_BYTES),
        cost_estimate=pl.CostEstimate(
            flops=6 * rows * width * (width + 3 * units),
            bytes_accessed=10 << 20,
            transcendentals=2 * rows * units,
        ),
        name="middle_stage",
    )(place, att_in, tokens, gains, cot, *arrays[0], *arrays[1])


def settle_kernel(metas, place_ref, *refs):
    out_ref, sems = refs[-2:]
    for copy in fetch_rows(place_ref, metas, refs[:-2], out_ref, 0, sems):
        copy.wait()


def settle(place, parts, width):
    arrays = [array for array, _ in parts]
    metas = [blocks for _, blocks in parts]
    anywhere = pl.BlockSpec(memory_space=pl.ANY)
    return pl.pallas_call(
        functools.partial(settle_kernel, metas),
        in_specs=[pl.BlockSpec(memory_space=pltpu.SMEM)] + [anywhere] * len(arrays),
        out_specs=pl.BlockSpec(memory_space=pltpu.VMEM),
        out_shape=jax.ShapeDtypeStruct((width, arrays[0].shape[-1]), bf16),
        scratch_shapes=[pltpu.SemaphoreType.DMA((sum(len(b) for b in metas),))],
        compiler_params=pltpu.CompilerParams(vmem_limit_bytes=VMEM_BYTES),
        cost_estimate=pl.CostEstimate(flops=0, bytes_accessed=8 << 20, transcendentals=0),
        name="settle",
    )(place, *arrays)


def finish_kernel(owners, splits, parts_ref, tokens_ref, gain_ref, grad_ref, w_ref, out_ref):
    rows = tokens_ref.shape[0]
    part = rows // splits
    packed = UNITS * part // 2
    joined = jnp.concatenate(
        [
            join_packed(parts_ref, len(owners), splits, part),
            join_heads(parts_ref, packed, rows, owners),
            join_heads(parts_ref, packed + rows, rows, owners),
        ],
        axis=1,
    )
    normed, inverse = norm_rows(tokens_ref[...].astype(f32))
    grad_hidden = dot_tt(joined, w_ref[...])
    back = norm_back(grad_hidden * gain_ref[:1, :], normed, inverse)
    out_ref[...] = (grad_ref[...] + back).astype(bf16)


def finish(owners, splits, joined, tokens, gains, grad_middle, w_joined):
    rows, width = tokens.shape
    vmem = pl.BlockSpec(memory_space=pltpu.VMEM)
    return pl.pallas_call(
        functools.partial(finish_kernel, owners, splits),
        in_specs=[vmem] * 5,
        out_specs=vmem,
        out_shape=jax.ShapeDtypeStruct((rows, width), bf16),
        compiler_params=pltpu.CompilerParams(vmem_limit_bytes=VMEM_BYTES),
        cost_estimate=pl.CostEstimate(
            flops=6 * rows * width * width, bytes_accessed=6 << 20, transcendentals=0
        ),
        name="finish",
    )(joined, tokens, gains, grad_middle, w_joined)


def half_rows(pairs, side, share, refs, lt_ref, emit):
    at = 0
    for pair in range(pairs):
        lt_ref[pair] = jnp.transpose(refs[2 * pair][...])
    for pair in range(pairs):
        right_ref = refs[2 * pair + 1]
        columns = right_ref.shape[1]
        for start in range(0, columns, CHUNK):
            right = right_ref[:, start : start + CHUNK]
            for half in range(lt_ref.shape[1] // share // 2):
                row = pl.multiple_of((2 * half + side) * share, share)
                emit(
                    half,
                    at + start,
                    jnp.dot(lt_ref[pair, pl.ds(row, share), :], right, preferred_element_type=f32),
                )
        at += columns


def pieces_of(cut, at, value):
    end = at + value.shape[1]
    found = []
    if at < cut:
        found.append((0, at, value[:, : min(end, cut) - at]))
    if end > cut:
        found.append((1, max(at, cut) - cut, value[:, max(at, cut) - at :]))
    return found


def gone_grads_kernel(pairs, cut, sides_ref, *refs):
    outs = refs[2 * pairs : 2 * pairs + 2]
    share = outs[0].shape[1]

    def emit(half, at, value):
        for which, start, piece in pieces_of(cut, at, value):
            span = slice(start, start + piece.shape[1])
            outs[which][half, :, span] = piece.astype(bf16)

    half_rows(pairs, 1 - sides_ref[0], share, refs, refs[-1], emit)


def kept_grads_kernel(pairs, cut, sides_ref, *refs):
    sources = refs[2 * pairs : 2 * pairs + 2]
    targets = refs[2 * pairs + 2 : 2 * pairs + 6]
    lt_ref, got_a, got_b, sum_a, sum_b, sems = refs[2 * pairs + 6 :]
    gots = (got_a, got_b)
    copies = [
        pltpu.make_async_copy(source, got, sems.at[i])
        for i, (source, got) in enumerate(zip(sources, gots))
    ]
    for copy in copies:
        copy.start()
    share = got_a.shape[1]
    shard = sum_b.shape[2]
    outer = share // shard // 2
    waits = list(copies)

    def emit(half, at, value):
        while waits:
            waits.pop().wait()
        for which, start, piece in pieces_of(cut, at, value):
            span = slice(start, start + piece.shape[1])
            total = piece + gots[which][half, :, span].astype(f32)
            if which == 0:
                sum_a[sides_ref[1] ^ half, :, span] = total.astype(bf16)
            else:
                for z in range(outer):
                    for x in range(2):
                        row = (z * 2 + x) * shard
                        block = total[row : row + shard].astype(bf16)
                        sum_b[sides_ref[2] ^ x, half * outer + z, :, span] = block

    half_rows(pairs, sides_ref[0], share, refs, lt_ref, emit)
    copies = []
    for i, total in enumerate((sum_a, sum_b)):
        for flip in range(2):
            copies.append(
                pltpu.make_async_copy(total.at[flip], targets[2 * i + flip], sems.at[2 * i + flip])
            )
            copies[-1].start()
    for copy in copies:
        copy.wait()


def weight_grads(kernel, sides, operands, gots, outs, cut, scratch, name):
    vmem = pl.BlockSpec(memory_space=pltpu.VMEM)
    outside = pl.BlockSpec(memory_space=pl.ANY)
    rows, width = operands[0].shape
    columns = sum(array.shape[1] for array in operands[1::2])
    return pl.pallas_call(
        functools.partial(kernel, len(operands) // 2, cut),
        in_specs=[pl.BlockSpec(memory_space=pltpu.SMEM)]
        + [vmem] * len(operands)
        + [outside] * len(gots),
        out_specs=[outside if gots else vmem] * len(outs),
        out_shape=[jax.ShapeDtypeStruct(shape, bf16) for shape in outs],
        scratch_shapes=[pltpu.VMEM((len(operands) // 2, width, rows), bf16)] + scratch,
        compiler_params=pltpu.CompilerParams(vmem_limit_bytes=VMEM_BYTES),
        cost_estimate=pl.CostEstimate(
            flops=rows * width * columns, bytes_accessed=3 * width * columns, transcendentals=0
        ),
        name=name,
    )(sides, *operands, *gots)


def head_grads_kernel(sides_ref, left_ref, right_ref, kept_ref, gone_ref, acc_ref):
    acc_ref[...] = jnp.zeros(acc_ref.shape, f32)
    count, rows, _ = right_ref.shape
    halves, share = kept_ref.shape[:2]

    def step(at, carry):
        span = pl.ds(pl.multiple_of(at * rows, rows), rows)
        left = jnp.transpose(left_ref[span, :])
        acc_ref[...] += jnp.dot(left, right_ref[at], preferred_element_type=f32)
        return carry

    lax.fori_loop(0, count, step, 0)
    for half in range(halves):
        for flip, ref in enumerate((kept_ref, gone_ref)):
            row = pl.multiple_of((2 * half + (sides_ref[0] ^ flip)) * share, share)
            ref[half] = acc_ref[pl.ds(row, share), :].astype(bf16)


def head_grads(fsdp, sides, hidden, grad_joined):
    total, width = hidden.shape
    columns = grad_joined.shape[2]
    vmem = pl.BlockSpec(memory_space=pltpu.VMEM)
    half = jax.ShapeDtypeStruct((fsdp // 2, width // fsdp, columns), bf16)
    return pl.pallas_call(
        head_grads_kernel,
        in_specs=[pl.BlockSpec(memory_space=pltpu.SMEM), vmem, vmem],
        out_specs=[vmem, vmem],
        out_shape=[half, half],
        scratch_shapes=[pltpu.VMEM((width, columns), f32)],
        compiler_params=pltpu.CompilerParams(vmem_limit_bytes=VMEM_BYTES),
        cost_estimate=pl.CostEstimate(
            flops=2 * total * width * columns,
            bytes_accessed=2 * total * (width + columns),
            transcendentals=0,
        ),
        name="head_grads",
    )(sides, hidden, grad_joined)


def add_halves_kernel(picks, joined, sides_ref, *refs):
    pairs = len(picks)
    outs = refs[2 * pairs :]
    begin = 0
    for i, pick in enumerate(picks):
        kept_ref, got_ref = refs[2 * i], refs[2 * i + 1]
        columns = kept_ref.shape[-1]
        for at in range(kept_ref.shape[0]):
            for flip in range(2):
                side = sides_ref[pick] ^ flip
                total = kept_ref[at, side].astype(f32) + got_ref[at, side].astype(f32)
                if joined:
                    outs[flip][at, :, begin : begin + columns] = total.astype(bf16)
                else:
                    outs[2 * i + flip][at] = total.astype(bf16)
        begin += columns


def add_halves(sides, pairs, joined=False):
    flat = []
    shapes = []
    for kept, got, axis, _ in pairs:
        shape = kept.shape
        shape = (
            math.prod(shape[:axis]), 2, math.prod(shape[axis + 1 : -1]), shape[-1]
        )
        flat += [kept.reshape(shape), got.reshape(shape)]
        shapes += [(shape[0], shape[2], shape[3])] * 2
    if joined:
        columns = sum(shape[2] for shape in shapes) // 2
        shapes = [shapes[0][:2] + (columns,)] * 2
    vmem = pl.BlockSpec(memory_space=pltpu.VMEM)
    size = sum(array.size for array in flat)
    return pl.pallas_call(
        functools.partial(add_halves_kernel, [pair[3] for pair in pairs], joined),
        in_specs=[pl.BlockSpec(memory_space=pltpu.SMEM)] + [vmem] * len(flat),
        out_specs=[vmem] * len(shapes),
        out_shape=[jax.ShapeDtypeStruct(shape, bf16) for shape in shapes],
        compiler_params=pltpu.CompilerParams(vmem_limit_bytes=VMEM_BYTES),
        cost_estimate=pl.CostEstimate(flops=size, bytes_accessed=3 * size, transcendentals=0),
        name="add_halves",
    )(sides, *flat)


def flips(count, bit):
    return [(i, i ^ bit) for i in range(count)]


def gate(*values):
    return lax.optimization_barrier(values)


def program(fsdp, ctx):
    def on_device(tokens, segment_ids, positions, gain_attn, w_qkv, w_out, gain_mlp, w_in, w_down,
                  cotangent):
        rows, width = tokens.shape[1:]
        shard = w_qkv.shape[0]
        share = ctx * shard
        heads = width // HD
        common = math.gcd(heads, ctx)
        splits = ctx // common
        units = heads // common
        part = rows // splits
        total = ctx * rows
        outer = ctx // 2
        first = [min(units * c // splits, heads - SLOTS) for c in range(ctx)]
        owners = [
            [
                (c, slot)
                for c in range(ctx)
                for slot in range(SLOTS)
                if first[c] + slot == head
                and max(units * c, head * splits) < min(units * (c + 1), (head + 1) * splits)
            ]
            for head in range(heads)
        ]
        me = lax.axis_index("ctx")
        mine = lax.axis_index("fsdp")
        sides = jnp.stack([mine % 2, mine // 2 % 2, me % 2, me // 2 % 2, me // 4 % 2])
        sides = sides.astype(jnp.int32)
        place = jnp.stack([mine, me // 2, 0 * me + outer, 0 * me + share]).astype(jnp.int32)
        swap = flips(ctx, 1)
        turn = lambda back: [
            (o * 2 + i, (o + back) % outer * 2 + i) for o in range(outer) for i in range(2)
        ]
        by_y = flips(fsdp, 2)
        by_core = flips(fsdp, 1)
        by_hand = (fsdp, ctx) == (4, 8) and shard % 8 == 0
        tile = KEY_TILE
        cot = cotangent[0]
        packed = jnp.concatenate([w_out, w_in, w_down.T], axis=1)
        columns = packed.shape[1]
        cut = (columns // LANES + 1) // 2 * LANES

        def weave(own, got):
            low = jnp.where(me % 2 == 0, own, got)
            high = jnp.where(me % 2 == 0, got, own)
            return jnp.concatenate([low, high], axis=1)

        def tables(sent):
            infos = sent[:, shard : shard + 2, :].astype(f32)
            docs = infos[:, 0, :rows].astype(jnp.int32)
            spots = (infos[:, 0, rows:] * 64 + infos[:, 1, :rows]).reshape(total, 1)
            half = jnp.arange(LANES) % (HD // 2)
            rates = THETA ** (-2.0 * half.astype(f32) / HD)
            angles = spots * rates[None, :]
            edges = docs.reshape(total // GRAIN, GRAIN)
            lo = jnp.sum((edges[None, :, -1] < docs[:, :1]).astype(jnp.int32), axis=1)
            hi = jnp.sum((edges[None, :, 0] <= docs[:, rows - 1 :]).astype(jnp.int32), axis=1)
            count = (hi - lo + tile // GRAIN - 1) // (tile // GRAIN)
            base = jnp.minimum(lo, total // GRAIN - count * (tile // GRAIN))
            unit = units * me + jnp.arange(units, dtype=jnp.int32)
            first_head = jnp.minimum(units * me // splits, heads - SLOTS)
            unit_places = jnp.concatenate([unit // splits - first_head, unit % splits])
            pick = (unit % splits)[:, None] == jnp.arange(splits, dtype=jnp.int32)[None, :]
            own_part = lambda array: jnp.sum(
                jnp.where(pick[None, :, :, None], array.reshape(ctx, 1, splits, part), 0), axis=2
            ).reshape(ctx, 1, units * part)
            doc_q = own_part(docs)
            spot_q = own_part(spots)
            ids = jnp.arange(IDS + 1, dtype=jnp.int32)
            before = jnp.sum((docs.reshape(1, total) < ids[:, None]).astype(jnp.int32), axis=1)
            is_id = doc_q == ids[None, :-1, None]
            bounds = [
                jnp.sum(jnp.where(is_id, edge[None, :, None], 0), axis=1, keepdims=True)
                for edge in (before[:-1], before[1:])
            ]
            return (
                jnp.cos(angles), jnp.sin(angles), base, count, unit_places.astype(jnp.int32),
                jnp.concatenate(bounds, axis=1), spot_q,
            )

        def query_tables(spot_q):
            half = jnp.arange(HD) % (HD // 2)
            angles = THETA ** (-2.0 * half.astype(f32) / HD)[None, :, None] * spot_q
            return jnp.cos(angles), jnp.sin(angles)

        sent = spread(first, w_qkv, gain_attn, gain_mlp, segment_ids, positions)
        sent = lax.all_to_all(sent, "ctx", 0, 0, tiled=True)
        masks = [0]
        if by_hand:
            own = [tokens[0]]
            near = [jnp.stack(
                [packed[:, :cut], jnp.pad(packed[:, cut:], ((0, 0), (0, 2 * cut - columns)))]
            )]
            own.append(lax.ppermute(own[0], "ctx", turn(1)))
            other = [lax.ppermute(own[0], "ctx", swap)]
            near.append(lax.ppermute(near[0], "ctx", turn(1)))
            own[1], other[0], near[1], sent = gate(own[1], other[0], near[1], sent)

        w_parts = sent[:, :shard, :].reshape(1, share, 4 * LANES)
        bit = fsdp // 2
        while bit:
            got = lax.ppermute(w_parts, "fsdp", flips(fsdp, bit))
            w_parts = jnp.concatenate([w_parts, got], axis=0)
            masks += [mask ^ bit for mask in masks]
            bit //= 2
        known = tables(sent)
        if by_hand:
            own.append(lax.ppermute(own[1], "ctx", turn(1)))
            other.append(lax.ppermute(own[1], "ctx", swap))
            near.append(lax.ppermute(near[1], "ctx", turn(1)))
            low_a = jnp.stack([near[0][0], near[1][0]])
            low_b = jnp.stack([near[0][1], near[1][1]])
            own[2], other[1], near[2], low_a, low_b, w_parts, known = gate(
                own[2], other[1], near[2], low_a, low_b, w_parts, known
            )
        cosine, sine, base, count, unit_places, ranges, spot_q = known

        w_heads, gains = ready(masks, mine.astype(jnp.int32).reshape(1), w_parts)

        def project_some(blocks, places, held):
            at = jnp.stack(places).astype(jnp.int32)
            return project(at, blocks, w_heads, gains, cosine, sine, total, held)

        def came_from(step, flip):
            return (me // 2 + outer - step) % outer * 2 + (me % 2 + flip) % 2

        if by_hand:
            own.append(lax.ppermute(own[2], "ctx", turn(1)))
            other.append(lax.ppermute(own[2], "ctx", swap))
            near.append(lax.ppermute(near[2], "ctx", turn(1)))
            next_a = lax.ppermute(low_a, "ctx", swap)
            next_b = lax.ppermute(low_b, "fsdp", by_y)
            held = []
            for step in range(2):
                held = project_some(
                    [own[step], other[step]], [came_from(step, 0), came_from(step, 1)], held
                )
            own[3], other[2], near[3], next_a, next_b, held, late = gate(
                own[3], other[2], near[3], next_a, next_b, held, w_qkv
            )

            other.append(lax.ppermute(own[3], "ctx", swap))
            high_a = jnp.stack([near[2][0], near[3][0]])
            high_b = jnp.stack([near[2][1], near[3][1]])
            past_a = lax.ppermute(high_a, "ctx", swap)
            past_b = lax.ppermute(high_b, "fsdp", by_y)
            held = project_some(
                [own[2], other[2], own[3]],
                [came_from(2, 0), came_from(2, 1), came_from(3, 0)], held,
            )
            ring_c = [late, lax.ppermute(late, "ctx", turn(1))]
            other[3], past_a, past_b, held, ring_c = gate(other[3], past_a, past_b, held, ring_c)
            ring_c = jnp.stack(ring_c)
            ring_c = [ring_c, lax.ppermute(ring_c, "ctx", turn(2))]

            pair_a = jnp.concatenate([weave(low_a, next_a), weave(high_a, past_a)])
            pair_b = jnp.concatenate([low_b, next_b, high_b, past_b])
            far_a = lax.ppermute(pair_a, "fsdp", by_y)
            far_b = lax.ppermute(pair_b, "ctx", swap)
            held = project_some([other[3]], [came_from(3, 1)], held)
        else:
            blocks = lax.all_gather(tokens[0], "ctx", axis=0, tiled=True)
            blocks = blocks.reshape(ctx, rows, width)
            held = []
            for c in range(0, ctx, 2):
                held = project_some(
                    [blocks[c], blocks[c + 1]], [jnp.int32(c), jnp.int32(c + 1)], held
                )
        hidden_one, qkv, turned = held
        att_low, att, lse = attend(
            base, count, unit_places, qkv, turned, ranges, rows, tile
        )
        if by_hand:
            att_low, far_a, far_b, ring_c, spot_q = gate(att_low, far_a, far_b, ring_c, spot_q)
            tables_q = query_tables(spot_q)
            pair_b = weave(pair_b, far_b)
            arrays = [pair_a, far_a, lax.ppermute(pair_a, "fsdp", by_core),
                      lax.ppermute(far_a, "fsdp", by_core),
                      pair_b, lax.ppermute(pair_b, "fsdp", by_core)]
            metas_a = [[(flip + 2 * far, back) for back in range(outer)]
                       for flip in range(2) for far in range(2)]
            metas_b = [[(flip + 2 * near, back) for near in (0, 1) for back in (0, 1)]
                       + [(flip + 2 * near, back) for near in (0, 1) for back in (2, 3)]
                       for flip in range(2)]
            att_in = lax.all_to_all(att_low, "ctx", 0, 0, tiled=True)
            pair_c = jnp.concatenate(ring_c)
            att_in, arrays, pair_c, tables_q = gate(att_in, arrays, pair_c, tables_q)
            near_c = lax.ppermute(pair_c, "ctx", swap)
        else:
            att_in = lax.all_to_all(att_low, "ctx", 0, 0, tiled=True)
            tables_q = query_tables(spot_q)
            every = lax.all_gather(packed, AXES, axis=0, tiled=True)
            arrays = [every[None, :, :cut], every[None, :, cut:]]
            metas_a = metas_b = [[(0, 0)]]
            place = jnp.stack([0 * me, 0 * me, 0 * me + 1, 0 * me]).astype(jnp.int32)
            w_joined = lax.all_gather(w_qkv, AXES, axis=0, tiled=True)
        parts_a = list(zip(arrays, metas_a))
        parts_b = list(zip(arrays[len(metas_a) :], metas_b))

        output, grad_heads, grad_middle, attended, grad_branch, hidden_two, grad_up, product = (
            middle_stage(
                heads, splits, place, att_in, tokens[0], gains, cot, parts_a, parts_b,
                w_down.shape[0],
            )
        )
        operands = [attended, grad_branch, hidden_two, grad_up, cot, product]
        if by_hand:
            grad_heads, operands, near_c = gate(grad_heads, operands, near_c)
            pair_c = weave(pair_c, near_c)
            far_c = lax.ppermute(pair_c, "fsdp", by_y)
        grad_heads = lax.all_to_all(grad_heads, "ctx", 0, 0, tiled=True)
        if by_hand:
            grad_cut = columns // LANES * 5 // 11 * LANES
            rest = columns - grad_cut
            gone_a, gone_b = weight_grads(
                gone_grads_kernel, sides, operands, [], [(2, share, grad_cut), (2, share, rest)],
                grad_cut, [], "gone_grads",
            )
            got_a = lax.ppermute(gone_a, "fsdp", by_core)
            got_b = lax.ppermute(gone_b, "fsdp", by_core)
            mine_a, other_a, mine_b, other_b = weight_grads(
                kept_grads_kernel, sides, operands, [got_a, got_b],
                [(share, grad_cut)] * 2 + [(2 * outer, shard, rest)] * 2, grad_cut,
                [
                    pltpu.VMEM((2, share, grad_cut), bf16),
                    pltpu.VMEM((2, share, rest), bf16),
                    pltpu.VMEM((2, share, grad_cut), bf16),
                    pltpu.VMEM((2, 2 * outer, shard, rest), bf16),
                    pltpu.SemaphoreType.DMA((4,)),
                ],
                "kept_grads",
            )
            grad_heads, mine_a, other_a, mine_b, other_b = gate(
                grad_heads, mine_a, other_a, mine_b, other_b
            )
            got_a = lax.ppermute(other_a, "fsdp", by_y)
            got_b = lax.ppermute(other_b, "ctx", swap)
        else:
            grad_packed = jnp.concatenate(
                [dot_rows(left, right) for left, right in zip(operands[::2], operands[1::2])],
                axis=1,
            ).astype(bf16)
            grad_packed = lax.psum_scatter(grad_packed, "fsdp", scatter_dimension=0, tiled=True)
            grad_packed = lax.psum_scatter(grad_packed, "ctx", scatter_dimension=0, tiled=True)
            grad_packed = grad_packed.astype(f32)

        grad_joined, grad_sent = attend_back(
            base, count, unit_places, qkv, turned, ranges, grad_heads, att, lse, tables_q,
            (cosine, sine), rows, tile,
        )
        if by_hand:
            grad_joined, grad_sent, mine_a, got_a, mine_b, got_b, pair_c, far_c = gate(
                grad_joined, grad_sent, mine_a, got_a, mine_b, got_b, pair_c, far_c
            )
            joined_in = lax.all_to_all(grad_sent, "ctx", 0, 0, tiled=True)
            arrays = [pair_c, far_c, lax.ppermute(pair_c, "fsdp", by_core),
                      lax.ppermute(far_c, "fsdp", by_core)]
            by_x = lambda array: array.reshape(outer, 2, shard, array.shape[-1])
            mine_a, other_a, mine_b, other_b = add_halves(
                sides,
                [(by_x(mine_a), by_x(got_a), 1, 2),
                 (mine_b.reshape(2, share // 2, rest), got_b.reshape(2, share // 2, rest), 0, 1)],
            )
            sides_late, other_a, other_b = gate(sides, other_a, other_b)
            got_a = lax.ppermute(other_a, "ctx", swap)
            got_b = lax.ppermute(other_b, "fsdp", by_y)
            kept_cols, gone_cols = head_grads(fsdp, sides_late, hidden_one, grad_joined)
            got_cols = lax.ppermute(gone_cols, "fsdp", by_core)
            mine_a, got_a, mine_b, got_b, kept_cols, got_cols, arrays = gate(
                mine_a, got_a, mine_b, got_b, kept_cols, got_cols, arrays
            )
            w_joined = settle(place, list(zip(arrays, metas_a)), width)
            pairs = lambda array: array.reshape(outer // 2, 2, shard, array.shape[-1])
            kept, gone = add_halves(
                sides,
                [(pairs(mine_a), pairs(got_a), 1, 3), (pairs(mine_b), pairs(got_b), 1, 3)],
                joined=True,
            )
            got = lax.ppermute(gone, "ctx", flips(ctx, 2))
            kept_cols, gone_cols = add_halves(sides, [(kept_cols, got_cols, 0, 1)])
            got_cols = lax.ppermute(gone_cols, "fsdp", by_y)
            joined_in, kept, got, kept_cols, got_cols, w_joined = gate(
                joined_in, kept, got, kept_cols, got_cols, w_joined
            )
            kept, gone = add_halves(sides, [(kept, got, 0, 4)])
            got = lax.ppermute(gone, "ctx", flips(ctx, 4))
            grad_packed = kept[0].astype(f32) + got[0].astype(f32)
            grad_cols = (kept_cols[0].astype(f32) + got_cols[0].astype(f32)).astype(bf16)
            grad_cols, _ = gate(grad_cols, gone)
        else:
            joined_in = lax.all_to_all(grad_sent, "ctx", 0, 0, tiled=True)
            grad_cols = dot_rows(hidden_one, grad_joined.reshape(total, 3 * LANES)).astype(bf16)
            grad_cols = lax.psum_scatter(grad_cols, "fsdp", scatter_dimension=0, tiled=True)
        input_grad = finish(owners, splits, joined_in, tokens[0], gains, grad_middle, w_joined)
        grad_cols = grad_cols.reshape(ctx, shard, 3 * LANES)
        grad_cols = lax.all_to_all(grad_cols, "ctx", 0, 0, tiled=True).astype(f32)

        sum_w_out = grad_packed[:, :width]
        sum_w_in = grad_packed[:, width : width + w_in.shape[1]]
        sum_w_down = grad_packed[:, width + w_in.shape[1] :].T
        sum_gain_mlp = jnp.sum(w_in.astype(f32) * sum_w_in, axis=1) / gain_mlp.astype(f32)
        pieces = []
        for third in range(3):
            for head in range(heads):
                column = 0.0
                for c, slot in owners[head]:
                    at = third * LANES + slot * HD
                    column = column + grad_cols[c, :, at : at + HD]
                pieces.append(column)
        sum_w_qkv = jnp.concatenate(pieces, axis=1)
        sum_gain_attn = jnp.sum(w_qkv.astype(f32) * sum_w_qkv, axis=1) / gain_attn.astype(f32)
        return (
            output[None],
            input_grad[None],
            sum_gain_attn,
            sum_w_qkv,
            sum_w_out,
            sum_gain_mlp,
            sum_w_in,
            sum_w_down,
        )

    return on_device


def solution(mesh):
    rows = P(AXES, None)
    tokens = P("fsdp", "ctx", None)
    return jax.shard_map(
        program(mesh.shape["fsdp"], mesh.shape["ctx"]),
        mesh=mesh,
        in_specs=(
            tokens,
            P("fsdp", "ctx"),
            P("fsdp", "ctx"),
            P(AXES),
            rows,
            rows,
            P(AXES),
            rows,
            P(None, AXES),
            tokens,
        ),
        out_specs=(tokens, tokens, P(AXES), rows, rows, P(AXES), rows, P(None, AXES)),
        check_vma=False,
    )
```
